32 devices in a mesh: dp: 8 (over y, x, core), tensor: 4 (over z).
Axes of the slice: x: 2, y: 2, z: 4, core: 2. Of those that a mesh axis runs over, the one named last changes fastest.
Arguments:
- x_in: bfloat16 [16384, 768], P(('dp', 'tensor')), may hold values from -6 to 6
- bucket: int32 [32], P(('dp', 'tensor')), may hold values from 0 to 1
- lengths: int32 [32, 4], P(('dp', 'tensor')), may hold values from 32 to 128, as said below
- qkv_weight: bfloat16 [2, 768, 2304], replicated, may hold values from -0.21875 to 0.21875
- out_weight: bfloat16 [2, 768, 768], replicated, may hold values from -0.875 to 0.875
- norm_gain1: float32 [2, 768], replicated, may hold values from 0.5 to 1.5
- norm_bias1: float32 [2, 768], replicated, may hold values from -1.8 to 1.8
- up_weight: bfloat16 [2, 768, 2, 3072], P(None, None, None, 'tensor'), may hold values from -0.21875 to 0.21875
- down_weight: bfloat16 [2, 3072, 768], P(None, 'tensor'), may hold values from -0.109375 to 0.109375
- norm_gain2: float32 [2, 768], replicated, may hold values from 0.5 to 1.5
- norm_bias2: float32 [2, 768], replicated, may hold values from -1.8 to 1.8
- cotangent: bfloat16 [16384, 768], P(('dp', 'tensor')), may hold values from -6 to 6
Outputs:
- activations: bfloat16 [2, 16384, 768], P(None, ('dp', 'tensor'))
- input_grad: float32 [16384, 768], P(('dp', 'tensor'))
- qkv_grad: float32 [2, 768, 2304], replicated
- out_grad: float32 [2, 768, 768], replicated
- gain1_grad: float32 [2, 768], replicated
- bias1_grad: float32 [2, 768], replicated
- up_grad: float32 [2, 768, 2, 3072], P(None, 'dp', None, 'tensor')
- down_grad: float32 [2, 3072, 768], P(None, 'tensor', 'dp')
- gain2_grad: float32 [2, 768], replicated
- bias2_grad: float32 [2, 768], replicated
The draws below stay inside these ranges and needn't reach their ends.
Inputs may be any that keep to these rules, and one draw needn't show every extreme that they name: Every entry is a length of a short sequence; each row of lengths has an entry equal to 128. A block of bucket 1 holds one sequence whose length is the sum of its row of lengths.
All inputs are finite; a program needn't handle non-finite values.
Results may differ from the reference program's by a relative error of at most 0.033.
Values may be sent and summed in bfloat16 or wider, within the bound.
No kernel may reach another device: no remote copies, remote signals or barrier semaphores. Data moves between devices by JAX's collectives and lax.ppermute only.
A program may use at most 256 MiB of HBM per device.

```python
import jax
import jax.numpy as jnp
from jax import lax

D = 768
HEADS = 12
HEAD_DIM = 64
FF = 3072
LONG = 512
SHORT = 128
LAYERS = 2
SLOTS = 4
TOKENS = 16384
N_TENSOR = 4


def draw_lengths(key, part):
    count = TOKENS // LONG
    base = jax.random.randint(jax.random.fold_in(key, 11), (count, SLOTS), SHORT // 4, SHORT + 1)
    pick = jax.random.randint(jax.random.fold_in(key, 12), (count, 1), 0, SLOTS)
    full = jnp.arange(SLOTS, dtype=jnp.int32)[None, :] == pick
    return jnp.where(full, SHORT, base).astype(jnp.int32)


def with_ends(drawn, stream_key, least, largest):
    dims = drawn.shape
    spot = [jax.random.randint(jax.random.fold_in(stream_key, axis), (), 0, dims[axis]) for axis in range(len(dims))]
    drawn = drawn.at[tuple(spot)].set(least)
    longest = dims.index(max(dims))
    spot[longest] = (spot[longest] + 1) % dims[longest]
    return drawn.at[tuple(spot)].set(largest)


def levels(key, extent, split, least, high):
    factor_of = 1.0
    for axis_at, parts in split:
        steps = jax.random.uniform(jax.random.fold_in(jax.random.fold_in(key, 6), axis_at), (parts,), jnp.float32, least / len(split), high / len(split))
        factor_of = factor_of * jnp.repeat(jnp.exp(steps), extent[axis_at] // parts).reshape((-1,) + (1,) * (len(extent) - 1 - axis_at))
    return factor_of


def gaussian(stream_key, dims, width, reach, shards=(), kind=jnp.bfloat16):
    level = levels(stream_key, dims, shards, -0.22, 0.18) if shards else 1.0
    result = jax.random.normal(stream_key, dims, jnp.float32) * width * level
    return jnp.minimum(jnp.maximum(result, -reach), reach).astype(kind)


def setup_inputs(seed: int = 0) -> dict:
    splits = jax.random.split(jax.random.key(seed), 13)
    return {
        "x_in": gaussian(splits[0], (TOKENS, D), 1.0, 6.0, ((0, 32),)),
        "bucket": with_ends(jax.random.randint(splits[1], (TOKENS // LONG,), 0, 2), jax.random.fold_in(splits[1], 1), 0, 1).astype(jnp.int32),
        "lengths": draw_lengths(jax.random.fold_in(splits[12], 71), 0),
        "qkv_weight": gaussian(splits[3], (LAYERS, D, 3 * D), D ** -0.5, 0.21875),
        "out_weight": gaussian(splits[4], (LAYERS, D, D), (D // 16) ** -0.5, 0.875),
        "norm_gain1": jnp.clip(1.0 + 0.1 * jax.random.normal(splits[5], (LAYERS, D), jnp.float32), 0.5, 1.5),
        "norm_bias1": gaussian(splits[6], (LAYERS, D), 0.3, 1.8, (), jnp.float32),
        "up_weight": gaussian(splits[7], (LAYERS, D, 2, FF), D ** -0.5, 0.21875, ((3, 4),)),
        "down_weight": gaussian(splits[8], (LAYERS, FF, D), FF ** -0.5, 0.109375, ((1, 4),)),
        "norm_gain2": jnp.clip(1.0 + 0.1 * jax.random.normal(splits[9], (LAYERS, D), jnp.float32), 0.5, 1.5),
        "norm_bias2": gaussian(splits[10], (LAYERS, D), 0.3, 1.8, (), jnp.float32),
        "cotangent": gaussian(splits[11], (TOKENS, D), 1.0, 6.0, ((0, 32),)),
    }


@jax.custom_vjp
def low(v):
    return lax.optimization_barrier(v.astype(jnp.bfloat16)).astype(jnp.float32)

@jax.custom_vjp
def low_back(v):
    return v

def low_keep(v):
    return (low(v), None)

def low_pass(kept, grad):
    return (grad,)

def back_keep(v):
    return (v, None)

def back_low(kept, grad):
    return (low(grad),)
low.defvjp(low_keep, low_pass)
low_back.defvjp(back_keep, back_low)
eps_norm = 1e-05
gelu_coef = 0.7978845608028654
highest = lax.Precision.HIGHEST
masked_score = -1e+30

def segments(bucket_one, lens, rows_dev, short_len):
    rows = jnp.arange(rows_dev, dtype=jnp.int32)
    slot = rows // short_len
    offset = rows - slot * short_len
    slots_all = jnp.arange(lens.shape[0], dtype=jnp.int32)
    slot_len = lax.optimization_barrier(jnp.sum(jnp.where(slot[:, None] == slots_all[None, :], lens[None, :], 0), axis=1))
    total = jnp.sum(lens)
    is_long = bucket_one == 1
    real = jnp.where(is_long, rows < total, offset < slot_len)
    group = jnp.where(is_long, 0, slot)
    return jnp.where(real, group, lens.shape[0] + rows).astype(jnp.int32)

def alibi(rows_dev, heads):
    slopes = jnp.exp2(-8.0 * (jnp.arange(heads, dtype=jnp.float32) + 1.0) / heads)
    place = jnp.arange(rows_dev, dtype=jnp.float32)
    dist = jnp.abs(place[:, None] - place[None, :])
    return slopes[:, None, None] * dist[None, :, :]

def layer_norm(value, gain, bias):
    mean = lax.optimization_barrier(jnp.mean(value, axis=-1, keepdims=True))
    centered = value - mean
    var = lax.optimization_barrier(jnp.mean(centered * centered, axis=-1, keepdims=True))
    return centered * lax.rsqrt(var + eps_norm) * gain + bias

def geglu(joined):
    half = joined.shape[1] // 2
    gate = joined[:, :half]
    value = joined[:, half:]
    return 0.5 * gate * (1.0 + jnp.tanh(gelu_coef * (gate + 0.044715 * gate * gate * gate))) * value

def both(value):
    return low(low_back(value))

def block_layer(x, seg, wqkv, wo, g1, b1, wup, wdown, g2, b2):
    rows = x.shape[0]
    qkv = both(jnp.dot(x, wqkv, precision=highest, preferred_element_type=jnp.float32))
    query = qkv[:, :D].reshape(rows, HEADS, HEAD_DIM)
    keys = qkv[:, D:2 * D].reshape(rows, HEADS, HEAD_DIM)
    values = qkv[:, 2 * D:].reshape(rows, HEADS, HEAD_DIM)
    scores = jnp.einsum('qhe,khe->hqk', query, keys, precision=highest) * HEAD_DIM ** (-0.5) - alibi(rows, HEADS)
    scores = low_back(scores)
    same = seg[:, None] == seg[None, :]
    scores = jnp.where(same[None, :, :], scores, masked_score)
    top = lax.optimization_barrier(jnp.max(scores, axis=-1, keepdims=True))
    expo = jnp.exp(scores - top)
    probs = low(expo / lax.optimization_barrier(jnp.sum(expo, axis=-1, keepdims=True)))
    ctx = jnp.einsum('hqk,khe->qhe', probs, values, precision=highest).reshape(rows, D)
    ctx = both(ctx)
    attn = low_back(jnp.dot(ctx, wo, precision=highest, preferred_element_type=jnp.float32))
    normed = layer_norm(x + attn, g1, b1)
    normed_low = low(normed)
    joined = low_back(jnp.dot(normed_low, wup.reshape(D, 2 * FF), precision=highest, preferred_element_type=jnp.float32))
    act = low(geglu(joined))
    terms = jnp.einsum('rtf,tfd->rtd', act.reshape(rows, N_TENSOR, FF // N_TENSOR), wdown.reshape(N_TENSOR, FF // N_TENSOR, D), precision=highest)
    mixed = low_back(lax.optimization_barrier(jnp.sum(low(terms), axis=1)))
    return low(layer_norm(normed + mixed, g2, b2))

def reference(x_in, bucket, lengths, qkv_weight, out_weight, norm_gain1, norm_bias1, up_weight, down_weight, norm_gain2, norm_bias2, cotangent):
    blocks = TOKENS // LONG
    segs = jax.vmap(lambda one, lens: segments(one, lens, LONG, SHORT))(bucket, lengths)

    def forward(x, wqkv, wo, g1, b1, wup, wdown, g2, b2):
        outputs = []
        for layer in range(LAYERS):

            def one_block(pair, layer=layer):
                return block_layer(pair[0], pair[1], wqkv[layer], wo[layer], g1[layer], b1[layer], wup[layer], wdown[layer], g2[layer], b2[layer])
            x = lax.map(jax.checkpoint(one_block), (x.reshape(blocks, LONG, D), segs)).reshape(TOKENS, D)
            outputs.append(x)
        return jnp.stack(outputs)
    floats = (x_in.astype(jnp.float32), qkv_weight.astype(jnp.float32), out_weight.astype(jnp.float32), norm_gain1, norm_bias1, up_weight.astype(jnp.float32), down_weight.astype(jnp.float32), norm_gain2, norm_bias2)
    acts, pull = jax.vjp(forward, *floats)
    start_grad = jnp.zeros(acts.shape, jnp.float32).at[LAYERS - 1].set(cotangent.astype(jnp.float32))
    grads = pull(start_grad)
    return (acts.astype(jnp.bfloat16), grads[0], grads[1], grads[2], grads[3], grads[4], grads[5], grads[6], grads[7], grads[8])
```

```python
import functools

import jax
import jax.numpy as jnp
from jax import lax
from jax.experimental import pallas as pl
from jax.experimental.pallas import tpu as pltpu
from jax.sharding import PartitionSpec as P

HEADS = 12
HEAD_DIM = 64
SHORT = 128
LAYERS = 2

eps_norm = 1e-05
gelu_coef = 0.7978845608028654
masked_score = -1e30
bf16 = jnp.bfloat16
f32 = jnp.float32
BOTH = ("dp", "tensor")


def segments(bucket_one, lens, rows_dev, short_len):
    rows = jnp.arange(rows_dev, dtype=jnp.int32)
    slot = rows // short_len
    offset = rows - slot * short_len
    slots_all = jnp.arange(lens.shape[0], dtype=jnp.int32)
    slot_len = jnp.sum(jnp.where(slot[:, None] == slots_all[None, :], lens[None, :], 0), axis=1)
    total = jnp.sum(lens)
    is_long = bucket_one == 1
    real = jnp.where(is_long, rows < total, offset < slot_len)
    group = jnp.where(is_long, 0, slot)
    return jnp.where(real, group, lens.shape[0] + rows)


def alibi(rows_dev, heads):
    slopes = jnp.exp2(-8.0 * (jnp.arange(heads, dtype=f32) + 1.0) / heads)
    place = jnp.arange(rows_dev, dtype=f32)
    dist = jnp.abs(place[:, None] - place[None, :])
    return slopes[:, None, None] * dist[None, :, :]


def layer_norm(value, gain, bias):
    mean = jnp.mean(value, axis=-1, keepdims=True)
    centered = value - mean
    var = jnp.mean(centered * centered, axis=-1, keepdims=True)
    return centered * lax.rsqrt(var + eps_norm) * gain + bias


def geglu(joined):
    half = joined.shape[1] // 2
    gate = joined[:, :half]
    value = joined[:, half:]
    return 0.5 * gate * (1.0 + jnp.tanh(gelu_coef * (gate + 0.044715 * gate * gate * gate))) * value


def split_heads(qkv_low, width):
    rows = qkv_low.shape[0]
    query = qkv_low[:, :width].reshape(rows, HEADS, HEAD_DIM)
    keys = qkv_low[:, width : 2 * width].reshape(rows, HEADS, HEAD_DIM)
    values = qkv_low[:, 2 * width :].reshape(rows, HEADS, HEAD_DIM)
    return (query, keys, values)


def scores_of(query, keys, same, decay):
    raw = (
        jnp.einsum("qhe,khe->hqk", query, keys, preferred_element_type=f32) * HEAD_DIM ** (-0.5)
        - decay
    )
    return jnp.where(same[None, :, :], raw, masked_score)


def dot(a, b):
    return jnp.dot(a, b, preferred_element_type=f32)


class Net:
    def __init__(self, mesh):
        self.n_dp = mesh.shape["dp"]
        self.n_t = mesh.shape["tensor"]

    def flip(self, value, bit):
        return lax.ppermute(value, "dp", [(i, i ^ bit) for i in range(self.n_dp)])

    def shift(self, value, step):
        n = self.n_t
        return lax.ppermute(value, "tensor", [(i, (i + step) % n) for i in range(n)])


COLOURS = ((2, 4), (4, 2))


def order_of(colour):
    one, two = COLOURS[colour]
    return [0, one, two, one ^ two]


def fold_order(colour):
    one, two = COLOURS[colour]
    return [0, two, one, one ^ two]


class Line:
    def __init__(self):
        self.last = None

    def after(self, value):
        if self.last is None:
            return value
        return lax.optimization_barrier((value, self.last))[0]

    def run(self, call, first, *rest):
        out = call(self.after(first), *rest)
        self.last = out[0] if isinstance(out, (tuple, list)) else out
        return out


class Gather:
    def __init__(self, net, line, slices):
        self.net, self.line = net, line
        half = slices[0].shape[0] // 2
        self.held = [
            jnp.stack([line.after(one)[c * half : (c + 1) * half] for one in slices])[None]
            for c in range(2)
        ]
        self.got = [net.flip(self.held[c], COLOURS[c][0]) for c in range(2)]

    def join(self):
        return [
            jnp.concatenate([self.held[c], self.line.after(self.got[c])], axis=0) for c in range(2)
        ]

    def second(self):
        self.held = self.join()
        self.got = [self.net.flip(self.held[c], COLOURS[c][1]) for c in range(2)]

    def core(self):
        self.held = self.join()
        self.got = [self.net.flip(self.held[c], 1) for c in range(2)]

    def pieces(self):
        return [one for c in range(2) for one in (self.held[c], self.got[c])]


VMEM_SPEC = pl.BlockSpec(memory_space=pltpu.VMEM)
ANY_SPEC = pl.BlockSpec(memory_space=pl.ANY)
SMEM_SPEC = pl.BlockSpec(memory_space=pltpu.SMEM)
NN = (((1,), (0,)), ((), ()))
NT = (((1,), (1,)), ((), ()))
TN = (((0,), (0,)), ((), ()))


def mm(a, b, dims=NN):
    return lax.dot_general(a, b, dims, preferred_element_type=f32)


def params(mib):
    return pltpu.CompilerParams(vmem_limit_bytes=mib << 20)


def cost(flops, nbytes):
    return pl.CostEstimate(flops=int(flops), transcendentals=0, bytes_accessed=int(nbytes))


def shape(dims, kind):
    return jax.ShapeDtypeStruct(dims, kind)


def normed_of(value):
    mean = jnp.mean(value, axis=-1, keepdims=True)
    centered = value - mean
    var = jnp.mean(centered * centered, axis=-1, keepdims=True)
    rstd = lax.rsqrt(var + eps_norm)
    return centered * rstd, rstd


def norm_back(grad, xhat, rstd, gain):
    scaled = grad * gain
    first = jnp.mean(scaled, axis=-1, keepdims=True)
    second = jnp.mean(scaled * xhat, axis=-1, keepdims=True)
    return rstd * (scaled - first - xhat * second)


def attn_fwd_kernel(slopes, x_ref, wqkv_ref, wo_ref, g_ref, b_ref, dist_ref, *outs):
    qkv_ref, lse_ref, ctx_ref, ctx_t_ref, pre_ref, hb_ref, hb_t_ref = outs
    rows, width = x_ref.shape
    x = x_ref[...]
    for c in range(3):
        cols = pl.ds(c * width, width)
        qkv_ref[:, cols] = mm(x, wqkv_ref[0, :, cols]).astype(bf16)
    lse_ref[...] = jnp.zeros_like(lse_ref)
    tile = 128

    def pair(p, _):
        def at(c):
            return pl.ds(pl.multiple_of(c * width + p * 128, 128), 128)

        key, val = qkv_ref[:, at(1)], qkv_ref[:, at(2)]
        lane = lax.broadcasted_iota(jnp.int32, (tile, 128), 1)
        for r in range(rows // tile):
            here = pl.ds(r * tile, tile)
            query = qkv_ref[here, at(0)] * bf16(HEAD_DIM ** (-0.5))
            dist = dist_ref[here, :]
            found = []
            for side in range(2):
                mine = (lane < HEAD_DIM) == (side == 0)
                s = mm(jnp.where(mine, query, bf16(0)), key, NT) - slopes[2 * p + side] * dist
                top = jnp.max(s, axis=-1, keepdims=True)
                e = jnp.exp(s - top)
                total = jnp.sum(e, axis=-1, keepdims=True)
                lse = top + jnp.log(total)
                lse_ref[here, :] += jnp.where(lane == 2 * p + side, lse, 0.0)
                found.append(mm((e * (1.0 / total)).astype(bf16), val))
            ctx_ref[here, at(0)] = jnp.where(lane < HEAD_DIM, found[0], found[1]).astype(bf16)
        return 0

    lax.fori_loop(0, width // 128, pair, 0)
    ctx = ctx_ref[...]
    ctx_t_ref[...] = ctx.T
    pre = x.astype(f32) + mm(ctx, wo_ref[0])
    pre_ref[...] = pre
    xhat, _ = normed_of(pre)
    hb = (xhat * g_ref[...] + b_ref[...]).astype(bf16)
    hb_ref[...] = hb
    hb_t_ref[...] = hb.T


def slopes_of():
    steps = jnp.arange(HEADS, dtype=f32)
    return jnp.exp2(-8.0 * (steps + 1.0) / HEADS)


def of_layer(weight, layer):
    return pl.BlockSpec((1,) + weight.shape[1:], lambda i: (layer,) + (0,) * (weight.ndim - 1))


def attn_fwd(layer, x, wqkv, wo, gain, bias, dist, slopes):
    rows, width = x.shape
    return pl.pallas_call(
        attn_fwd_kernel,
        name="attn_fwd",
        grid=(1,),
        out_shape=(
            shape((rows, 3 * width), bf16),
            shape((rows, 128), f32),
            shape((rows, width), bf16),
            shape((width, rows), bf16),
            shape((rows, width), f32),
            shape((rows, width), bf16),
            shape((width, rows), bf16),
        ),
        in_specs=[SMEM_SPEC, VMEM_SPEC, of_layer(wqkv, layer), of_layer(wo, layer)]
        + [VMEM_SPEC] * 3,
        out_specs=(VMEM_SPEC,) * 7,
        compiler_params=params(40),
        cost_estimate=cost(2 * rows * width * width * 8, 16 << 20),
    )(slopes, x, wqkv, wo, gain[None], bias[None], dist)


def attn_bwd_kernel(slopes, dab_ref, qkv_ref, lse_ref, wo_ref, dist_ref, out_ref, *scratch):
    dctx_ref, p_ref, ds_ref = scratch
    rows, width = dab_ref.shape
    scale = HEAD_DIM ** (-0.5)
    dctx_ref[...] = mm(dab_ref[...], wo_ref[0], NT).astype(bf16)
    tile = 128

    def pair(p, _):
        def at(c):
            return pl.ds(pl.multiple_of(c * width + p * 128, 128), 128)

        key, val, query = qkv_ref[:, at(1)], qkv_ref[:, at(2)], qkv_ref[:, at(0)]
        dctx = dctx_ref[:, at(0)]
        lane = lax.broadcasted_iota(jnp.int32, (tile, 128), 1)
        wide = lax.broadcasted_iota(jnp.int32, (rows, 128), 1)
        d_q, d_k, d_v = [], [], []
        for side in range(2):
            mine = (lane < HEAD_DIM) == (side == 0)
            for r in range(rows // tile):
                here = pl.ds(r * tile, tile)
                q = jnp.where(mine, qkv_ref[here, at(0)] * bf16(scale), bf16(0))
                dc = jnp.where(mine, dctx_ref[here, at(0)], bf16(0))
                lse = jnp.sum(
                    jnp.where(lane == 2 * p + side, lse_ref[here, :], 0.0), axis=-1, keepdims=True
                )
                s = mm(q, key, NT) - slopes[2 * p + side] * dist_ref[here, :]
                prob = jnp.exp(s - lse)
                d_prob = mm(dc, val, NT)
                mean = jnp.sum(prob * d_prob, axis=-1, keepdims=True)
                p_ref[here, :] = prob.astype(bf16)
                ds_ref[here, :] = (prob * (d_prob - mean)).astype(bf16)
            d_s = ds_ref[...]
            d_q.append(mm(d_s, key))
            d_k.append(mm(d_s, query, TN))
            d_v.append(mm(p_ref[...], dctx, TN))
        low = wide < HEAD_DIM
        out_ref[:, at(0)] = (jnp.where(low, d_q[0], d_q[1]) * scale).astype(bf16)
        out_ref[:, at(1)] = (jnp.where(low, d_k[0], d_k[1]) * scale).astype(bf16)
        out_ref[:, at(2)] = jnp.where(low, d_v[0], d_v[1]).astype(bf16)
        return 0

    lax.fori_loop(0, width // 128, pair, 0)


def attn_bwd(layer, dab, qkv, lse, wo, dist, slopes):
    rows, width = dab.shape
    return pl.pallas_call(
        attn_bwd_kernel,
        name="attn_bwd",
        grid=(1,),
        out_shape=shape((rows, 3 * width), bf16),
        in_specs=[SMEM_SPEC] + [VMEM_SPEC] * 3 + [of_layer(wo, layer), VMEM_SPEC],
        out_specs=VMEM_SPEC,
        scratch_shapes=[
            pltpu.VMEM((rows, width), bf16),
            pltpu.VMEM((rows, rows), bf16),
            pltpu.VMEM((rows, rows), bf16),
        ],
        compiler_params=params(40),
        cost_estimate=cost(2 * rows * width * width * 12, 12 << 20),
    )(slopes, dab, qkv, lse, wo, dist)


def load_groups(groups, d, refs, w_ref, sems):
    copies = []
    at = 0
    shared = None
    for s, group in enumerate(groups):
        mine = []
        if group is None:
            up_ref, down_ref = refs[at : at + 2]
            at += 2
            split = up_ref.shape[1]
            mine = [
                pltpu.make_async_copy(up_ref, w_ref.at[s, :, pl.ds(0, split)], sems.at[s, 0]),
                pltpu.make_async_copy(
                    down_ref, w_ref.at[s, :, pl.ds(split, down_ref.shape[1])], sems.at[s, 1]
                ),
            ]
        else:
            if group == 0:
                shared = refs[at : at + 4]
                at += 4
            half = shared[0].shape[2]
            for c in range(4):
                for i, j in enumerate(order_of(c // 2)):
                    row = jnp.bitwise_xor(d, j ^ (c % 2)) * (2 * half) + (c // 2) * half
                    to = w_ref.at[s, pl.ds(pl.multiple_of(row, half), half)]
                    sem = sems.at[s, 4 * c + i]
                    mine.append(pltpu.make_async_copy(shared[c].at[i, group], to, sem))
        copies.append(mine)
    for mine in copies:
        for copy in mine:
            copy.start()
    return copies


def gelu_parts(gate):
    square = gate * gate
    t = jnp.tanh(gelu_coef * gate * (1.0 + 0.044715 * square))
    half = 0.5 * (1.0 + t)
    slope = half + 0.5 * gate * (1.0 - t * t) * gelu_coef * (1.0 + 3 * 0.044715 * square)
    return gate * half, slope


TILE = 256


def ff_fwd_kernel(groups, n_refs, first, last, at_ref, hb_ref, *refs):
    acc_refs, refs = refs[: 3 if first else 1], refs[3 if first else 1 :]
    weight_refs, refs = refs[:n_refs], refs[n_refs:]
    if last:
        g_ref, b_ref, pre_ref, out_ref, out_t_ref, w_ref, sems = refs
    else:
        pre_ref, w_ref, sems = refs
    width = hb_ref.shape[1]
    copies = load_groups(groups, at_ref[0], weight_refs, w_ref, sems)
    if first:
        xhat, _ = normed_of(acc_refs[0][...])
        pre_ref[...] = xhat * acc_refs[1][...] + acc_refs[2][...]
    else:
        pre_ref[...] = acc_refs[0][...]
    for s in range(len(groups)):
        for copy in copies[s]:
            copy.wait()

        def step(n, _, s=s):
            def at(c):
                return pl.ds(pl.multiple_of(c * width + n * TILE, TILE), TILE)

            hb = hb_ref[...]
            gate, value = mm(hb, w_ref[s, :, at(0)]), mm(hb, w_ref[s, :, at(1)])
            act = (gelu_parts(gate)[0] * value).astype(bf16)
            pre_ref[...] += mm(act, w_ref[s, at(0), pl.ds(2 * width, width)])
            return 0

        lax.fori_loop(0, width // TILE, step, 0)
    if last:
        xhat, _ = normed_of(pre_ref[...])
        out = (xhat * g_ref[...] + b_ref[...]).astype(bf16)
        out_ref[...] = out
        out_t_ref[...] = out.T


def ff_fwd(groups, d, hb, acc, weights, norm=None):
    rows, width = hb.shape
    last = norm is not None
    acc = acc if isinstance(acc, tuple) else (acc,)
    outs = [shape((rows, width), f32)]
    if last:
        outs += [shape((rows, width), bf16), shape((width, rows), bf16)]
    extra = list(norm) if last else []
    n = len(groups)
    return pl.pallas_call(
        functools.partial(ff_fwd_kernel, groups, len(weights), len(acc) == 3, last),
        name="ff_fwd",
        out_shape=tuple(outs),
        in_specs=[SMEM_SPEC, VMEM_SPEC]
        + [VMEM_SPEC] * len(acc)
        + [ANY_SPEC] * len(weights)
        + [VMEM_SPEC] * len(extra),
        out_specs=(VMEM_SPEC,) * len(outs),
        scratch_shapes=[
            pltpu.VMEM((n, width, 3 * width), bf16),
            pltpu.SemaphoreType.DMA((n, 16)),
        ],
        compiler_params=params(44),
        cost_estimate=cost(6 * rows * width * width * n, 5 * n << 20),
    )(d, hb, *acc, *weights, *extra)


def ff_bwd_kernel(groups, at_ref, hb_ref, dyb_ref, acc_ref, *refs):
    weight_refs, (r_ref, dh_ref, w_ref, sems) = refs[:-4], refs[-4:]
    width = hb_ref.shape[1]
    copies = load_groups(groups, at_ref[0], weight_refs, w_ref, sems)
    dh_ref[...] = acc_ref[...]
    for s in range(len(groups)):
        for copy in copies[s]:
            copy.wait()

        def step(n, _, s=s):
            def at(c):
                return pl.ds(pl.multiple_of(c * width + n * TILE, TILE), TILE)

            hb = hb_ref[...]
            gate, value = mm(hb, w_ref[s, :, at(0)]), mm(hb, w_ref[s, :, at(1)])
            d_act = mm(dyb_ref[...], w_ref[s, at(0), pl.ds(2 * width, width)], NT)
            gelu, slope = gelu_parts(gate)
            d_gate = (d_act * value * slope).astype(bf16)
            d_value = (d_act * gelu).astype(bf16)
            r_ref[s, :, at(0)] = d_gate
            r_ref[s, :, at(1)] = d_value
            r_ref[s, :, at(2)] = (gelu * value).astype(bf16)
            dh_ref[...] += mm(d_gate, w_ref[s, :, at(0)], NT) + mm(d_value, w_ref[s, :, at(1)], NT)
            return 0

        lax.fori_loop(0, width // TILE, step, 0)


def ff_bwd(groups, d, hb, dyb, acc, weights):
    rows, width = hb.shape
    n = len(groups)
    return pl.pallas_call(
        functools.partial(ff_bwd_kernel, groups),
        name="ff_bwd",
        out_shape=(shape((n, rows, 3 * width), bf16), shape((rows, width), f32)),
        in_specs=[SMEM_SPEC] + [VMEM_SPEC] * 3 + [ANY_SPEC] * len(weights),
        out_specs=(VMEM_SPEC, VMEM_SPEC),
        scratch_shapes=[
            pltpu.VMEM((n, width, 3 * width), bf16),
            pltpu.SemaphoreType.DMA((n, 16)),
        ],
        compiler_params=params(48),
        cost_estimate=cost(12 * rows * width * width * n, 8 * n << 20),
    )(d, hb, dyb, acc, *weights)


def norm2_bwd_kernel(grad_ref, pre_ref, g_ref, dpre_ref, dyb_ref, dyb_t_ref, small_ref):
    grad = grad_ref[...].astype(f32)
    xhat, rstd = normed_of(pre_ref[...])
    small_ref[0:1] = jnp.sum(grad * xhat, axis=0, keepdims=True)
    small_ref[1:2] = jnp.sum(grad, axis=0, keepdims=True)
    d_pre = norm_back(grad, xhat, rstd, g_ref[...])
    dpre_ref[...] = d_pre
    dyb = d_pre.astype(bf16)
    dyb_ref[...] = dyb
    dyb_t_ref[...] = dyb.T


def norm_bwd(grad, pre, gain):
    rows, width = pre.shape
    return pl.pallas_call(
        norm2_bwd_kernel,
        name="norm_bwd",
        out_shape=(
            shape((rows, width), f32),
            shape((rows, width), bf16),
            shape((width, rows), bf16),
            shape((2, width), f32),
        ),
        in_specs=[VMEM_SPEC] * 3,
        out_specs=(VMEM_SPEC,) * 4,
        compiler_params=params(24),
        cost_estimate=cost(rows * width * 20, 6 << 20),
    )(grad, pre, gain[None])


def pick_rows(d, order, from_ref, to_ref):
    rows = from_ref.shape[0] // 8
    for i, j in enumerate(order):
        at = pl.multiple_of(jnp.bitwise_xor(d, j) * rows, rows)
        to_ref[pl.ds(i * rows, rows), :] = from_ref[pl.ds(at, rows), :]


def send_kernel(order, at_ref, hb_t_ref, dyb_t_ref, r_ref, out_ref, h_ref, y_ref):
    @pl.when((pl.program_id(0) == 0) & (pl.program_id(1) == 0))
    def _():
        pick_rows(at_ref[0], order, hb_t_ref, h_ref)
        pick_rows(at_ref[0], order, dyb_t_ref, y_ref)

    part = pl.program_id(1)

    @pl.when(part < 2)
    def _():
        out_ref[0] = mm(h_ref[...], r_ref[0]).astype(bf16)

    @pl.when(part == 2)
    def _():
        out_ref[0] = mm(y_ref[...], r_ref[0]).astype(bf16)


def keep_kernel(order, at_ref, hb_t_ref, dyb_t_ref, r_ref, got_ref, one_ref, two_ref, h_ref, y_ref):
    @pl.when((pl.program_id(0) == 0) & (pl.program_id(1) == 0))
    def _():
        pick_rows(at_ref[0], order, hb_t_ref, h_ref)
        pick_rows(at_ref[0], order, dyb_t_ref, y_ref)

    part = pl.program_id(1)

    def put(lhs_ref):
        total = (mm(lhs_ref[...], r_ref[0]) + got_ref[0].astype(f32)).astype(bf16)
        half = total.shape[0] // 2
        one_ref[0] = total[:half]
        two_ref[0] = total[half:]

    @pl.when(part < 2)
    def _():
        put(h_ref)

    @pl.when(part == 2)
    def _():
        put(y_ref)


def ff_send(colour, d, hb_t, dyb_t, r):
    width, rows = hb_t.shape
    half = width // 2
    order = [j ^ 1 for j in fold_order(colour)]
    whole = pl.BlockSpec((width, rows), lambda s, c: (0, 0))
    return pl.pallas_call(
        functools.partial(send_kernel, order),
        name="ff_send",
        grid=(2, 3),
        out_shape=shape((2, half, 3 * width), bf16),
        in_specs=[SMEM_SPEC, whole, whole, pl.BlockSpec((1, rows, width), lambda s, c: (s, 0, c))],
        out_specs=pl.BlockSpec((1, half, width), lambda s, c: (s, 0, c)),
        scratch_shapes=[pltpu.VMEM((half, rows), bf16)] * 2,
        compiler_params=params(24),
        cost_estimate=cost(2 * rows * half * width * 6, 10 << 20),
    )(d, hb_t, dyb_t, r)


def ff_keep(colour, d, hb_t, dyb_t, r, got):
    width, rows = hb_t.shape
    half = width // 2
    order = fold_order(colour)
    whole = pl.BlockSpec((width, rows), lambda s, c: (0, 0))
    out = pl.BlockSpec((1, half // 2, width), lambda s, c: (s, 0, c))
    return pl.pallas_call(
        functools.partial(keep_kernel, order),
        name="ff_keep",
        grid=(2, 3),
        out_shape=(shape((2, half // 2, 3 * width), bf16),) * 2,
        in_specs=[
            SMEM_SPEC,
            whole,
            whole,
            pl.BlockSpec((1, rows, width), lambda s, c: (s, 0, c)),
            pl.BlockSpec((1, half, width), lambda s, c: (s, 0, c)),
        ],
        out_specs=(out, out),
        scratch_shapes=[pltpu.VMEM((half, rows), bf16)] * 2,
        compiler_params=params(24),
        cost_estimate=cost(2 * rows * half * width * 6, 12 << 20),
    )(d, hb_t, dyb_t, r, got)


def add_low(a, b):
    return (a.astype(f32) + b.astype(f32)).astype(bf16)


class Fold:
    def __init__(self, net, line, colour, sent, keep):
        self.net, self.line, self.bits = net, line, COLOURS[colour]
        self.keep = keep
        self.got = net.flip(sent, 1)

    def first(self):
        self.kept, sent = self.line.run(self.keep, self.got)
        self.got = self.net.flip(sent, self.bits[0])

    def second(self):
        half = self.kept.shape[1] // 2
        got = self.line.after(self.got)
        sent = add_low(self.kept[:, half:], got[:, half:])
        self.kept = add_low(self.kept[:, :half], got[:, :half])
        self.got = self.net.flip(sent, self.bits[1])

    def done(self):
        return add_low(self.kept, self.line.after(self.got))


def attn_send_kernel(colour, at_ref, x_t_ref, c_t_ref, r_ref, dab_ref, out_ref, h_ref):
    width = x_t_ref.shape[0]
    order = [j ^ 1 for j in fold_order(colour)]
    pick_rows(at_ref[0], order, x_t_ref, h_ref)
    for s in range(2):
        block = 2 * colour + s
        if block < 3:
            out_ref[s] = mm(h_ref[...], r_ref[:, pl.ds(block * width, width)]).astype(bf16)
        else:
            pick_rows(at_ref[0], order, c_t_ref, h_ref)
            out_ref[s] = mm(h_ref[...], dab_ref[...]).astype(bf16)


def attn_keep_kernel(
    colour, at_ref, x_t_ref, c_t_ref, r_ref, dab_ref, got_ref, one_ref, two_ref, h_ref
):
    width = x_t_ref.shape[0]
    order = fold_order(colour)
    pick_rows(at_ref[0], order, x_t_ref, h_ref)
    for s in range(2):
        block = 2 * colour + s
        if block < 3:
            total = mm(h_ref[...], r_ref[:, pl.ds(block * width, width)])
        else:
            pick_rows(at_ref[0], order, c_t_ref, h_ref)
            total = mm(h_ref[...], dab_ref[...])
        total = (total + got_ref[s].astype(f32)).astype(bf16)
        half = total.shape[0] // 2
        one_ref[s] = total[:half]
        two_ref[s] = total[half:]


def attn_send(colour, d, d_qkv, x_t, ctx_t, dab):
    width, rows = x_t.shape
    half = width // 2
    return pl.pallas_call(
        functools.partial(attn_send_kernel, colour),
        name="attn_send",
        out_shape=shape((2, half, width), bf16),
        in_specs=[SMEM_SPEC] + [VMEM_SPEC] * 4,
        out_specs=VMEM_SPEC,
        scratch_shapes=[pltpu.VMEM((half, rows), bf16)],
        compiler_params=params(24),
        cost_estimate=cost(4 * rows * half * width, 6 << 20),
    )(d, x_t, ctx_t, d_qkv, dab)


def attn_keep(colour, d, d_qkv, x_t, ctx_t, dab, got):
    width, rows = x_t.shape
    half = width // 2
    return pl.pallas_call(
        functools.partial(attn_keep_kernel, colour),
        name="attn_keep",
        out_shape=(shape((2, half // 2, width), bf16),) * 2,
        in_specs=[SMEM_SPEC] + [VMEM_SPEC] * 5,
        out_specs=(VMEM_SPEC, VMEM_SPEC),
        scratch_shapes=[pltpu.VMEM((half, rows), bf16)],
        compiler_params=params(24),
        cost_estimate=cost(4 * rows * half * width, 7 << 20),
    )(d, x_t, ctx_t, d_qkv, dab, got)


class Share:
    def __init__(self, net, line, d, z, d_qkv, x_t, ctx_t, dab):
        self.net, self.line, self.z = net, line, z
        self.folds = []
        for colour in range(2):
            sent = line.run(functools.partial(attn_send, colour, d), d_qkv, x_t, ctx_t, dab)

            def keep(got, colour=colour):
                return attn_keep(colour, d, d_qkv, x_t, ctx_t, dab, got)

            self.folds.append(Fold(net, line, colour, sent, keep))

    def first(self):
        for one in self.folds:
            one.first()

    def second(self):
        for one in self.folds:
            one.second()

    def far(self):
        n = self.net.n_t
        stacked = jnp.concatenate([one.done() for one in self.folds], axis=0)
        parts = [
            lax.dynamic_index_in_dim(stacked, lax.rem(self.z - k + n, n), 0, keepdims=False)
            for k in range(n)
        ]
        self.parts = [parts[0]] + [self.net.shift(parts[k], -k) for k in range(1, n)]

    def far_back(self):
        total = self.parts[0].astype(f32)
        for part in self.parts[1:]:
            total = total + self.line.after(part).astype(f32)
        total = total.astype(bf16)
        self.slices = [total] + [self.net.shift(total, k) for k in range(1, self.net.n_t)]

    def gather(self):
        self.gathered = Gather(self.net, self.line, self.slices)


def spread_kernel(layer, at_ref, *refs):
    held = refs[:4]
    qkv_out, wo_out, qkv_buf, wo_buf, sems = refs[-5:]
    d, z = at_ref[0], at_ref[1]
    rows, cols = held[0].shape[2:]
    for k in range(4):
        block = lax.rem(z - k + 4, 4)
        for c in range(4):
            for i, j in enumerate(order_of(c // 2)):
                value = held[c][i, k].astype(f32)
                row = jnp.bitwise_xor(d, j ^ (c % 2)) * (2 * rows) + (c // 2) * rows
                row = pl.multiple_of(row, rows)

                @pl.when(block < 3)
                def _(value=value, row=row, block=block):
                    col = pl.multiple_of(block * cols, cols)
                    qkv_buf[pl.ds(row, rows), pl.ds(col, cols)] = value

                @pl.when(block == 3)
                def _(value=value, row=row):
                    wo_buf[pl.ds(row, rows), :] = value

    one = pltpu.make_async_copy(qkv_buf, qkv_out.at[layer], sems.at[0])
    two = pltpu.make_async_copy(wo_buf, wo_out.at[layer], sems.at[1])
    one.start()
    two.start()
    one.wait()
    two.wait()


def spread_out(layer, where, pieces, before):
    rows, cols = pieces[0].shape[2:]
    width = 16 * rows
    extra = [] if before is None else list(before)
    return pl.pallas_call(
        functools.partial(spread_kernel, layer),
        name="spread_out",
        out_shape=(shape((LAYERS, width, 3 * cols), f32), shape((LAYERS, width, cols), f32)),
        in_specs=[SMEM_SPEC] + [VMEM_SPEC] * 4 + [ANY_SPEC] * len(extra),
        out_specs=(ANY_SPEC, ANY_SPEC),
        scratch_shapes=[
            pltpu.VMEM((width, 3 * cols), f32),
            pltpu.VMEM((width, cols), f32),
            pltpu.SemaphoreType.DMA((2,)),
        ],
        input_output_aliases={5: 0, 6: 1} if extra else {},
        compiler_params=params(32),
        cost_estimate=cost(0, 14 << 20),
    )(where, *pieces, *extra)


class Small:
    def __init__(self, net, line, z, value):
        self.net, self.line, self.z = net, line, z
        self.value, self.got = value, net.flip(value, 1)

    def flip(self, bit):
        self.value = self.value + self.line.after(self.got)
        self.got = self.net.flip(self.value, bit)

    def far(self):
        self.value = self.value + self.line.after(self.got)
        self.got = [self.net.shift(self.value, k) for k in range(1, self.net.n_t)]

    def done(self):
        n = self.net.n_t
        stacked = jnp.stack([self.value] + self.got)
        total = None
        for q in range(n):
            one = lax.dynamic_index_in_dim(stacked, lax.rem(self.z - q + n, n), 0, keepdims=False)
            total = one if total is None else total + one
        return total


def quick_program(
    net,
    x_in,
    bucket,
    lengths,
    qkv_weight,
    out_weight,
    norm_gain1,
    norm_bias1,
    up_weight,
    down_weight,
    norm_gain2,
    norm_bias2,
    cotangent,
):
    rows, width = x_in.shape
    d, z = lax.axis_index("dp").astype(jnp.int32), lax.axis_index("tensor").astype(jnp.int32)
    d_at, dz_at = jnp.reshape(d, (1,)), jnp.stack([d, z])
    part = width // net.n_dp
    line = Line()
    gains1, biases1 = norm_gain1[:, None], norm_bias1[:, None]
    gains2, biases2 = norm_gain2[:, None], norm_bias2[:, None]

    def own_slice(l):
        up = lax.dynamic_slice(up_weight, (l, d * part, 0, 0), (1, part, 2, width))
        down = lax.dynamic_slice(down_weight, (l, d * part, 0), (1, part, width))
        return jnp.concatenate([up.reshape(part, 2 * width), down[0]], axis=1)

    def far_slices(own):
        return {k: net.shift(own, k) for k in (1, 3, 2)}

    own = [own_slice(l) for l in range(LAYERS)]
    far = [far_slices(own[0]), None]
    seg = segments(bucket[0], lengths[0], rows, SHORT)
    same = seg[:, None] == seg[None, :]
    place = jnp.arange(rows, dtype=f32)
    dist = jnp.where(same, jnp.abs(place[:, None] - place[None, :]), 1e34)
    slopes = slopes_of()
    outputs, kept, weights = [], [], []
    x, x_t = x_in, x_in.T

    def run_attn(l, x):
        def call(x):
            return attn_fwd(l, x, qkv_weight, out_weight, norm_gain1[l], norm_bias1[l], dist, slopes)

        return line.run(call, x)

    def run_ff(groups, hb, acc, weights, norm=None):
        return line.run(lambda hb: ff_fwd(groups, d_at, hb, acc, weights, norm), hb)

    def own_weights(l):
        return [up_weight[l].reshape(width, 2 * width), down_weight[l]]

    saved = run_attn(0, x)
    qkv, lse, ctx, ctx_t, pre1, hb, hb_t = saved
    near = Gather(net, line, [far[0][1], far[0][3]])
    far[1] = far_slices(line.after(own[1]))
    mine = own_weights(0)
    acc = run_ff((None,), hb, (pre1, gains1[0], biases1[0]), mine)[0]
    near.second()
    back = Gather(net, line, [far[0][2]])
    near.core()
    back.second()
    acc = run_ff((0, 1), hb, acc, near.pieces())[0]
    back.core()
    near2 = Gather(net, line, [far[1][1], far[1][3]])
    pre2, out, out_t = run_ff((0,), hb, acc, back.pieces(), (gains2[0], biases2[0]))
    weights.append((mine + back.pieces(), near.pieces()))
    kept.append((x_t, qkv, lse, ctx_t, pre1, hb, hb_t, pre2))
    outputs.append(out)
    near2.second()
    back2 = Gather(net, line, [far[1][2]])
    qkv, lse, ctx, ctx_t, pre1, hb, hb_t = run_attn(1, out)
    near2.core()
    back2.second()
    mine = own_weights(1)
    acc = run_ff((None, 0, 1), hb, (pre1, gains1[1], biases1[1]), mine + near2.pieces())[0]
    back2.core()
    pre2, out, _ = run_ff((0,), hb, acc, back2.pieces(), (gains2[1], biases2[1]))
    weights.append((mine + back2.pieces(), near2.pieces()))
    kept.append((out_t, qkv, lse, ctx_t, pre1, hb, hb_t, pre2))
    outputs.append(out)

    def run_norm(grad, pre, gain):
        return line.run(lambda grad: norm_bwd(grad, pre, gain), grad)

    def run_ff_bwd(groups, hb, dyb, acc, weights):
        return line.run(lambda hb: ff_bwd(groups, d_at, hb, dyb, acc, weights), hb)

    def run_send(colour, r, hb_t, dyb_t):
        sent = line.run(lambda r: ff_send(colour, d_at, hb_t, dyb_t, r), r)
        return Fold(
            net, line, colour, sent, lambda got: ff_keep(colour, d_at, hb_t, dyb_t, r, got)
        )

    def to_owners(folded, shifts):
        return [
            folded[i] if k == 0 else net.shift(folded[i], -k) for i, k in enumerate(shifts)
        ]

    def run_grad(l, d_qkv, d_pre1):
        return line.run(lambda d_qkv: d_pre1 + dot(d_qkv, qkv_weight[l].T), d_qkv)

    ff_parts = {}
    x_t, qkv, lse, ctx_t, pre1, hb, hb_t, pre2 = kept[1]
    d_pre2, dyb, dyb_t, small2 = run_norm(cotangent, pre2, norm_gain2[1])
    r, d_h = run_ff_bwd((None, 0), hb, dyb, d_pre2, weights[1][0])
    fold0 = run_send(0, r, hb_t, dyb_t)
    r, d_h = run_ff_bwd((0, 1), hb, dyb, d_h, weights[1][1])
    fold1 = run_send(1, r, hb_t, dyb_t)
    fold0.first()
    d_pre1, dab, _, small1 = run_norm(d_h, pre1, norm_gain1[1])
    small = {1: jnp.concatenate([small1, small2], axis=0)}
    fold1.first()
    d_qkv = line.run(
        lambda dab: attn_bwd(1, dab, qkv, lse, out_weight, dist, slopes), dab
    )
    fold0.second()
    share = Share(net, line, d_at, z, d_qkv, x_t, ctx_t, dab)
    fold1.second()
    grad = run_grad(1, d_qkv, d_pre1)
    share.first()
    ff_parts[1] = to_owners(fold0.done(), (0, 2))
    x_t, qkv, lse, ctx_t, pre1, hb, hb_t, pre2 = kept[0]
    d_pre2, dyb, dyb_t, small2 = run_norm(grad, pre2, norm_gain2[0])
    ff_parts[1] += to_owners(fold1.done(), (1, 3))
    r, d_h = run_ff_bwd((None, 0), hb, dyb, d_pre2, weights[0][0])
    share.second()
    fold0 = run_send(0, r, hb_t, dyb_t)
    r, d_h = run_ff_bwd((0, 1), hb, dyb, d_h, weights[0][1])
    share.far()
    fold1 = run_send(1, r, hb_t, dyb_t)
    fold0.first()
    d_pre1, dab, _, small1 = run_norm(d_h, pre1, norm_gain1[0])
    small[0] = jnp.concatenate([small1, small2], axis=0)
    few = Small(net, line, z, jnp.concatenate([small[0], small[1]], axis=0))
    share.far_back()
    fold1.first()
    few.flip(2)
    d_qkv = line.run(
        lambda dab: attn_bwd(0, dab, qkv, lse, out_weight, dist, slopes), dab
    )
    share.gather()
    fold0.second()
    few.flip(4)
    last_share = Share(net, line, d_at, z, d_qkv, x_t, ctx_t, dab)
    fold1.second()
    few.far()
    share.gathered.second()
    last_share.first()
    ff_parts[0] = to_owners(fold0.done(), (0, 2))
    share.gathered.core()
    last_share.second()
    ff_parts[0] += to_owners(fold1.done(), (1, 3))
    last_share.far()
    grad = run_grad(0, d_qkv, d_pre1)
    last_share.far_back()
    attention_grads = line.run(
        lambda first: spread_out(1, dz_at, [first] + share.gathered.pieces()[1:], None),
        share.gathered.pieces()[0],
    )
    last_share.gather()
    last_share.gathered.second()
    last_share.gathered.core()
    attention_grads = spread_out(0, dz_at, last_share.gathered.pieces(), attention_grads)
    small = few.done().reshape(LAYERS, 4, width)
    up_grads, down_grads = [], []
    for l in range(LAYERS):
        total = ff_parts[l][0].astype(f32)
        for one in ff_parts[l][1:]:
            total = total + one.astype(f32)
        up_grads.append(total[:, : 2 * width].reshape(part, 2, width))
        down_grads.append(total[:, 2 * width :].T)
    return (
        jnp.stack(outputs),
        grad,
        attention_grads[0],
        attention_grads[1],
        small[:, 0],
        small[:, 1],
        jnp.stack(up_grads),
        jnp.stack(down_grads),
        small[:, 2],
        small[:, 3],
    )


def attention_forward(x_low, wqkv, wo, g1, b1, same, decay):
    rows, width = x_low.shape
    qkv_low = dot(x_low, wqkv).astype(bf16)
    query, keys, values = split_heads(qkv_low, width)
    scores = scores_of(query, keys, same, decay)
    top = jnp.max(scores, axis=-1, keepdims=True)
    log_total = top + jnp.log(jnp.sum(jnp.exp(scores - top), axis=-1, keepdims=True))
    probs_low = jnp.exp(scores - log_total).astype(bf16)
    ctx_low = (
        jnp.einsum("hqk,khe->qhe", probs_low, values, preferred_element_type=f32)
        .reshape(rows, width)
        .astype(bf16)
    )
    pre_first = x_low.astype(f32) + dot(ctx_low, wo)
    normed = layer_norm(pre_first, g1, b1)
    return normed, (qkv_low, log_total, ctx_low, pre_first)


def attention_backward(d_attn_low, qkv_low, log_total, ctx_low, wo, same, decay):
    rows, width = d_attn_low.shape
    d_ctx = dot(d_attn_low, wo.T).astype(bf16).reshape(rows, HEADS, HEAD_DIM)
    query, keys, values = split_heads(qkv_low, width)
    probs = jnp.exp(scores_of(query, keys, same, decay) - log_total)
    probs_low = probs.astype(bf16)
    d_values = jnp.einsum("hqk,qhe->khe", probs_low, d_ctx, preferred_element_type=f32)
    d_probs = jnp.einsum("qhe,khe->hqk", d_ctx, values, preferred_element_type=f32)
    d_scores = (probs * (d_probs - jnp.sum(probs * d_probs, axis=-1, keepdims=True))).astype(bf16)
    d_query = jnp.einsum("hqk,khe->qhe", d_scores, keys, preferred_element_type=f32)
    d_keys = jnp.einsum("hqk,qhe->khe", d_scores, query, preferred_element_type=f32)
    scale = HEAD_DIM ** (-0.5)
    return jnp.concatenate(
        [
            (d_query * scale).reshape(rows, width),
            (d_keys * scale).reshape(rows, width),
            d_values.reshape(rows, width),
        ],
        axis=1,
    ).astype(bf16)


def plain_program(
    net,
    x_in,
    bucket,
    lengths,
    qkv_weight,
    out_weight,
    norm_gain1,
    norm_bias1,
    up_weight,
    down_weight,
    norm_gain2,
    norm_bias2,
    cotangent,
):
    rows, width = x_in.shape
    n_t = net.n_t
    hidden = down_weight.shape[1]
    seg = segments(bucket[0], lengths[0], rows, SHORT)
    same = seg[:, None] == seg[None, :]
    decay = alibi(rows, HEADS)
    ups = lax.all_gather(up_weight, "tensor", axis=0)
    downs = lax.all_gather(down_weight, "tensor", axis=0)
    groups = [
        [(ups[k, l].reshape(width, -1), downs[k, l]) for k in range(n_t)] for l in range(LAYERS)
    ]
    layer_in = x_in
    outputs, kept = [], []
    for l in range(LAYERS):
        x_low = layer_in
        normed, keep = attention_forward(
            x_low, qkv_weight[l], out_weight[l], norm_gain1[l], norm_bias1[l], same, decay
        )
        hb = normed.astype(bf16)
        pre_second = normed
        joined, act = [], []
        for up, down in groups[l]:
            joined.append(dot(hb, up))
            act.append(geglu(joined[-1]).astype(bf16))
            pre_second = pre_second + dot(act[-1], down)
        layer_in = layer_norm(pre_second, norm_gain2[l], norm_bias2[l]).astype(bf16)
        outputs.append(layer_in)
        kept.append((x_low, *keep, hb, pre_second, joined, act))
    grad = cotangent.astype(f32)
    attention_grads, small, up_grads, down_grads = ([None] * LAYERS for _ in range(4))
    for l in reversed(range(LAYERS)):
        x_low, qkv_low, log_total, ctx_low, pre_first, hb, pre_second, joined, act = kept[l]
        pull = jax.vjp(layer_norm, pre_second, norm_gain2[l], norm_bias2[l])[1]
        d_pre2, d_gain2, d_bias2 = pull(grad)
        dyb = d_pre2.astype(bf16)
        d_h = d_pre2
        d_joined = []
        for k, (up, down) in enumerate(groups[l]):
            d_act = dot(dyb, down.T)
            d_joined.append(jax.vjp(geglu, joined[k])[1](d_act)[0].astype(bf16))
            d_h = d_h + dot(d_joined[k], up.T)
        d_up = jnp.stack([dot(hb.T, one) for one in d_joined]).astype(bf16)
        d_down = jnp.stack([dot(dyb.T, one) for one in act]).astype(bf16)
        d_up = lax.psum_scatter(d_up, "tensor", scatter_dimension=0)
        d_down = lax.psum_scatter(d_down, "tensor", scatter_dimension=0)
        d_up = lax.psum_scatter(d_up, "dp", scatter_dimension=0, tiled=True)
        d_down = lax.psum_scatter(d_down, "dp", scatter_dimension=0, tiled=True)
        up_grads[l], down_grads[l] = d_up.astype(f32), d_down.astype(f32)
        pull = jax.vjp(layer_norm, pre_first, norm_gain1[l], norm_bias1[l])[1]
        d_pre1, d_gain1, d_bias1 = pull(d_h)
        small[l] = [d_gain1, d_bias1, d_gain2, d_bias2]
        dab = d_pre1.astype(bf16)
        d_qkv = attention_backward(dab, qkv_low, log_total, ctx_low, out_weight[l], same, decay)
        found = lax.psum(
            (dot(x_low.T, d_qkv).astype(bf16), dot(ctx_low.T, dab).astype(bf16)), BOTH
        )
        attention_grads[l] = [one.astype(f32) for one in found]
        grad = d_pre1 + dot(d_qkv, qkv_weight[l].T)
    small = lax.psum(jnp.stack(small[0] + small[1]), BOTH).reshape(LAYERS, 4, width)
    return (
        jnp.stack(outputs),
        grad,
        jnp.stack([one[0] for one in attention_grads]),
        jnp.stack([one[1] for one in attention_grads]),
        small[:, 0],
        small[:, 1],
        jnp.stack(up_grads).reshape(LAYERS, -1, 2, hidden),
        jnp.stack([one.T for one in down_grads]),
        small[:, 2],
        small[:, 3],
    )


def program(net, *args):
    width, hidden = args[0].shape[1], args[8].shape[1]
    quick = net.n_dp == 8 and net.n_t == 4 and hidden == width and width % 256 == 0
    return (quick_program if quick else plain_program)(net, *args)


def solution(mesh):
    in_specs = (
        P(BOTH, None),
        P(BOTH),
        P(BOTH, None),
        P(),
        P(),
        P(),
        P(),
        P(None, None, None, "tensor"),
        P(None, "tensor", None),
        P(),
        P(),
        P(BOTH, None),
    )
    out_specs = (
        P(None, BOTH, None),
        P(BOTH, None),
        P(),
        P(),
        P(),
        P(),
        P(None, "dp", None, "tensor"),
        P(None, "tensor", "dp"),
        P(),
        P(),
    )
    net = Net(mesh)
    return jax.shard_map(
        functools.partial(program, net),
        mesh=mesh,
        in_specs=in_specs,
        out_specs=out_specs,
        check_vma=False,
    )
```

```python
import functools

import jax
import jax.numpy as jnp
from jax import lax
from jax.experimental import pallas as pl
from jax.experimental.pallas import tpu as pltpu
from jax.sharding import PartitionSpec as P

HEADS = 12
HEAD_DIM = 64
SHORT = 128
LAYERS = 2

eps_norm = 1e-05
gelu_coef = 0.7978845608028654
masked_score = -1e30
bf16 = jnp.bfloat16
f32 = jnp.float32
BOTH = ("dp", "tensor")


def segments(bucket_one, lens, rows_dev, short_len):
    rows = jnp.arange(rows_dev, dtype=jnp.int32)
    slot = rows // short_len
    offset = rows - slot * short_len
    slots_all = jnp.arange(lens.shape[0], dtype=jnp.int32)
    slot_len = jnp.sum(jnp.where(slot[:, None] == slots_all[None, :], lens[None, :], 0), axis=1)
    total = jnp.sum(lens)
    is_long = bucket_one == 1
    real = jnp.where(is_long, rows < total, offset < slot_len)
    group = jnp.where(is_long, 0, slot)
    return jnp.where(real, group, lens.shape[0] + rows)


def alibi(rows_dev, heads):
    slopes = jnp.exp2(-8.0 * (jnp.arange(heads, dtype=f32) + 1.0) / heads)
    place = jnp.arange(rows_dev, dtype=f32)
    dist = jnp.abs(place[:, None] - place[None, :])
    return slopes[:, None, None] * dist[None, :, :]


def layer_norm(value, gain, bias):
    mean = jnp.mean(value, axis=-1, keepdims=True)
    centered = value - mean
    var = jnp.mean(centered * centered, axis=-1, keepdims=True)
    return centered * lax.rsqrt(var + eps_norm) * gain + bias


def geglu(joined):
    half = joined.shape[1] // 2
    gate = joined[:, :half]
    value = joined[:, half:]
    return 0.5 * gate * (1.0 + jnp.tanh(gelu_coef * (gate + 0.044715 * gate * gate * gate))) * value


def split_heads(qkv_low, width):
    rows = qkv_low.shape[0]
    query = qkv_low[:, :width].reshape(rows, HEADS, HEAD_DIM)
    keys = qkv_low[:, width : 2 * width].reshape(rows, HEADS, HEAD_DIM)
    values = qkv_low[:, 2 * width :].reshape(rows, HEADS, HEAD_DIM)
    return (query, keys, values)


def scores_of(query, keys, same, decay):
    raw = (
        jnp.einsum("qhe,khe->hqk", query, keys, preferred_element_type=f32) * HEAD_DIM ** (-0.5)
        - decay
    )
    return jnp.where(same[None, :, :], raw, masked_score)


def dot(a, b):
    return jnp.dot(a, b, preferred_element_type=f32)


class Net:
    def __init__(self, mesh):
        self.n_dp = mesh.shape["dp"]
        self.n_t = mesh.shape["tensor"]
        self.flying = []

    def flip(self, value, bit):
        got = lax.ppermute(value, "dp", [(i, i ^ bit) for i in range(self.n_dp)])
        self.flying.append(got)
        return got

    def shift(self, value, step):
        n = self.n_t
        got = lax.ppermute(value, "tensor", [(i, (i + step) % n) for i in range(n)])
        self.flying.append(got)
        return got


CHIPS = (0, 2, 4, 6)
COLOURS = ((2, 4), (4, 2))


def order_of(colour):
    one, two = COLOURS[colour]
    return [0, one, two, one ^ two]


def fold_order(colour):
    one, two = COLOURS[colour]
    return [0, two, one, one ^ two]


class Line:
    def __init__(self, net):
        self.net = net
        self.last = []

    def after(self, value):
        if not self.last:
            return value
        return lax.optimization_barrier((value, *self.last))[0]

    def sync(self):
        self.need(*self.net.flying)
        self.net.flying = []

    def need(self, *values):
        self.last = self.last + list(values)

    def run(self, call, first, *rest):
        out = call(self.after(first), *rest)
        self.last = [out[0] if isinstance(out, (tuple, list)) else out]
        self.sync()
        return out


class Gather:
    def __init__(self, net, line, slices):
        self.net, self.line = net, line
        held = jnp.stack([line.after(one) for one in slices])
        self.held = [held] + [net.flip(held, bit) for bit in CHIPS[1:]]

    def core(self):
        self.held = jnp.stack([self.line.after(one) for one in self.held])
        self.got = self.net.flip(self.held, 1)

    def pieces(self):
        return [self.held, self.got]


class Gather2:
    def __init__(self, net, line, slices):
        self.net, self.line = net, line
        n = len(slices) // 2
        self.held = [
            jnp.stack([line.after(one) for one in slices[c * n : (c + 1) * n]])[None]
            for c in range(2)
        ]
        self.got = [net.flip(self.held[c], COLOURS[c][0]) for c in range(2)]

    def join(self):
        self.held = [
            jnp.concatenate([self.held[c], self.line.after(self.got[c])], axis=0) for c in range(2)
        ]

    def second(self):
        self.join()
        self.got = [self.net.flip(self.held[c], COLOURS[c][1]) for c in range(2)]

    def core(self):
        self.join()
        self.got = [self.net.flip(self.held[c], 1) for c in range(2)]

    def pieces(self):
        return [one for c in range(2) for one in (self.held[c], self.got[c])]


VMEM_SPEC = pl.BlockSpec(memory_space=pltpu.VMEM)
ANY_SPEC = pl.BlockSpec(memory_space=pl.ANY)
SMEM_SPEC = pl.BlockSpec(memory_space=pltpu.SMEM)
NN = (((1,), (0,)), ((), ()))
NT = (((1,), (1,)), ((), ()))
TN = (((0,), (0,)), ((), ()))


def mm(a, b, dims=NN):
    return lax.dot_general(a, b, dims, preferred_element_type=f32)


def params(mib):
    return pltpu.CompilerParams(vmem_limit_bytes=60 << 20)


def cost(flops, nbytes):
    return pl.CostEstimate(flops=1024, transcendentals=0, bytes_accessed=1024)


def shape(dims, kind):
    return jax.ShapeDtypeStruct(dims, kind)


HBM_SPEC = pl.BlockSpec(memory_space=pltpu.MemorySpace.HBM)


class Copies:
    def __init__(self, ins, outs, sems):
        self.ins = [pltpu.make_async_copy(src, dst, sems.at[i]) for i, (src, dst) in enumerate(ins)]
        n = len(ins)
        self.outs = [
            pltpu.make_async_copy(src, dst, sems.at[n + i]) for i, (src, dst) in enumerate(outs)
        ]
        self.waited, self.put_out = set(), set()
        for copy in self.ins:
            copy.start()

    def wait(self, *which):
        for i in which or range(len(self.ins)):
            if i not in self.waited:
                self.waited.add(i)
                self.ins[i].wait()

    def put(self, *which):
        for i in which or range(len(self.outs)):
            if i not in self.put_out:
                self.put_out.add(i)
                self.outs[i].start()

    def finish(self):
        self.put()
        for copy in self.outs:
            copy.wait()


def staged_kernel(body, layers, n_smem, n_raw, n_out, n_raw_out, *refs):
    n_in = len(layers)
    smem, refs = refs[:n_smem], refs[n_smem:]
    ins, refs = refs[:n_in], refs[n_in:]
    raw, refs = refs[:n_raw], refs[n_raw:]
    outs, refs = refs[:n_out], refs[n_out:]
    raw_outs, refs = refs[:n_raw_out], refs[n_raw_out:]
    held, refs = refs[:n_in], refs[n_in:]
    made, refs = refs[:n_out], refs[n_out:]
    sems, scratch = refs[0], refs[1:]
    copies = Copies(
        [
            (ref if layer is None else ref.at[layer], to)
            for ref, layer, to in zip(ins, layers, held)
        ],
        list(zip(made, outs)),
        sems,
    )
    body(copies, smem, held, raw, made, raw_outs, scratch)
    copies.finish()


def staged(body, name, smem, ins, raw, outs, raw_outs, scratch, mib, work, aliases=None):
    pairs = [one if isinstance(one, tuple) else (one, None) for one in ins]
    layers = [layer for _, layer in pairs]
    held = [
        pltpu.VMEM(one.shape if layer is None else one.shape[1:], one.dtype) for one, layer in pairs
    ]
    made = [pltpu.VMEM(one.shape, one.dtype) for one in outs]
    n_copies = len(pairs) + len(outs)
    found = pl.pallas_call(
        functools.partial(
            staged_kernel, body, layers, len(smem), len(raw), len(outs), len(raw_outs)
        ),
        name=name,
        out_shape=tuple(outs) + tuple(raw_outs),
        in_specs=[SMEM_SPEC] * len(smem) + [HBM_SPEC] * (len(pairs) + len(raw)),
        out_specs=(HBM_SPEC,) * (len(outs) + len(raw_outs)),
        scratch_shapes=held + made + [pltpu.SemaphoreType.DMA((n_copies,))] + scratch,
        input_output_aliases=aliases or {},
        compiler_params=params(mib),
        cost_estimate=work,
    )(*smem, *[one for one, _ in pairs], *raw)
    return found


def normed_of(value):
    mean = jnp.mean(value, axis=-1, keepdims=True)
    centered = value - mean
    var = jnp.mean(centered * centered, axis=-1, keepdims=True)
    rstd = lax.rsqrt(var + eps_norm)
    return centered * rstd, rstd


def norm_back(grad, xhat, rstd, gain):
    scaled = grad * gain
    first = jnp.mean(scaled, axis=-1, keepdims=True)
    second = jnp.mean(scaled * xhat, axis=-1, keepdims=True)
    return rstd * (scaled - first - xhat * second)


def attn_fwd_kernel(copies, smem, ins, raw, outs, raw_outs, scratch):
    (slopes,) = smem
    x_ref, wqkv_ref, dist_ref, wo_ref, g_ref, b_ref = ins
    qkv_ref, lse_ref, ctx_ref, ctx_t_ref, pre_ref, hb_ref, hb_t_ref = outs
    rows, width = x_ref.shape
    copies.wait(0, 1)
    x = x_ref[...]
    for c in range(3):
        cols = pl.ds(c * width, width)
        qkv_ref[:, cols] = mm(x, wqkv_ref[:, cols]).astype(bf16)
    copies.put(0)
    copies.wait()
    lse_ref[...] = jnp.zeros_like(lse_ref)
    s_ref, p_ref = scratch

    def pair(p, _):
        def at(c):
            return pl.ds(pl.multiple_of(c * width + p * 128, 128), 128)

        key, val = qkv_ref[:, at(1)], qkv_ref[:, at(2)]
        query = qkv_ref[:, at(0)] * bf16(HEAD_DIM ** (-0.5))
        wide = lax.broadcasted_iota(jnp.int32, (rows, 128), 1)
        for side in range(2):
            mine = (wide < HEAD_DIM) == (side == 0)
            s_ref[side] = mm(jnp.where(mine, query, bf16(0)), key, NT)

        dist = dist_ref[...]
        total_lse = lse_ref[...]
        for side in range(2):
            s = s_ref[side] - slopes[2 * p + side] * dist
            top = jnp.max(s, axis=-1, keepdims=True)
            e = jnp.exp(s - top)
            total = jnp.sum(e, axis=-1, keepdims=True)
            p_ref[side] = (e * (1.0 / total)).astype(bf16)
            total_lse += jnp.where(wide == 2 * p + side, top + jnp.log(total), 0.0)
        lse_ref[...] = total_lse
        found = [mm(p_ref[side], val) for side in range(2)]
        ctx_ref[:, at(0)] = jnp.where(wide < HEAD_DIM, found[0], found[1]).astype(bf16)
        return 0

    lax.fori_loop(0, width // 128, pair, 0)
    copies.put(1, 2)
    ctx = ctx_ref[...]
    pre = x.astype(f32) + mm(ctx, wo_ref[...])
    pre_ref[...] = pre
    ctx_t_ref[...] = ctx.T
    copies.put(3, 4)
    xhat, _ = normed_of(pre)
    hb = (xhat * g_ref[...] + b_ref[...]).astype(bf16)
    hb_ref[...] = hb
    hb_t_ref[...] = hb.T


def slopes_of():
    steps = jnp.arange(HEADS, dtype=f32)
    return jnp.exp2(-8.0 * (steps + 1.0) / HEADS)


def attn_fwd(layer, x, wqkv, wo, gain, bias, dist, slopes):
    rows, width = x.shape
    return staged(
        attn_fwd_kernel,
        "attn_fwd",
        [slopes],
        [x, (wqkv, layer), dist, (wo, layer), gain, bias],
        [],
        [
            shape((rows, 3 * width), bf16),
            shape((rows, 128), f32),
            shape((rows, width), bf16),
            shape((width, rows), bf16),
            shape((rows, width), f32),
            shape((rows, width), bf16),
            shape((width, rows), bf16),
        ],
        [],
        [pltpu.VMEM((2, rows, rows), f32), pltpu.VMEM((2, rows, rows), bf16)],
        36,
        cost(0, 0),
    )


def attn_bwd_kernel(copies, smem, ins, raw, outs, raw_outs, scratch):
    slopes, at_ref = smem
    dab_ref, wo_ref, qkv_ref, lse_ref, dist_ref, x_t_ref, c_t_ref, wqkv_ref, dpre_ref = ins[:9]
    small_refs = ins[9:]
    dctx_ref, s_ref, dp_ref, p_ref, ds_ref, out_ref, rows_ref = scratch
    sent_ref, kept_ref, grad_ref = outs
    rows, width = dab_ref.shape
    scale = HEAD_DIM ** (-0.5)
    copies.wait(0, 1)
    dctx_ref[...] = mm(dab_ref[...], wo_ref[...], NT).astype(bf16)
    copies.wait(2, 3, 4)
    def pair(p, _):
        def at(c):
            return pl.ds(pl.multiple_of(c * width + p * 128, 128), 128)

        key, val, query = qkv_ref[:, at(1)], qkv_ref[:, at(2)], qkv_ref[:, at(0)]
        dctx = dctx_ref[:, at(0)]
        wide = lax.broadcasted_iota(jnp.int32, (rows, 128), 1)
        low = wide < HEAD_DIM
        for side in range(2):
            mine = low == (side == 0)
            s_ref[side] = mm(jnp.where(mine, query * bf16(scale), bf16(0)), key, NT)
            dp_ref[side] = mm(jnp.where(mine, dctx, bf16(0)), val, NT)

        dist = dist_ref[...]
        for side in range(2):
            lse = jnp.sum(jnp.where(wide == 2 * p + side, lse_ref[...], 0.0), axis=-1, keepdims=True)
            prob = jnp.exp(s_ref[side] - slopes[2 * p + side] * dist - lse)
            d_prob = dp_ref[side]
            mean = jnp.sum(prob * d_prob, axis=-1, keepdims=True)
            p_ref[side] = prob.astype(bf16)
            ds_ref[side] = (prob * (d_prob - mean)).astype(bf16)
        d_q = [mm(ds_ref[side], key) for side in range(2)]
        query_t, dctx_t = query.T, dctx.T
        d_k = [mm(query_t, ds_ref[side]).T for side in range(2)]
        d_v = [mm(dctx_t, p_ref[side]).T for side in range(2)]
        out_ref[:, at(0)] = (jnp.where(low, d_q[0], d_q[1]) * scale).astype(bf16)
        out_ref[:, at(1)] = (jnp.where(low, d_k[0], d_k[1]) * scale).astype(bf16)
        out_ref[:, at(2)] = jnp.where(low, d_v[0], d_v[1]).astype(bf16)
        return 0

    lax.fori_loop(0, width // 128, pair, 0)
    part = width // 8
    copies.wait()
    for colour in range(2):
        order = fold_order(colour)
        order = order + [j ^ 1 for j in order]
        pick_rows(at_ref[0], order, x_t_ref, rows_ref)
        for block in (2 * colour, 2 * colour + 1):
            if block < 3:
                rhs = out_ref[:, pl.ds(block * width, width)]
            else:
                rhs = dab_ref[...]
                pick_rows(at_ref[0], order, c_t_ref, rows_ref)
            total = mm(rows_ref[...], rhs).astype(bf16)
            few = small_refs[block // 2][block % 2 : block % 2 + 1]
            for i, j in enumerate(order):
                to = (kept_ref, sent_ref)[i // 4].at[block, i % 4]
                to[pl.ds(0, part)] = total[i * part : (i + 1) * part]
                here = jnp.where(jnp.bitwise_xor(at_ref[0], j) == 0, few, 0.0)
                to[pl.ds(part, FEW)] = jnp.broadcast_to(here, (FEW, width)).astype(bf16)
    copies.put(0, 1)
    grad_ref[...] = dpre_ref[...] + mm(out_ref[...], wqkv_ref[...], NT)


FEW = 8


def attn_bwd(layer, d, dab, qkv, lse, wo, dist, slopes, d_pre, x_t, ctx_t, wqkv, small):
    rows, width = dab.shape
    part = shape((4, 4, width // 8 + FEW, width), bf16)
    return staged(
        attn_bwd_kernel,
        "attn_bwd",
        [slopes, d],
        [dab, (wo, layer), qkv, lse, dist, x_t, ctx_t, (wqkv, layer), d_pre, *small],
        [],
        [part, part, shape((rows, width), f32)],
        [],
        [
            pltpu.VMEM((rows, width), bf16),
            pltpu.VMEM((2, rows, rows), f32),
            pltpu.VMEM((2, rows, rows), f32),
            pltpu.VMEM((2, rows, rows), bf16),
            pltpu.VMEM((2, rows, rows), bf16),
            pltpu.VMEM((rows, 3 * width), bf16),
            pltpu.VMEM((width, rows), bf16),
        ],
        40,
        cost(0, 0),
    )


def load_groups(groups, d, refs, w_ref, sems, slots):
    loads = []
    at = 0
    sources = {}
    for g, (kind, index) in enumerate(groups):
        mine = []
        s = g % slots
        count = {"own": 2, "pair": 2, "two": 4, "all": 1}[kind]
        if kind not in sources:
            sources[kind] = refs[at : at + count]
            at += count
        source = sources[kind]
        if kind == "own":
            split = source[0].shape[1]
            rest = source[1].shape[1]
            pairs = [
                (source[0], w_ref.at[s, :, pl.ds(0, split)]),
                (source[1], w_ref.at[s, :, pl.ds(split, rest)]),
            ]
        elif kind == "all":
            part = source[0].shape[2]
            pairs = [(source[0].at[j, index], w_ref.at[s, pl.ds(j * part, part)]) for j in range(8)]
        else:
            colour, place = index if kind == "two" else (0, index)
            chips = order_of(colour) if kind == "two" else CHIPS
            part = source[0].shape[2]
            pairs = []
            for c in range(2):
                for i, j in enumerate(chips):
                    row = pl.multiple_of(jnp.bitwise_xor(d, j ^ c) * part, part)
                    pairs.append(
                        (source[2 * colour + c].at[i, place], w_ref.at[s, pl.ds(row, part)])
                    )
        for i, (one, to) in enumerate(pairs):
            mine.append(pltpu.make_async_copy(one, to, sems.at[g, i]))
        loads.append(mine)
    return loads


def gelu_parts(gate):
    square = gate * gate
    t = jnp.tanh(gelu_coef * gate * (1.0 + 0.044715 * square))
    half = 0.5 * (1.0 + t)
    slope = half + 0.5 * gate * (1.0 - t * t) * gelu_coef * (1.0 + 3 * 0.044715 * square)
    return gate * half, slope


TILE = 768


def ff_fwd_kernel(groups, first, last, copies, smem, ins, raw, outs, raw_outs, scratch):
    (at_ref,) = smem
    hb_ref, acc_refs, norm_refs = ins[0], ins[1 : 4 if first else 2], ins[4 if first else 2 :]
    pre_ref = outs[0]
    w_ref, sems = scratch
    width = hb_ref.shape[1]
    loads = load_groups(groups, at_ref[0], raw, w_ref, sems, len(groups))
    for load in loads:
        for copy in load:
            copy.start()
    copies.wait()
    if first:
        xhat, _ = normed_of(acc_refs[0][...])
        pre_ref[...] = xhat * acc_refs[1][...] + acc_refs[2][...]
    else:
        pre_ref[...] = acc_refs[0][...]
    for s in range(len(groups)):
        for copy in loads[s]:
            copy.wait()

        def step(n, _, s=s):
            def at(c):
                return pl.ds(pl.multiple_of(c * width + n * TILE, TILE), TILE)

            hb = hb_ref[...]
            gate, value = mm(hb, w_ref[s, :, at(0)]), mm(hb, w_ref[s, :, at(1)])
            act = (gelu_parts(gate)[0] * value).astype(bf16)
            pre_ref[...] += mm(act, w_ref[s, at(0), pl.ds(2 * width, width)])
            return 0

        step(0, 0)
    if last:
        copies.put(0)
        xhat, _ = normed_of(pre_ref[...])
        out = (xhat * norm_refs[0][...] + norm_refs[1][...]).astype(bf16)
        outs[1][...] = out
        outs[2][...] = out.T


def ff_fwd(groups, d, hb, acc, weights, norm=None):
    rows, width = hb.shape
    last = norm is not None
    acc = acc if isinstance(acc, tuple) else (acc,)
    outs = [shape((rows, width), f32)]
    if last:
        outs += [shape((rows, width), bf16), shape((width, rows), bf16)]
    n = len(groups)
    return staged(
        functools.partial(ff_fwd_kernel, groups, len(acc) == 3, last),
        "ff_fwd",
        [d],
        [hb, *acc, *(norm if last else ())],
        weights,
        outs,
        [],
        [
            pltpu.VMEM((n, width, 3 * width), bf16),
            pltpu.SemaphoreType.DMA((n, 16)),
        ],
        36,
        cost(0, 0),
    )


def pick_rows(d, order, from_ref, to_ref):
    rows = from_ref.shape[0] // 8
    for i, j in enumerate(order):
        at = pl.multiple_of(jnp.bitwise_xor(d, j) * rows, rows)
        to_ref[pl.ds(i * rows, rows), :] = from_ref[pl.ds(at, rows), :]


def norm_bwd(grad, pre, gain_ref, small_ref):
    xhat, rstd = normed_of(pre)
    small_ref[0:1] = jnp.sum(grad * xhat, axis=0, keepdims=True)
    small_ref[1:2] = jnp.sum(grad, axis=0, keepdims=True)
    return norm_back(grad, xhat, rstd, gain_ref[...])


def ff_bwd_kernel(groups, first, last, slot, copies, smem, ins, raw, outs, raw_outs, scratch):
    (at_ref,) = smem
    hb_ref, hb_t_ref, *ins = ins
    w_ref, g_ref, sems, out_sems = scratch
    width = hb_ref.shape[1]
    part = width // 8
    n = len(groups)
    loads = load_groups(groups, at_ref[0], raw, w_ref, sems, 2)
    for copy in loads[0]:
        copy.start()
    copies.wait()
    dh_ref, *outs = outs
    if first:
        grad_ref, pre_ref, gain_ref, *ins = ins
        dyb_ref, dyb_t_ref, small2_ref, *outs = outs
        d_pre = norm_bwd(grad_ref[...].astype(f32), pre_ref[...], gain_ref, small2_ref)
        dh_ref[...] = d_pre
        dyb_ref[...] = d_pre.astype(bf16)
        dyb_t_ref[...] = dyb_ref[...].T
    else:
        dyb_ref, dyb_t_ref, acc_ref, *ins = ins
        dh_ref[...] = acc_ref[...]
    out = []
    for s in range(n):
        if s + 1 < n:
            for copy in loads[s + 1]:
                copy.start()
        for copy in loads[s]:
            copy.wait()
        if s >= 2:
            out[s - 2].wait()
        weights = w_ref.at[s % 2]
        grads = g_ref.at[s % 2]

        def at(c):
            return pl.ds(c * width, width)

        hb = hb_ref[...]
        gate, value = mm(hb, weights[:, at(0)]), mm(hb, weights[:, at(1)])
        d_act = mm(dyb_ref[...], weights[:, at(2)], NT)
        gelu, slope = gelu_parts(gate)
        d_gate = (d_act * value * slope).astype(bf16)
        d_value = (d_act * gelu).astype(bf16)
        act = (gelu * value).astype(bf16)
        dh_ref[...] += mm(d_gate, weights[:, at(0)], NT) + mm(d_value, weights[:, at(1)], NT)
        for c, (lhs, rhs) in enumerate(((hb_t_ref, d_gate), (hb_t_ref, d_value), (dyb_t_ref, act))):
            total = mm(lhs[...], rhs).astype(bf16)
            for j in range(8):
                grads[j, :, at(c)] = total[j * part : (j + 1) * part]
        out.append(pltpu.make_async_copy(grads, raw_outs[0].at[:, slot + s], out_sems.at[s]))
        out[s].start()
    if last:
        pre_ref, gain_ref = ins
        dab_ref, small1_ref = outs
        d_pre = norm_bwd(dh_ref[...], pre_ref[...], gain_ref, small1_ref)
        dh_ref[...] = d_pre
        dab_ref[...] = d_pre.astype(bf16)
    for one in out[-2:]:
        one.wait()


def ff_bwd(groups, slot, d, hb, hb_t, ins, weights, first=False, last=False, into=None):
    rows, width = hb.shape
    n = len(groups)
    low, few = shape((rows, width), bf16), shape((2, width), f32)
    outs = [shape((rows, width), f32)]
    outs += [low, shape((width, rows), bf16), few] if first else []
    outs += [low, few] if last else []
    extra = [] if into is None else [into]
    n_in = 3 + len(ins) + len(weights)
    return staged(
        functools.partial(ff_bwd_kernel, groups, first, last, slot),
        "ff_bwd",
        [d],
        [hb, hb_t, *ins],
        weights + extra,
        outs,
        [shape((8, 4, width // 8, 3 * width), bf16)],
        [
            pltpu.VMEM((2, width, 3 * width), bf16),
            pltpu.VMEM((2, 8, width // 8, 3 * width), bf16),
            pltpu.SemaphoreType.DMA((n, 16)),
            pltpu.SemaphoreType.DMA((n,)),
        ],
        60,
        cost(0, 0),
        {n_in: len(outs)} if extra else {},
    )


def add_low(a, b):
    return (a.astype(f32) + b.astype(f32)).astype(bf16)


class Share:
    def __init__(self, net, line, z, sent, kept):
        self.net, self.line, self.z = net, line, z
        self.kept, self.got = kept, net.flip(line.after(sent), 1)

    def first(self):
        got = self.line.after(self.got)
        half = [(self.kept[2 * c : 2 * c + 2], got[2 * c : 2 * c + 2]) for c in range(2)]
        self.got = [
            self.net.flip(add_low(kept[:, 2:], got[:, 2:]), COLOURS[c][0])
            for c, (kept, got) in enumerate(half)
        ]
        self.kept = [add_low(kept[:, :2], got[:, :2]) for kept, got in half]

    def second(self):
        got = [self.line.after(one) for one in self.got]
        self.got = [
            self.net.flip(add_low(self.kept[c][:, 1], got[c][:, 1]), COLOURS[c][1])
            for c in range(2)
        ]
        self.kept = [add_low(self.kept[c][:, 0], got[c][:, 0]) for c in range(2)]

    def far(self):
        n = self.net.n_t
        total = [add_low(self.kept[c], self.line.after(self.got[c])) for c in range(2)]
        total = jnp.concatenate(total, axis=0)
        parts = [
            lax.dynamic_index_in_dim(total, lax.rem(self.z - k + n, n), 0, keepdims=False)
            for k in range(n)
        ]
        self.parts = [parts[0]] + [self.net.shift(parts[k], -k) for k in range(1, n)]

    def far_back(self):
        total = self.parts[0].astype(f32)
        for part in self.parts[1:]:
            total = total + self.line.after(part).astype(f32)
        total = total.astype(bf16)
        self.slices = [total] + [self.net.shift(total, k) for k in range(1, self.net.n_t)]

    def gather(self):
        self.gathered = Gather2(self.net, self.line, self.slices)


def spread_kernel(layer, copies, smem, ins, raw, outs, raw_outs, scratch):
    (at_ref,) = smem
    held = ins
    (small_ref,) = outs
    qkv_out, wo_out = raw_outs
    qkv_buf, wo_buf, sems = scratch
    d, z = at_ref[0], at_ref[1]
    rows, cols = held[0].shape[2:]
    rows = rows - FEW
    copies.wait()
    for k in range(4):
        block = lax.rem(z - k + 4, 4)
        for c in range(2):
            for i, j in enumerate(order_of(k // 2)):
                ref = held[2 * (k // 2) + c].at[i, k % 2]
                value = ref[pl.ds(0, rows)].astype(f32)
                slot = jnp.bitwise_xor(d, j ^ c)
                row = pl.multiple_of(slot * rows, rows)

                @pl.when(block < 3)
                def _(value=value, row=row, block=block):
                    col = pl.multiple_of(block * cols, cols)
                    qkv_buf[pl.ds(row, rows), pl.ds(col, cols)] = value

                @pl.when(block == 3)
                def _(value=value, row=row):
                    wo_buf[pl.ds(row, rows), :] = value

                @pl.when(slot == 0)
                def _(ref=ref, block=block):
                    small_ref[block] = ref[pl.ds(rows, FEW)].astype(f32)

    one = pltpu.make_async_copy(qkv_buf, qkv_out.at[layer], sems.at[0])
    two = pltpu.make_async_copy(wo_buf, wo_out.at[layer], sems.at[1])
    one.start()
    two.start()
    one.wait()
    two.wait()


def spread_out(layer, where, pieces, before):
    rows, cols = pieces[0].shape[2:]
    width = 8 * (rows - FEW)
    return staged(
        functools.partial(spread_kernel, layer),
        "spread_out",
        [where],
        pieces,
        [] if before is None else list(before),
        [shape((4, FEW, cols), f32)],
        [shape((LAYERS, width, 3 * cols), f32), shape((LAYERS, width, cols), f32)],
        [
            pltpu.VMEM((width, 3 * cols), f32),
            pltpu.VMEM((width, cols), f32),
            pltpu.SemaphoreType.DMA((2,)),
        ],
        24,
        cost(0, 0),
        {} if before is None else {5: 1, 6: 2},
    )


def quick_program(
    net,
    x_in,
    bucket,
    lengths,
    qkv_weight,
    out_weight,
    norm_gain1,
    norm_bias1,
    up_weight,
    down_weight,
    norm_gain2,
    norm_bias2,
    cotangent,
):
    rows, width = x_in.shape
    d, z = lax.axis_index("dp").astype(jnp.int32), lax.axis_index("tensor").astype(jnp.int32)
    d_at, dz_at = jnp.reshape(d, (1,)), jnp.stack([d, z])
    part = width // net.n_dp
    net.flying = []
    line = Line(net)
    gains1, biases1 = norm_gain1[:, None], norm_bias1[:, None]
    gains2, biases2 = norm_gain2[:, None], norm_bias2[:, None]

    def own_slice(l):
        up = lax.dynamic_slice(up_weight, (l, d * part, 0, 0), (1, part, 2, width))
        down = lax.dynamic_slice(down_weight, (l, d * part, 0), (1, part, width))
        return jnp.concatenate([up.reshape(part, 2 * width), down[0]], axis=1)

    def own_weights(l):
        return [up_weight[l].reshape(width, 2 * width), down_weight[l]]

    seg = segments(bucket[0], lengths[0], rows, SHORT)
    same = seg[:, None] == seg[None, :]
    place = jnp.arange(rows, dtype=f32)
    dist = jnp.where(same, jnp.abs(place[:, None] - place[None, :]), 1e34)
    slopes = slopes_of()
    outputs, kept = [], []

    def run_attn(l, x):
        def call(x):
            return attn_fwd(l, x, qkv_weight, out_weight, gains1[l], biases1[l], dist, slopes)

        return line.run(call, x)

    def run_ff(groups, hb, acc, weights, norm=None):
        return line.run(lambda hb: ff_fwd(groups, d_at, hb, acc, weights, norm), hb)

    OWN, PAIR, TWO, ALL = "own", "pair", "two", "all"
    own = own_slice(0)
    far = {k: net.shift(own, k) for k in (1, 3)}
    x_t = x_in.T
    qkv, lse, ctx, ctx_t, pre1, hb, hb_t = run_attn(0, x_in)
    planes = lax.all_gather(line.after(own_slice(1)), "tensor")
    near = Gather2(net, line, [far[1], far[3]])
    far[2] = net.shift(line.after(own), 2)
    mine = own_weights(0)
    acc = run_ff(((OWN, 0),), hb, (pre1, gains1[0], biases1[0]), mine)[0]
    near.second()
    back = Gather(net, line, [far[2]])
    line.sync()
    near.core()
    line.need(planes)
    planes = line.after(planes)
    others = jnp.stack(
        [
            lax.dynamic_index_in_dim(planes, lax.rem(z - k + net.n_t, net.n_t), 0, keepdims=False)
            for k in range(1, net.n_t)
        ]
    )
    others = lax.all_gather(others, "dp")
    back.core()
    line.sync()
    pre2, out, out_t = run_ff(
        ((TWO, (0, 0)), (TWO, (1, 0)), (PAIR, 0)),
        hb,
        acc,
        near.pieces() + back.pieces(),
        (gains2[0], biases2[0]),
    )
    kept.append((x_t, qkv, lse, ctx_t, pre1, hb, hb_t, pre2))
    outputs.append(out)
    weights = [
        [
            (((OWN, 0), (PAIR, 0)), mine + back.pieces()),
            (((TWO, (0, 0)), (TWO, (1, 0))), near.pieces()),
        ]
    ]
    qkv, lse, ctx, ctx_t, pre1, hb, hb_t = run_attn(1, out)
    mine = own_weights(1)
    acc = run_ff(((OWN, 0),), hb, (pre1, gains1[1], biases1[1]), mine)[0]
    pre2, out, _ = run_ff(
        ((ALL, 0), (ALL, 1), (ALL, 2)), hb, acc, [others], (gains2[1], biases2[1])
    )
    weights.append([(((OWN, 0), (ALL, 1), (ALL, 0), (ALL, 2)), mine + [others])])
    kept.append((out_t, qkv, lse, ctx_t, pre1, hb, hb_t, pre2))
    outputs.append(out)

    order = (0, 2, 1, 3)

    def run_ff_bwd(l, at, ins, **how):
        groups, arrays = weights[l][at]
        hb, hb_t = kept[l][5:7]
        return line.run(lambda hb: ff_bwd(groups, 2 * at, d_at, hb, hb_t, ins, arrays, **how), hb)

    def run_attn_bwd(l, dab, d_pre, small):
        x_t, qkv, lse, ctx_t = kept[l][:4]
        return line.run(
            lambda dab: attn_bwd(
                l,
                d_at,
                dab,
                qkv,
                lse,
                out_weight,
                dist,
                slopes,
                d_pre,
                x_t,
                ctx_t,
                qkv_weight,
                small,
            ),
            dab,
        )

    def over_dp(grads):
        return lax.psum_scatter(line.after(grads), "dp", scatter_dimension=0, tiled=True)[0]

    def to_owner(l, i):
        return net.shift(line.after(ff[l][i]), -order[i])

    pre1, pre2 = kept[1][4], kept[1][7]
    d_pre1, _, _, small2, dab, small1, g = run_ff_bwd(
        1, 0, (cotangent, pre2, gains2[1], pre1, gains1[1]), first=True, last=True
    )
    ff = {1: over_dp(g)}
    sent, keep, grad = run_attn_bwd(1, dab, d_pre1, (small1, small2))
    pre1, pre2 = kept[0][4], kept[0][7]
    share = Share(net, line, z, sent, keep)
    d_h, dyb, dyb_t, small2, g = run_ff_bwd(0, 0, (grad, pre2, gains2[0]), first=True)
    share.first()
    d_pre1, dab, small1, g = run_ff_bwd(
        0, 1, (dyb, dyb_t, d_h, pre1, gains1[0]), into=g, last=True
    )
    ff[0] = over_dp(g)
    share.second()
    sent, keep, grad = run_attn_bwd(0, dab, d_pre1, (small1, small2))
    last_share = Share(net, line, z, sent, keep)
    line.sync()
    last_share.first()
    share.far()
    line.sync()
    last_share.second()
    share.far_back()
    line.sync()
    last_share.far()
    share.gather()
    line.sync()
    last_share.far_back()
    share.gathered.second()
    line.sync()
    line.need(ff[1])
    last_share.gather()
    share.gathered.core()
    ff_parts = {1: [ff[1][0], to_owner(1, 1)]}
    line.sync()
    last_share.gathered.second()
    ff_parts[1] += [to_owner(1, 2), to_owner(1, 3)]
    found = line.run(
        lambda first: spread_out(1, dz_at, [first] + share.gathered.pieces()[1:], None),
        share.gathered.pieces()[0],
    )
    last_share.gathered.core()
    line.need(ff[0])
    ff_parts[0] = [ff[0][0]] + [to_owner(0, i) for i in (1, 2, 3)]
    small = {1: found[0]}
    found = spread_out(0, dz_at, last_share.gathered.pieces(), found[1:])
    small[0] = found[0]
    attention_grads = found[1:]
    small = jnp.stack([small[l][:, 0] for l in range(LAYERS)])
    up_grads, down_grads = [], []
    for l in range(LAYERS):
        total = ff_parts[l][0].astype(f32)
        for one in ff_parts[l][1:]:
            total = total + one.astype(f32)
        up_grads.append(total[:, : 2 * width].reshape(part, 2, width))
        down_grads.append(total[:, 2 * width :].T)
    return (
        jnp.stack(outputs),
        grad,
        attention_grads[0],
        attention_grads[1],
        small[:, 0],
        small[:, 1],
        jnp.stack(up_grads),
        jnp.stack(down_grads),
        small[:, 2],
        small[:, 3],
    )


def attention_forward(x_low, wqkv, wo, g1, b1, same, decay):
    rows, width = x_low.shape
    qkv_low = dot(x_low, wqkv).astype(bf16)
    query, keys, values = split_heads(qkv_low, width)
    scores = scores_of(query, keys, same, decay)
    top = jnp.max(scores, axis=-1, keepdims=True)
    log_total = top + jnp.log(jnp.sum(jnp.exp(scores - top), axis=-1, keepdims=True))
    probs_low = jnp.exp(scores - log_total).astype(bf16)
    ctx_low = (
        jnp.einsum("hqk,khe->qhe", probs_low, values, preferred_element_type=f32)
        .reshape(rows, width)
        .astype(bf16)
    )
    pre_first = x_low.astype(f32) + dot(ctx_low, wo)
    normed = layer_norm(pre_first, g1, b1)
    return normed, (qkv_low, log_total, ctx_low, pre_first)


def attention_backward(d_attn_low, qkv_low, log_total, ctx_low, wo, same, decay):
    rows, width = d_attn_low.shape
    d_ctx = dot(d_attn_low, wo.T).astype(bf16).reshape(rows, HEADS, HEAD_DIM)
    query, keys, values = split_heads(qkv_low, width)
    probs = jnp.exp(scores_of(query, keys, same, decay) - log_total)
    probs_low = probs.astype(bf16)
    d_values = jnp.einsum("hqk,qhe->khe", probs_low, d_ctx, preferred_element_type=f32)
    d_probs = jnp.einsum("qhe,khe->hqk", d_ctx, values, preferred_element_type=f32)
    d_scores = (probs * (d_probs - jnp.sum(probs * d_probs, axis=-1, keepdims=True))).astype(bf16)
    d_query = jnp.einsum("hqk,khe->qhe", d_scores, keys, preferred_element_type=f32)
    d_keys = jnp.einsum("hqk,qhe->khe", d_scores, query, preferred_element_type=f32)
    scale = HEAD_DIM ** (-0.5)
    return jnp.concatenate(
        [
            (d_query * scale).reshape(rows, width),
            (d_keys * scale).reshape(rows, width),
            d_values.reshape(rows, width),
        ],
        axis=1,
    ).astype(bf16)


def plain_program(
    net,
    x_in,
    bucket,
    lengths,
    qkv_weight,
    out_weight,
    norm_gain1,
    norm_bias1,
    up_weight,
    down_weight,
    norm_gain2,
    norm_bias2,
    cotangent,
):
    rows, width = x_in.shape
    n_t = net.n_t
    hidden = down_weight.shape[1]
    seg = segments(bucket[0], lengths[0], rows, SHORT)
    same = seg[:, None] == seg[None, :]
    decay = alibi(rows, HEADS)
    ups = lax.all_gather(up_weight, "tensor", axis=0)
    downs = lax.all_gather(down_weight, "tensor", axis=0)
    groups = [
        [(ups[k, l].reshape(width, -1), downs[k, l]) for k in range(n_t)] for l in range(LAYERS)
    ]
    layer_in = x_in
    outputs, kept = [], []
    for l in range(LAYERS):
        x_low = layer_in
        normed, keep = attention_forward(
            x_low, qkv_weight[l], out_weight[l], norm_gain1[l], norm_bias1[l], same, decay
        )
        hb = normed.astype(bf16)
        pre_second = normed
        joined, act = [], []
        for up, down in groups[l]:
            joined.append(dot(hb, up))
            act.append(geglu(joined[-1]).astype(bf16))
            pre_second = pre_second + dot(act[-1], down)
        layer_in = layer_norm(pre_second, norm_gain2[l], norm_bias2[l]).astype(bf16)
        outputs.append(layer_in)
        kept.append((x_low, *keep, hb, pre_second, joined, act))
    grad = cotangent.astype(f32)
    attention_grads, small, up_grads, down_grads = ([None] * LAYERS for _ in range(4))
    for l in reversed(range(LAYERS)):
        x_low, qkv_low, log_total, ctx_low, pre_first, hb, pre_second, joined, act = kept[l]
        pull = jax.vjp(layer_norm, pre_second, norm_gain2[l], norm_bias2[l])[1]
        d_pre2, d_gain2, d_bias2 = pull(grad)
        dyb = d_pre2.astype(bf16)
        d_h = d_pre2
        d_joined = []
        for k, (up, down) in enumerate(groups[l]):
            d_act = dot(dyb, down.T)
            d_joined.append(jax.vjp(geglu, joined[k])[1](d_act)[0].astype(bf16))
            d_h = d_h + dot(d_joined[k], up.T)
        d_up = jnp.stack([dot(hb.T, one) for one in d_joined]).astype(bf16)
        d_down = jnp.stack([dot(dyb.T, one) for one in act]).astype(bf16)
        d_up = lax.psum_scatter(d_up, "tensor", scatter_dimension=0)
        d_down = lax.psum_scatter(d_down, "tensor", scatter_dimension=0)
        d_up = lax.psum_scatter(d_up, "dp", scatter_dimension=0, tiled=True)
        d_down = lax.psum_scatter(d_down, "dp", scatter_dimension=0, tiled=True)
        up_grads[l], down_grads[l] = d_up.astype(f32), d_down.astype(f32)
        pull = jax.vjp(layer_norm, pre_first, norm_gain1[l], norm_bias1[l])[1]
        d_pre1, d_gain1, d_bias1 = pull(d_h)
        small[l] = [d_gain1, d_bias1, d_gain2, d_bias2]
        dab = d_pre1.astype(bf16)
        d_qkv = attention_backward(dab, qkv_low, log_total, ctx_low, out_weight[l], same, decay)
        found = lax.psum(
            (dot(x_low.T, d_qkv).astype(bf16), dot(ctx_low.T, dab).astype(bf16)), BOTH
        )
        attention_grads[l] = [one.astype(f32) for one in found]
        grad = d_pre1 + dot(d_qkv, qkv_weight[l].T)
    small = lax.psum(jnp.stack(small[0] + small[1]), BOTH).reshape(LAYERS, 4, width)
    return (
        jnp.stack(outputs),
        grad,
        jnp.stack([one[0] for one in attention_grads]),
        jnp.stack([one[1] for one in attention_grads]),
        small[:, 0],
        small[:, 1],
        jnp.stack(up_grads).reshape(LAYERS, -1, 2, hidden),
        jnp.stack([one.T for one in down_grads]),
        small[:, 2],
        small[:, 3],
    )


def program(net, *args):
    width, hidden = args[0].shape[1], args[8].shape[1]
    quick = net.n_dp == 8 and net.n_t == 4 and hidden == width and width % 256 == 0
    return (quick_program if quick else plain_program)(net, *args)


def solution(mesh):
    in_specs = (
        P(BOTH, None),
        P(BOTH),
        P(BOTH, None),
        P(),
        P(),
        P(),
        P(),
        P(None, None, None, "tensor"),
        P(None, "tensor", None),
        P(),
        P(),
        P(BOTH, None),
    )
    out_specs = (
        P(None, BOTH, None),
        P(BOTH, None),
        P(),
        P(),
        P(),
        P(),
        P(None, "dp", None, "tensor"),
        P(None, "tensor", "dp"),
        P(),
        P(),
    )
    net = Net(mesh)
    return jax.shard_map(
        functools.partial(program, net),
        mesh=mesh,
        in_specs=in_specs,
        out_specs=out_specs,
        check_vma=False,
    )
```

```python
import functools

import jax
import jax.numpy as jnp
from jax import lax
from jax.experimental import pallas as pl
from jax.experimental.pallas import tpu as pltpu
from jax.sharding import PartitionSpec as P

HEADS = 12
HEAD_DIM = 64
SHORT = 128
LAYERS = 2

eps_norm = 1e-05
gelu_coef = 0.7978845608028654
masked_score = -1e30
bf16 = jnp.bfloat16
f32 = jnp.float32
BOTH = ("dp", "tensor")


def segments(bucket_one, lens, rows_dev, short_len):
    rows = jnp.arange(rows_dev, dtype=jnp.int32)
    slot = rows // short_len
    offset = rows - slot * short_len
    slots_all = jnp.arange(lens.shape[0], dtype=jnp.int32)
    slot_len = jnp.sum(jnp.where(slot[:, None] == slots_all[None, :], lens[None, :], 0), axis=1)
    total = jnp.sum(lens)
    is_long = bucket_one == 1
    real = jnp.where(is_long, rows < total, offset < slot_len)
    group = jnp.where(is_long, 0, slot)
    return jnp.where(real, group, lens.shape[0] + rows)


def alibi(rows_dev, heads):
    slopes = jnp.exp2(-8.0 * (jnp.arange(heads, dtype=f32) + 1.0) / heads)
    place = jnp.arange(rows_dev, dtype=f32)
    dist = jnp.abs(place[:, None] - place[None, :])
    return slopes[:, None, None] * dist[None, :, :]


def layer_norm(value, gain, bias):
    mean = jnp.mean(value, axis=-1, keepdims=True)
    centered = value - mean
    var = jnp.mean(centered * centered, axis=-1, keepdims=True)
    return centered * lax.rsqrt(var + eps_norm) * gain + bias


def geglu(joined):
    half = joined.shape[1] // 2
    gate = joined[:, :half]
    value = joined[:, half:]
    return 0.5 * gate * (1.0 + jnp.tanh(gelu_coef * (gate + 0.044715 * gate * gate * gate))) * value


def split_heads(qkv_low, width):
    rows = qkv_low.shape[0]
    query = qkv_low[:, :width].reshape(rows, HEADS, HEAD_DIM)
    keys = qkv_low[:, width : 2 * width].reshape(rows, HEADS, HEAD_DIM)
    values = qkv_low[:, 2 * width :].reshape(rows, HEADS, HEAD_DIM)
    return (query, keys, values)


def scores_of(query, keys, same, decay):
    raw = (
        jnp.einsum("qhe,khe->hqk", query, keys, preferred_element_type=f32) * HEAD_DIM ** (-0.5)
        - decay
    )
    return jnp.where(same[None, :, :], raw, masked_score)


def dot(a, b):
    return jnp.dot(a, b, preferred_element_type=f32)


class Net:
    def __init__(self, mesh):
        self.n_dp = mesh.shape["dp"]
        self.n_t = mesh.shape["tensor"]
        self.flying = []

    def flip(self, value, bit, wait=True):
        got = lax.ppermute(value, "dp", [(i, i ^ bit) for i in range(self.n_dp)])
        if wait:
            self.flying.append(got)
        return got

    def shift(self, value, step):
        n = self.n_t
        got = lax.ppermute(value, "tensor", [(i, (i + step) % n) for i in range(n)])
        self.flying.append(got)
        return got


CHIPS = (0, 2, 4, 6)
COLOURS = ((2, 4), (4, 2))


def order_of(colour):
    one, two = COLOURS[colour]
    return [0, one, two, one ^ two]


def fold_order(colour):
    one, two = COLOURS[colour]
    return [0, two, one, one ^ two]


class Line:
    def __init__(self, net):
        self.net = net
        self.last = []

    def after(self, value):
        if not self.last:
            return value
        return lax.optimization_barrier((value, *self.last))[0]

    def sync(self):
        self.need(*self.net.flying)
        self.net.flying = []

    def need(self, *values):
        self.last = self.last + list(values)

    def run(self, call, first, *rest):
        out = call(self.after(first), *rest)
        self.last = [out[0] if isinstance(out, (tuple, list)) else out]
        self.sync()
        return out


class Gather:
    def __init__(self, net, line, slices):
        self.net, self.line = net, line
        n = len(slices) // 2
        self.held = [
            jnp.stack([line.after(one) for one in slices[c * n : (c + 1) * n]])[None]
            for c in range(2)
        ]
        self.got = [net.flip(self.held[c], COLOURS[c][0]) for c in range(2)]

    def join(self):
        self.held = [
            jnp.concatenate([self.held[c], self.line.after(self.got[c])], axis=0) for c in range(2)
        ]

    def second(self):
        self.join()
        self.got = [self.net.flip(self.held[c], COLOURS[c][1]) for c in range(2)]

    def core(self):
        self.join()
        self.held = jnp.concatenate(self.held, axis=0)
        self.got = self.net.flip(self.held, 1)

    def pieces(self):
        return [self.held, self.got]


VMEM_SPEC = pl.BlockSpec(memory_space=pltpu.VMEM)
ANY_SPEC = pl.BlockSpec(memory_space=pl.ANY)
SMEM_SPEC = pl.BlockSpec(memory_space=pltpu.SMEM)
NN = (((1,), (0,)), ((), ()))
NT = (((1,), (1,)), ((), ()))
TN = (((0,), (0,)), ((), ()))


def mm(a, b, dims=NN):
    return lax.dot_general(a, b, dims, preferred_element_type=f32)


def params(mib):
    return pltpu.CompilerParams(vmem_limit_bytes=60 << 20)


def cost(flops, nbytes):
    return pl.CostEstimate(flops=1024, transcendentals=0, bytes_accessed=1024)


def shape(dims, kind):
    return jax.ShapeDtypeStruct(dims, kind)


HBM_SPEC = pl.BlockSpec(memory_space=pltpu.MemorySpace.HBM)


class Copies:
    def __init__(self, ins, outs, sems):
        self.ins = [pltpu.make_async_copy(src, dst, sems.at[i]) for i, (src, dst) in enumerate(ins)]
        n = len(ins)
        self.outs = [
            pltpu.make_async_copy(src, dst, sems.at[n + i]) for i, (src, dst) in enumerate(outs)
        ]
        self.waited, self.put_out = set(), set()
        for copy in self.ins:
            copy.start()

    def wait(self, *which):
        for i in which or range(len(self.ins)):
            if i not in self.waited:
                self.waited.add(i)
                self.ins[i].wait()

    def put(self, *which):
        for i in which or range(len(self.outs)):
            if i not in self.put_out:
                self.put_out.add(i)
                self.outs[i].start()

    def finish(self):
        self.put()
        for copy in self.outs:
            copy.wait()


def staged_kernel(body, layers, n_smem, n_raw, n_out, n_raw_out, *refs):
    n_in = len(layers)
    smem, refs = refs[:n_smem], refs[n_smem:]
    ins, refs = refs[:n_in], refs[n_in:]
    raw, refs = refs[:n_raw], refs[n_raw:]
    outs, refs = refs[:n_out], refs[n_out:]
    raw_outs, refs = refs[:n_raw_out], refs[n_raw_out:]
    held, refs = refs[:n_in], refs[n_in:]
    made, refs = refs[:n_out], refs[n_out:]
    sems, scratch = refs[0], refs[1:]
    copies = Copies(
        [
            (ref if layer is None else ref.at[layer], to)
            for ref, layer, to in zip(ins, layers, held)
        ],
        list(zip(made, outs)),
        sems,
    )
    body(copies, smem, held, raw, made, raw_outs, scratch)
    copies.finish()


def staged(body, name, smem, ins, raw, outs, raw_outs, scratch, mib, work, aliases=None):
    pairs = [one if isinstance(one, tuple) else (one, None) for one in ins]
    layers = [layer for _, layer in pairs]
    held = [
        pltpu.VMEM(one.shape if layer is None else one.shape[1:], one.dtype) for one, layer in pairs
    ]
    made = [pltpu.VMEM(one.shape, one.dtype) for one in outs]
    n_copies = len(pairs) + len(outs)
    found = pl.pallas_call(
        functools.partial(
            staged_kernel, body, layers, len(smem), len(raw), len(outs), len(raw_outs)
        ),
        name=name,
        out_shape=tuple(outs) + tuple(raw_outs),
        in_specs=[SMEM_SPEC] * len(smem) + [HBM_SPEC] * (len(pairs) + len(raw)),
        out_specs=(HBM_SPEC,) * (len(outs) + len(raw_outs)),
        scratch_shapes=held + made + [pltpu.SemaphoreType.DMA((n_copies,))] + scratch,
        input_output_aliases=aliases or {},
        compiler_params=params(mib),
        cost_estimate=work,
    )(*smem, *[one for one, _ in pairs], *raw)
    return found


def normed_of(value):
    mean = jnp.mean(value, axis=-1, keepdims=True)
    centered = value - mean
    var = jnp.mean(centered * centered, axis=-1, keepdims=True)
    rstd = lax.rsqrt(var + eps_norm)
    return centered * rstd, rstd


def norm_back(grad, xhat, rstd, gain):
    scaled = grad * gain
    first = jnp.mean(scaled, axis=-1, keepdims=True)
    second = jnp.mean(scaled * xhat, axis=-1, keepdims=True)
    return rstd * (scaled - first - xhat * second)


def attn_fwd_kernel(copies, smem, ins, raw, outs, raw_outs, scratch):
    (slopes,) = smem
    x_ref, wqkv_ref, dist_ref, wo_ref, g_ref, b_ref = ins
    qkv_ref, lse_ref, ctx_ref, ctx_t_ref, pre_ref, hb_ref, hb_t_ref = outs
    rows, width = x_ref.shape
    copies.wait(0, 1)
    x = x_ref[...]
    for c in range(3):
        cols = pl.ds(c * width, width)
        qkv_ref[:, cols] = mm(x, wqkv_ref[:, cols]).astype(bf16)
    copies.put(0)
    copies.wait()
    lse_ref[...] = jnp.zeros_like(lse_ref)
    s_ref, p_ref = scratch

    def pair(p, _):
        def at(c):
            return pl.ds(pl.multiple_of(c * width + p * 128, 128), 128)

        key, val = qkv_ref[:, at(1)], qkv_ref[:, at(2)]
        query = qkv_ref[:, at(0)] * bf16(HEAD_DIM ** (-0.5))
        wide = lax.broadcasted_iota(jnp.int32, (rows, 128), 1)
        for side in range(2):
            mine = (wide < HEAD_DIM) == (side == 0)
            s_ref[side] = mm(jnp.where(mine, query, bf16(0)), key, NT)

        dist = dist_ref[...]
        total_lse = lse_ref[...]
        for side in range(2):
            s = s_ref[side] - slopes[2 * p + side] * dist
            top = jnp.max(s, axis=-1, keepdims=True)
            e = jnp.exp(s - top)
            total = jnp.sum(e, axis=-1, keepdims=True)
            p_ref[side] = (e * (1.0 / total)).astype(bf16)
            total_lse += jnp.where(wide == 2 * p + side, top + jnp.log(total), 0.0)
        lse_ref[...] = total_lse
        found = [mm(p_ref[side], val) for side in range(2)]
        ctx_ref[:, at(0)] = jnp.where(wide < HEAD_DIM, found[0], found[1]).astype(bf16)
        return 0

    lax.fori_loop(0, width // 128, pair, 0)
    copies.put(1, 2)
    ctx = ctx_ref[...]
    pre = x.astype(f32) + mm(ctx, wo_ref[...])
    pre_ref[...] = pre
    ctx_t_ref[...] = ctx.T
    copies.put(3, 4)
    xhat, _ = normed_of(pre)
    hb = (xhat * g_ref[...] + b_ref[...]).astype(bf16)
    hb_ref[...] = hb
    hb_t_ref[...] = hb.T


def slopes_of():
    steps = jnp.arange(HEADS, dtype=f32)
    return jnp.exp2(-8.0 * (steps + 1.0) / HEADS)


def attn_fwd(layer, x, wqkv, wo, gain, bias, dist, slopes):
    rows, width = x.shape
    return staged(
        attn_fwd_kernel,
        "attn_fwd",
        [slopes],
        [x, (wqkv, layer), dist, (wo, layer), gain, bias],
        [],
        [
            shape((rows, 3 * width), bf16),
            shape((rows, 128), f32),
            shape((rows, width), bf16),
            shape((width, rows), bf16),
            shape((rows, width), f32),
            shape((rows, width), bf16),
            shape((width, rows), bf16),
        ],
        [],
        [pltpu.VMEM((2, rows, rows), f32), pltpu.VMEM((2, rows, rows), bf16)],
        36,
        cost(0, 0),
    )


def attn_bwd_kernel(copies, smem, ins, raw, outs, raw_outs, scratch):
    slopes, at_ref = smem
    dab_ref, wo_ref, qkv_ref, lse_ref, dist_ref, x_t_ref, c_t_ref, wqkv_ref, dpre_ref = ins[:9]
    small_refs = ins[9:]
    dctx_ref, s_ref, dp_ref, p_ref, ds_ref, out_ref, rows_ref = scratch
    sent_ref, kept_ref, grad_ref = outs
    rows, width = dab_ref.shape
    scale = HEAD_DIM ** (-0.5)
    copies.wait(0, 1)
    dctx_ref[...] = mm(dab_ref[...], wo_ref[...], NT).astype(bf16)
    copies.wait(2, 3, 4)
    def pair(p, _):
        def at(c):
            return pl.ds(pl.multiple_of(c * width + p * 128, 128), 128)

        key, val, query = qkv_ref[:, at(1)], qkv_ref[:, at(2)], qkv_ref[:, at(0)]
        dctx = dctx_ref[:, at(0)]
        wide = lax.broadcasted_iota(jnp.int32, (rows, 128), 1)
        low = wide < HEAD_DIM
        for side in range(2):
            mine = low == (side == 0)
            s_ref[side] = mm(jnp.where(mine, query * bf16(scale), bf16(0)), key, NT)
            dp_ref[side] = mm(jnp.where(mine, dctx, bf16(0)), val, NT)

        dist = dist_ref[...]
        for side in range(2):
            lse = jnp.sum(jnp.where(wide == 2 * p + side, lse_ref[...], 0.0), axis=-1, keepdims=True)
            prob = jnp.exp(s_ref[side] - slopes[2 * p + side] * dist - lse)
            d_prob = dp_ref[side]
            mean = jnp.sum(prob * d_prob, axis=-1, keepdims=True)
            p_ref[side] = prob.astype(bf16)
            ds_ref[side] = (prob * (d_prob - mean)).astype(bf16)
        d_q = [mm(ds_ref[side], key) for side in range(2)]
        query_t, dctx_t = query.T, dctx.T
        d_k = [mm(query_t, ds_ref[side]).T for side in range(2)]
        d_v = [mm(dctx_t, p_ref[side]).T for side in range(2)]
        out_ref[:, at(0)] = (jnp.where(low, d_q[0], d_q[1]) * scale).astype(bf16)
        out_ref[:, at(1)] = (jnp.where(low, d_k[0], d_k[1]) * scale).astype(bf16)
        out_ref[:, at(2)] = jnp.where(low, d_v[0], d_v[1]).astype(bf16)
        return 0

    lax.fori_loop(0, width // 128, pair, 0)
    part = width // 8
    copies.wait()
    for colour in range(2):
        order = fold_order(colour)
        order = order + [j ^ 1 for j in order]
        pick_rows(at_ref[0], order, x_t_ref, rows_ref)
        for block in (2 * colour, 2 * colour + 1):
            if block < 3:
                rhs = out_ref[:, pl.ds(block * width, width)]
            else:
                rhs = dab_ref[...]
                pick_rows(at_ref[0], order, c_t_ref, rows_ref)
            total = mm(rows_ref[...], rhs).astype(bf16)
            few = small_refs[block // 2][block % 2 : block % 2 + 1]
            for i, j in enumerate(order):
                to = (kept_ref, sent_ref)[i // 4].at[block, i % 4]
                to[pl.ds(0, part)] = total[i * part : (i + 1) * part]
                here = jnp.where(jnp.bitwise_xor(at_ref[0], j) == 0, few, 0.0)
                to[pl.ds(part, FEW)] = jnp.broadcast_to(here, (FEW, width)).astype(bf16)
    copies.put(0, 1)
    grad_ref[...] = dpre_ref[...] + mm(out_ref[...], wqkv_ref[...], NT)


FEW = 8


def attn_bwd(layer, d, dab, qkv, lse, wo, dist, slopes, d_pre, x_t, ctx_t, wqkv, small):
    rows, width = dab.shape
    part = shape((4, 4, width // 8 + FEW, width), bf16)
    return staged(
        attn_bwd_kernel,
        "attn_bwd",
        [slopes, d],
        [dab, (wo, layer), qkv, lse, dist, x_t, ctx_t, (wqkv, layer), d_pre, *small],
        [],
        [part, part, shape((rows, width), f32)],
        [],
        [
            pltpu.VMEM((rows, width), bf16),
            pltpu.VMEM((2, rows, rows), f32),
            pltpu.VMEM((2, rows, rows), f32),
            pltpu.VMEM((2, rows, rows), bf16),
            pltpu.VMEM((2, rows, rows), bf16),
            pltpu.VMEM((rows, 3 * width), bf16),
            pltpu.VMEM((width, rows), bf16),
        ],
        40,
        cost(0, 0),
    )


def load_groups(groups, d, refs, w_ref, sems, slots):
    loads = []
    at = 0
    sources = {}
    for g, (kind, index) in enumerate(groups):
        mine = []
        s = g % slots
        if kind not in sources:
            count = 1 if kind == "all" else 2
            sources[kind] = refs[at : at + count]
            at += count
        source = sources[kind]
        part = source[0].shape[2] if kind != "own" else 0
        if kind == "own":
            split = source[0].shape[1]
            rest = source[1].shape[1]
            pairs = [
                (source[0], w_ref.at[s, :, pl.ds(0, split)]),
                (source[1], w_ref.at[s, :, pl.ds(split, rest)]),
            ]
        elif kind == "all":
            pairs = [(source[0].at[j, index], w_ref.at[s, pl.ds(j * part, part)]) for j in range(8)]
        else:
            pairs = []
            for colour in (index,) if kind == "two" else (0, 1):
                for c in range(2):
                    for i, j in enumerate(order_of(colour)):
                        slot = jnp.bitwise_xor(d, j ^ c)
                        if kind == "two":
                            row = slot * part
                        else:
                            row = slot * (2 * part) + colour * part
                        row = pl.multiple_of(row, part)
                        one = source[c].at[4 * colour + i, 0]
                        pairs.append((one, w_ref.at[s, pl.ds(row, part)]))
        for i, (one, to) in enumerate(pairs):
            mine.append(pltpu.make_async_copy(one, to, sems.at[g, i]))
        loads.append(mine)
    return loads


def gelu_parts(gate):
    square = gate * gate
    t = jnp.tanh(gelu_coef * gate * (1.0 + 0.044715 * square))
    half = 0.5 * (1.0 + t)
    slope = half + 0.5 * gate * (1.0 - t * t) * gelu_coef * (1.0 + 3 * 0.044715 * square)
    return gate * half, slope


TILE = 768


def ff_fwd_kernel(groups, first, last, copies, smem, ins, raw, outs, raw_outs, scratch):
    (at_ref,) = smem
    hb_ref, acc_refs, norm_refs = ins[0], ins[1 : 4 if first else 2], ins[4 if first else 2 :]
    pre_ref = outs[0]
    w_ref, sems = scratch
    width = hb_ref.shape[1]
    loads = load_groups(groups, at_ref[0], raw, w_ref, sems, len(groups))
    for load in loads:
        for copy in load:
            copy.start()
    copies.wait()
    if first:
        xhat, _ = normed_of(acc_refs[0][...])
        pre_ref[...] = xhat * acc_refs[1][...] + acc_refs[2][...]
    else:
        pre_ref[...] = acc_refs[0][...]
    for s in range(len(groups)):
        for copy in loads[s]:
            copy.wait()

        def step(n, _, s=s):
            def at(c):
                return pl.ds(pl.multiple_of(c * width + n * TILE, TILE), TILE)

            hb = hb_ref[...]
            gate, value = mm(hb, w_ref[s, :, at(0)]), mm(hb, w_ref[s, :, at(1)])
            act = (gelu_parts(gate)[0] * value).astype(bf16)
            pre_ref[...] += mm(act, w_ref[s, at(0), pl.ds(2 * width, width)])
            return 0

        step(0, 0)
    if last:
        copies.put(0)
        xhat, _ = normed_of(pre_ref[...])
        out = (xhat * norm_refs[0][...] + norm_refs[1][...]).astype(bf16)
        outs[1][...] = out
        outs[2][...] = out.T


def ff_fwd(groups, d, hb, acc, weights, norm=None):
    rows, width = hb.shape
    last = norm is not None
    acc = acc if isinstance(acc, tuple) else (acc,)
    outs = [shape((rows, width), f32)]
    if last:
        outs += [shape((rows, width), bf16), shape((width, rows), bf16)]
    n = len(groups)
    return staged(
        functools.partial(ff_fwd_kernel, groups, len(acc) == 3, last),
        "ff_fwd",
        [d],
        [hb, *acc, *(norm if last else ())],
        weights,
        outs,
        [],
        [
            pltpu.VMEM((n, width, 3 * width), bf16),
            pltpu.SemaphoreType.DMA((n, 16)),
        ],
        36,
        cost(0, 0),
    )


def pick_rows(d, order, from_ref, to_ref):
    rows = from_ref.shape[0] // 8
    for i, j in enumerate(order):
        at = pl.multiple_of(jnp.bitwise_xor(d, j) * rows, rows)
        to_ref[pl.ds(i * rows, rows), :] = from_ref[pl.ds(at, rows), :]


def norm_bwd(grad, pre, gain_ref, small_ref):
    xhat, rstd = normed_of(pre)
    small_ref[0:1] = jnp.sum(grad * xhat, axis=0, keepdims=True)
    small_ref[1:2] = jnp.sum(grad, axis=0, keepdims=True)
    return norm_back(grad, xhat, rstd, gain_ref[...])


def ff_bwd_kernel(
    groups, first, last, slot, with_grads, copies, smem, ins, raw, outs, raw_outs, scratch
):
    (at_ref,) = smem
    hb_ref, *ins = ins
    w_ref, sems, *scratch = scratch
    if with_grads:
        hb_t_ref, *ins = ins
        g_ref, out_sems = scratch
    width = hb_ref.shape[1]
    part = width // 8
    n = len(groups)
    loads = load_groups(groups, at_ref[0], raw, w_ref, sems, 2)
    for copy in loads[0]:
        copy.start()
    copies.wait()
    dh_ref, *outs = outs
    if first:
        grad_ref, pre_ref, gain_ref, *ins = ins
        dyb_ref, dyb_t_ref, small2_ref, *outs = outs
        d_pre = norm_bwd(grad_ref[...].astype(f32), pre_ref[...], gain_ref, small2_ref)
        dh_ref[...] = d_pre
        dyb_ref[...] = d_pre.astype(bf16)
        dyb_t_ref[...] = dyb_ref[...].T
    else:
        dyb_ref, dyb_t_ref, acc_ref, *ins = ins
        dh_ref[...] = acc_ref[...]
    out = []
    for s in range(n):
        if s + 1 < n:
            for copy in loads[s + 1]:
                copy.start()
        for copy in loads[s]:
            copy.wait()
        weights = w_ref.at[s % 2]

        def at(c):
            return pl.ds(c * width, width)

        hb = hb_ref[...]
        gate, value = mm(hb, weights[:, at(0)]), mm(hb, weights[:, at(1)])
        d_act = mm(dyb_ref[...], weights[:, at(2)], NT)
        gelu, slope = gelu_parts(gate)
        d_gate = (d_act * value * slope).astype(bf16)
        d_value = (d_act * gelu).astype(bf16)
        act = (gelu * value).astype(bf16)
        dh_ref[...] += mm(d_gate, weights[:, at(0)], NT) + mm(d_value, weights[:, at(1)], NT)
        if not with_grads:
            continue
        if s >= 2:
            out[s - 2].wait()
        grads = g_ref.at[s % 2]
        for c, (lhs, rhs) in enumerate(((hb_t_ref, d_gate), (hb_t_ref, d_value), (dyb_t_ref, act))):
            total = mm(lhs[...], rhs).astype(bf16)
            for j in range(8):
                grads[j, :, at(c)] = total[j * part : (j + 1) * part]
        out.append(pltpu.make_async_copy(grads, raw_outs[0].at[:, slot + s], out_sems.at[s]))
        out[s].start()
    if last:
        pre_ref, gain_ref = ins
        dab_ref, small1_ref = outs
        d_pre = norm_bwd(dh_ref[...], pre_ref[...], gain_ref, small1_ref)
        dh_ref[...] = d_pre
        dab_ref[...] = d_pre.astype(bf16)
    for one in out[-2:]:
        one.wait()


def ff_bwd(groups, slot, d, hb, hb_t, ins, weights, first=False, last=False, into=None, grads=True):
    rows, width = hb.shape
    n = len(groups)
    low, few = shape((rows, width), bf16), shape((2, width), f32)
    outs = [shape((rows, width), f32)]
    outs += [low, shape((width, rows), bf16), few] if first else []
    outs += [low, few] if last else []
    extra = [] if into is None else [into]
    n_in = 3 + len(ins) + len(weights)
    scratch = [pltpu.VMEM((2, width, 3 * width), bf16), pltpu.SemaphoreType.DMA((n, 16))]
    if grads:
        scratch += [
            pltpu.VMEM((2, 8, width // 8, 3 * width), bf16),
            pltpu.SemaphoreType.DMA((n,)),
        ]
    return staged(
        functools.partial(ff_bwd_kernel, groups, first, last, slot, grads),
        "ff_bwd",
        [d],
        [hb, *([hb_t] if grads else []), *ins],
        weights + extra,
        outs,
        [shape((8, 4, width // 8, 3 * width), bf16)] if grads else [],
        scratch,
        60,
        cost(0, 0),
        {n_in: len(outs)} if extra else {},
    )


def ff_grads_kernel(n, copies, smem, ins, raw, outs, raw_outs, scratch):
    up_ref, down_ref, *rows_refs = ins
    (total_ref,) = scratch
    (at_ref,) = smem
    sent_ref, kept_ref = outs
    width = up_ref.shape[0]
    part = width // 8
    copies.wait(0, 1)
    for s in range(n):
        copies.wait(2 + 2 * s, 3 + 2 * s)
        hb, dyb = rows_refs[2 * s][...], rows_refs[2 * s + 1][...]
        gate, value = mm(hb, up_ref[:, pl.ds(0, width)]), mm(hb, up_ref[:, pl.ds(width, width)])
        d_act = mm(dyb, down_ref[...], NT)
        gelu, slope = gelu_parts(gate)
        d_gate = (d_act * value * slope).astype(bf16)
        d_value = (d_act * gelu).astype(bf16)
        act = (gelu * value).astype(bf16)
        hb_t, dyb_t = hb.T, dyb.T
        for c, (lhs, rhs) in enumerate(((hb_t, d_gate), (hb_t, d_value), (dyb_t, act))):
            at = pl.ds(c * width, width)
            total = mm(lhs, rhs)
            total_ref[:, at] = total if s == 0 else total + total_ref[:, at]
    order = fold_order(0)
    for to_ref, flip in ((sent_ref, 1), (kept_ref, 0)):
        for i, j in enumerate(order):
            row = pl.multiple_of(jnp.bitwise_xor(at_ref[0], j ^ flip) * part, part)
            to_ref[i] = total_ref[pl.ds(row, part), :].astype(bf16)
        copies.put(flip ^ 1)


def ff_grads(d, up, down, all_hb, all_dyb):
    width = up.shape[0]
    return staged(
        functools.partial(ff_grads_kernel, all_hb.shape[0]),
        "ff_grads",
        [d],
        [up, down, *[(one, s) for s in range(all_hb.shape[0]) for one in (all_hb, all_dyb)]],
        [],
        [shape((4, width // 8, 3 * width), bf16)] * 2,
        [],
        [pltpu.VMEM((width, 3 * width), f32)],
        60,
        cost(0, 0),
    )


def add_low(a, b):
    return (a.astype(f32) + b.astype(f32)).astype(bf16)


class Fold:
    def __init__(self, net, line, sent, kept):
        self.net, self.line = net, line
        self.kept, self.got = kept, net.flip(line.after(sent), 1)

    def step(self, bit):
        got = self.line.after(self.got)
        half = self.kept.shape[0] // 2
        self.got = self.net.flip(add_low(self.kept[half:], got[half:]), bit, wait=False)
        self.kept = add_low(self.kept[:half], got[:half])

    def first(self):
        self.step(COLOURS[0][0])

    def second(self):
        self.step(COLOURS[0][1])

    def done(self):
        return self.kept[0].astype(f32) + self.line.after(self.got)[0].astype(f32)


class Share:
    def __init__(self, net, line, z, sent, kept):
        self.net, self.line, self.z = net, line, z
        self.kept, self.got = kept, net.flip(line.after(sent), 1)

    def first(self):
        got = self.line.after(self.got)
        half = [(self.kept[2 * c : 2 * c + 2], got[2 * c : 2 * c + 2]) for c in range(2)]
        self.got = [
            self.net.flip(add_low(kept[:, 2:], got[:, 2:]), COLOURS[c][0])
            for c, (kept, got) in enumerate(half)
        ]
        self.kept = [add_low(kept[:, :2], got[:, :2]) for kept, got in half]

    def second(self):
        got = [self.line.after(one) for one in self.got]
        self.got = [
            self.net.flip(add_low(self.kept[c][:, 1], got[c][:, 1]), COLOURS[c][1])
            for c in range(2)
        ]
        self.kept = [add_low(self.kept[c][:, 0], got[c][:, 0]) for c in range(2)]

    def far(self):
        n = self.net.n_t
        total = [add_low(self.kept[c], self.line.after(self.got[c])) for c in range(2)]
        total = jnp.concatenate(total, axis=0)
        parts = [
            lax.dynamic_index_in_dim(total, lax.rem(self.z - k + n, n), 0, keepdims=False)
            for k in range(n)
        ]
        self.parts = [parts[0]] + [self.net.shift(parts[k], -k) for k in range(1, n)]

    def far_back(self):
        total = self.parts[0].astype(f32)
        for part in self.parts[1:]:
            total = total + self.line.after(part).astype(f32)
        total = total.astype(bf16)
        self.slices = [total] + [self.net.shift(total, k) for k in range(1, self.net.n_t)]

    def gather(self):
        self.gathered = Gather(self.net, self.line, self.slices)


def spread_kernel(layer, copies, smem, ins, raw, outs, raw_outs, scratch):
    (at_ref,) = smem
    held = ins
    (small_ref,) = outs
    qkv_out, wo_out = raw_outs
    buf, sems = scratch
    d, z = at_ref[0], at_ref[1]
    rows, cols = held[0].shape[2:]
    rows = rows - FEW

    def each(act):
        for c in range(2):
            for k in range(4):
                block = lax.rem(z - k + 4, 4)
                for i, j in enumerate(order_of(k // 2)):
                    act(c, k, i, j, block, 16 * c + 4 * k + i)

    def copy_of(n, slot, block, to_qkv):
        row = pl.ds(pl.multiple_of(slot * rows, rows), rows)
        if to_qkv:
            col = pl.ds(pl.multiple_of(block * cols, cols), cols)
            to = qkv_out.at[layer, row, col]
        else:
            to = wo_out.at[layer, row, :]
        return pltpu.make_async_copy(buf.at[n], to, sems.at[n])

    def begin(c, k, i, j, block, n):
        if k == 0 and i == 0:
            copies.wait(c)
        ref = held[c].at[4 * (k // 2) + i, k % 2]
        slot = jnp.bitwise_xor(d, j ^ c)
        buf[n] = ref[pl.ds(0, rows)].astype(f32)

        @pl.when(block < 3)
        def _():
            copy_of(n, slot, block, True).start()

        @pl.when(block == 3)
        def _():
            copy_of(n, slot, block, False).start()

        @pl.when(slot == 0)
        def _():
            small_ref[block] = ref[pl.ds(rows, FEW)].astype(f32)

    def end(c, k, i, j, block, n):
        slot = jnp.bitwise_xor(d, j ^ c)

        @pl.when(block < 3)
        def _():
            copy_of(n, slot, block, True).wait()

        @pl.when(block == 3)
        def _():
            copy_of(n, slot, block, False).wait()

    each(begin)
    each(end)


def spread_out(layer, where, pieces, before):
    rows, cols = pieces[0].shape[2:]
    width = 8 * (rows - FEW)
    return staged(
        functools.partial(spread_kernel, layer),
        "spread_out",
        [where],
        pieces,
        [] if before is None else list(before),
        [shape((4, FEW, cols), f32)],
        [shape((LAYERS, width, 3 * cols), f32), shape((LAYERS, width, cols), f32)],
        [pltpu.VMEM((32, rows - FEW, cols), f32), pltpu.SemaphoreType.DMA((32,))],
        24,
        cost(0, 0),
        {} if before is None else {3: 1, 4: 2},
    )


def quick_program(
    net,
    x_in,
    bucket,
    lengths,
    qkv_weight,
    out_weight,
    norm_gain1,
    norm_bias1,
    up_weight,
    down_weight,
    norm_gain2,
    norm_bias2,
    cotangent,
):
    rows, width = x_in.shape
    d, z = lax.axis_index("dp").astype(jnp.int32), lax.axis_index("tensor").astype(jnp.int32)
    d_at, dz_at = jnp.reshape(d, (1,)), jnp.stack([d, z])
    part = width // net.n_dp
    net.flying = []
    line = Line(net)
    gains1, biases1 = norm_gain1[:, None], norm_bias1[:, None]
    gains2, biases2 = norm_gain2[:, None], norm_bias2[:, None]

    def own_slice(l):
        up = lax.dynamic_slice(up_weight, (l, d * part, 0, 0), (1, part, 2, width))
        down = lax.dynamic_slice(down_weight, (l, d * part, 0), (1, part, width))
        return jnp.concatenate([up.reshape(part, 2 * width), down[0]], axis=1)

    def own_weights(l):
        return [up_weight[l].reshape(width, 2 * width), down_weight[l]]

    seg = segments(bucket[0], lengths[0], rows, SHORT)
    same = seg[:, None] == seg[None, :]
    place = jnp.arange(rows, dtype=f32)
    dist = jnp.where(same, jnp.abs(place[:, None] - place[None, :]), 1e34)
    slopes = slopes_of()
    outputs, kept = [], []

    def run_attn(l, x):
        def call(x):
            return attn_fwd(l, x, qkv_weight, out_weight, gains1[l], biases1[l], dist, slopes)

        return line.run(call, x)

    def run_ff(groups, hb, acc, weights, norm=None):
        return line.run(lambda hb: ff_fwd(groups, d_at, hb, acc, weights, norm), hb)

    OWN, HALF, TWO, ALL = "own", "half", "two", "all"
    own = own_slice(0)
    far = {k: net.shift(own, k) for k in (1, 3)}
    x_t = x_in.T
    qkv, lse, ctx, ctx_t, pre1, hb, hb_t = run_attn(0, x_in)
    near = Gather(net, line, [far[1], far[3]])
    far[2] = net.shift(line.after(own), 2)
    mine = own_weights(0)
    acc = run_ff(((OWN, 0),), hb, (pre1, gains1[0], biases1[0]), mine)[0]
    planes = lax.all_gather(line.after(own_slice(1)), "tensor")
    near.second()
    back = Gather(net, line, [far[2][: part // 2], far[2][part // 2 :]])
    line.sync()
    line.need(planes)
    planes = line.after(planes)
    others = jnp.stack(
        [
            lax.dynamic_index_in_dim(planes, lax.rem(z - k + net.n_t, net.n_t), 0, keepdims=False)
            for k in range(1, net.n_t)
        ]
    )
    others = lax.all_gather(others, "dp")
    near.core()
    back.second()
    line.sync()
    back.core()
    line.sync()
    pre2, out, out_t = run_ff(
        ((TWO, 0), (TWO, 1), (HALF, 0)),
        hb,
        acc,
        near.pieces() + back.pieces(),
        (gains2[0], biases2[0]),
    )
    kept.append((x_t, qkv, lse, ctx_t, pre1, hb, hb_t, pre2))
    outputs.append(out)
    weights = [
        [
            (((OWN, 0),), mine),
            (((HALF, 0), (TWO, 0), (TWO, 1)), back.pieces() + near.pieces()),
        ]
    ]
    qkv, lse, ctx, ctx_t, pre1, hb, hb_t = run_attn(1, out)
    mine = own_weights(1)
    acc = run_ff(((OWN, 0),), hb, (pre1, gains1[1], biases1[1]), mine)[0]
    line.need(others)
    all_hb = lax.all_gather(line.after(hb), "tensor")
    pre2, out, _ = run_ff(
        ((ALL, 0), (ALL, 1), (ALL, 2)), hb, acc, [others], (gains2[1], biases2[1])
    )
    weights.append([(((OWN, 0), (ALL, 1), (ALL, 0), (ALL, 2)), mine + [others])])
    kept.append((out_t, qkv, lse, ctx_t, pre1, hb, hb_t, pre2))
    outputs.append(out)

    order = (0, 2, 1, 3)

    def run_ff_bwd(l, at, ins, **how):
        groups, arrays = weights[l][at]
        hb, hb_t = kept[l][5:7]
        return line.run(lambda hb: ff_bwd(groups, at, d_at, hb, hb_t, ins, arrays, **how), hb)

    def run_attn_bwd(l, dab, d_pre, small):
        x_t, qkv, lse, ctx_t = kept[l][:4]
        return line.run(
            lambda dab: attn_bwd(
                l,
                d_at,
                dab,
                qkv,
                lse,
                out_weight,
                dist,
                slopes,
                d_pre,
                x_t,
                ctx_t,
                qkv_weight,
                small,
            ),
            dab,
        )

    def over_dp(grads):
        return lax.psum_scatter(line.after(grads), "dp", scatter_dimension=0, tiled=True)[0]

    def to_owner(l, i):
        return net.shift(line.after(ff[l][i]), -order[i])

    pre1, pre2 = kept[1][4], kept[1][7]
    d_pre1, dyb, _, small2, dab, small1 = run_ff_bwd(
        1, 0, (cotangent, pre2, gains2[1], pre1, gains1[1]), first=True, last=True, grads=False
    )
    sent, keep, grad = run_attn_bwd(1, dab, d_pre1, (small1, small2))
    line.need(all_hb)
    all_dyb = lax.all_gather(line.after(dyb), "tensor")
    pre1, pre2 = kept[0][4], kept[0][7]
    share = Share(net, line, z, sent, keep)
    d_h, dyb, dyb_t, small2, g = run_ff_bwd(0, 0, (grad, pre2, gains2[0]), first=True)
    share.first()
    d_pre1, dab, small1, g = run_ff_bwd(
        0, 1, (dyb, dyb_t, d_h, pre1, gains1[0]), into=g, last=True
    )
    share.second()
    sent, keep, grad = run_attn_bwd(0, dab, d_pre1, (small1, small2))
    line.need(all_dyb)
    ff = {0: over_dp(g)}
    last_share = Share(net, line, z, sent, keep)
    share.far()
    line.sync()
    last_share.first()
    share.far_back()
    own_up, own_down = weights[1][0][1][:2]
    sent, keep = line.run(lambda up: ff_grads(d_at, up, own_down, all_hb, all_dyb), own_up)
    last_share.second()
    share.gather()
    fold = Fold(net, line, sent, keep)
    line.sync()
    last_share.far()
    share.gathered.second()
    line.sync()
    last_share.far_back()
    share.gathered.core()
    fold.first()
    line.sync()
    last_share.gather()
    found = line.run(
        lambda first: spread_out(1, dz_at, [first] + share.gathered.pieces()[1:], None),
        share.gathered.pieces()[0],
    )
    small = {1: found[0]}
    line.need(ff[0], fold.got)
    last_share.gathered.second()
    ff_parts = {0: [ff[0][0], to_owner(0, 1), to_owner(0, 2)]}
    fold.second()
    line.sync()
    last_share.gathered.core()
    line.sync()
    ff_parts[0].append(to_owner(0, 3))
    rest = found[1:]
    found = line.run(
        lambda first: spread_out(0, dz_at, [first] + last_share.gathered.pieces()[1:], rest),
        last_share.gathered.pieces()[0],
    )
    ff_parts[1] = [fold.done()]
    small[0] = found[0]
    attention_grads = found[1:]
    small = jnp.stack([small[l][:, 0] for l in range(LAYERS)])
    up_grads, down_grads = [], []
    for l in range(LAYERS):
        total = ff_parts[l][0].astype(f32)
        for one in ff_parts[l][1:]:
            total = total + one.astype(f32)
        up_grads.append(total[:, : 2 * width].reshape(part, 2, width))
        down_grads.append(total[:, 2 * width :].T)
    return (
        jnp.stack(outputs),
        grad,
        attention_grads[0],
        attention_grads[1],
        small[:, 0],
        small[:, 1],
        jnp.stack(up_grads),
        jnp.stack(down_grads),
        small[:, 2],
        small[:, 3],
    )


def attention_forward(x_low, wqkv, wo, g1, b1, same, decay):
    rows, width = x_low.shape
    qkv_low = dot(x_low, wqkv).astype(bf16)
    query, keys, values = split_heads(qkv_low, width)
    scores = scores_of(query, keys, same, decay)
    top = jnp.max(scores, axis=-1, keepdims=True)
    log_total = top + jnp.log(jnp.sum(jnp.exp(scores - top), axis=-1, keepdims=True))
    probs_low = jnp.exp(scores - log_total).astype(bf16)
    ctx_low = (
        jnp.einsum("hqk,khe->qhe", probs_low, values, preferred_element_type=f32)
        .reshape(rows, width)
        .astype(bf16)
    )
    pre_first = x_low.astype(f32) + dot(ctx_low, wo)
    normed = layer_norm(pre_first, g1, b1)
    return normed, (qkv_low, log_total, ctx_low, pre_first)


def attention_backward(d_attn_low, qkv_low, log_total, ctx_low, wo, same, decay):
    rows, width = d_attn_low.shape
    d_ctx = dot(d_attn_low, wo.T).astype(bf16).reshape(rows, HEADS, HEAD_DIM)
    query, keys, values = split_heads(qkv_low, width)
    probs = jnp.exp(scores_of(query, keys, same, decay) - log_total)
    probs_low = probs.astype(bf16)
    d_values = jnp.einsum("hqk,qhe->khe", probs_low, d_ctx, preferred_element_type=f32)
    d_probs = jnp.einsum("qhe,khe->hqk", d_ctx, values, preferred_element_type=f32)
    d_scores = (probs * (d_probs - jnp.sum(probs * d_probs, axis=-1, keepdims=True))).astype(bf16)
    d_query = jnp.einsum("hqk,khe->qhe", d_scores, keys, preferred_element_type=f32)
    d_keys = jnp.einsum("hqk,qhe->khe", d_scores, query, preferred_element_type=f32)
    scale = HEAD_DIM ** (-0.5)
    return jnp.concatenate(
        [
            (d_query * scale).reshape(rows, width),
            (d_keys * scale).reshape(rows, width),
            d_values.reshape(rows, width),
        ],
        axis=1,
    ).astype(bf16)


def plain_program(
    net,
    x_in,
    bucket,
    lengths,
    qkv_weight,
    out_weight,
    norm_gain1,
    norm_bias1,
    up_weight,
    down_weight,
    norm_gain2,
    norm_bias2,
    cotangent,
):
    rows, width = x_in.shape
    n_t = net.n_t
    hidden = down_weight.shape[1]
    seg = segments(bucket[0], lengths[0], rows, SHORT)
    same = seg[:, None] == seg[None, :]
    decay = alibi(rows, HEADS)
    ups = lax.all_gather(up_weight, "tensor", axis=0)
    downs = lax.all_gather(down_weight, "tensor", axis=0)
    groups = [
        [(ups[k, l].reshape(width, -1), downs[k, l]) for k in range(n_t)] for l in range(LAYERS)
    ]
    layer_in = x_in
    outputs, kept = [], []
    for l in range(LAYERS):
        x_low = layer_in
        normed, keep = attention_forward(
            x_low, qkv_weight[l], out_weight[l], norm_gain1[l], norm_bias1[l], same, decay
        )
        hb = normed.astype(bf16)
        pre_second = normed
        joined, act = [], []
        for up, down in groups[l]:
            joined.append(dot(hb, up))
            act.append(geglu(joined[-1]).astype(bf16))
            pre_second = pre_second + dot(act[-1], down)
        layer_in = layer_norm(pre_second, norm_gain2[l], norm_bias2[l]).astype(bf16)
        outputs.append(layer_in)
        kept.append((x_low, *keep, hb, pre_second, joined, act))
    grad = cotangent.astype(f32)
    attention_grads, small, up_grads, down_grads = ([None] * LAYERS for _ in range(4))
    for l in reversed(range(LAYERS)):
        x_low, qkv_low, log_total, ctx_low, pre_first, hb, pre_second, joined, act = kept[l]
        pull = jax.vjp(layer_norm, pre_second, norm_gain2[l], norm_bias2[l])[1]
        d_pre2, d_gain2, d_bias2 = pull(grad)
        dyb = d_pre2.astype(bf16)
        d_h = d_pre2
        d_joined = []
        for k, (up, down) in enumerate(groups[l]):
            d_act = dot(dyb, down.T)
            d_joined.append(jax.vjp(geglu, joined[k])[1](d_act)[0].astype(bf16))
            d_h = d_h + dot(d_joined[k], up.T)
        d_up = jnp.stack([dot(hb.T, one) for one in d_joined]).astype(bf16)
        d_down = jnp.stack([dot(dyb.T, one) for one in act]).astype(bf16)
        d_up = lax.psum_scatter(d_up, "tensor", scatter_dimension=0)
        d_down = lax.psum_scatter(d_down, "tensor", scatter_dimension=0)
        d_up = lax.psum_scatter(d_up, "dp", scatter_dimension=0, tiled=True)
        d_down = lax.psum_scatter(d_down, "dp", scatter_dimension=0, tiled=True)
        up_grads[l], down_grads[l] = d_up.astype(f32), d_down.astype(f32)
        pull = jax.vjp(layer_norm, pre_first, norm_gain1[l], norm_bias1[l])[1]
        d_pre1, d_gain1, d_bias1 = pull(d_h)
        small[l] = [d_gain1, d_bias1, d_gain2, d_bias2]
        dab = d_pre1.astype(bf16)
        d_qkv = attention_backward(dab, qkv_low, log_total, ctx_low, out_weight[l], same, decay)
        found = lax.psum(
            (dot(x_low.T, d_qkv).astype(bf16), dot(ctx_low.T, dab).astype(bf16)), BOTH
        )
        attention_grads[l] = [one.astype(f32) for one in found]
        grad = d_pre1 + dot(d_qkv, qkv_weight[l].T)
    small = lax.psum(jnp.stack(small[0] + small[1]), BOTH).reshape(LAYERS, 4, width)
    return (
        jnp.stack(outputs),
        grad,
        jnp.stack([one[0] for one in attention_grads]),
        jnp.stack([one[1] for one in attention_grads]),
        small[:, 0],
        small[:, 1],
        jnp.stack(up_grads).reshape(LAYERS, -1, 2, hidden),
        jnp.stack([one.T for one in down_grads]),
        small[:, 2],
        small[:, 3],
    )


def program(net, *args):
    width, hidden = args[0].shape[1], args[8].shape[1]
    quick = net.n_dp == 8 and net.n_t == 4 and hidden == width and width % 256 == 0
    return (quick_program if quick else plain_program)(net, *args)


def solution(mesh):
    in_specs = (
        P(BOTH, None),
        P(BOTH),
        P(BOTH, None),
        P(),
        P(),
        P(),
        P(),
        P(None, None, None, "tensor"),
        P(None, "tensor", None),
        P(),
        P(),
        P(BOTH, None),
    )
    out_specs = (
        P(None, BOTH, None),
        P(BOTH, None),
        P(),
        P(),
        P(),
        P(),
        P(None, "dp", None, "tensor"),
        P(None, "tensor", "dp"),
        P(),
        P(),
    )
    net = Net(mesh)
    return jax.shard_map(
        functools.partial(program, net),
        mesh=mesh,
        in_specs=in_specs,
        out_specs=out_specs,
        check_vma=False,
    )
```

```python
import functools

import jax
import jax.numpy as jnp
from jax import lax
from jax.experimental import pallas as pl
from jax.experimental.pallas import tpu as pltpu
from jax.sharding import PartitionSpec as P

HEADS = 12
HEAD_DIM = 64
SHORT = 128
LAYERS = 2

eps_norm = 1e-05
gelu_coef = 0.7978845608028654
masked_score = -1e30
bf16 = jnp.bfloat16
f32 = jnp.float32
BOTH = ("dp", "tensor")


def segments(bucket_one, lens, rows_dev, short_len):
    rows = jnp.arange(rows_dev, dtype=jnp.int32)
    slot = rows // short_len
    offset = rows - slot * short_len
    slots_all = jnp.arange(lens.shape[0], dtype=jnp.int32)
    slot_len = jnp.sum(jnp.where(slot[:, None] == slots_all[None, :], lens[None, :], 0), axis=1)
    total = jnp.sum(lens)
    is_long = bucket_one == 1
    real = jnp.where(is_long, rows < total, offset < slot_len)
    group = jnp.where(is_long, 0, slot)
    return jnp.where(real, group, lens.shape[0] + rows)


def alibi(rows_dev, heads):
    slopes = jnp.exp2(-8.0 * (jnp.arange(heads, dtype=f32) + 1.0) / heads)
    place = jnp.arange(rows_dev, dtype=f32)
    dist = jnp.abs(place[:, None] - place[None, :])
    return slopes[:, None, None] * dist[None, :, :]


def layer_norm(value, gain, bias):
    mean = jnp.mean(value, axis=-1, keepdims=True)
    centered = value - mean
    var = jnp.mean(centered * centered, axis=-1, keepdims=True)
    return centered * lax.rsqrt(var + eps_norm) * gain + bias


def geglu(joined):
    half = joined.shape[1] // 2
    gate = joined[:, :half]
    value = joined[:, half:]
    return 0.5 * gate * (1.0 + jnp.tanh(gelu_coef * (gate + 0.044715 * gate * gate * gate))) * value


def split_heads(qkv_low, width):
    rows = qkv_low.shape[0]
    query = qkv_low[:, :width].reshape(rows, HEADS, HEAD_DIM)
    keys = qkv_low[:, width : 2 * width].reshape(rows, HEADS, HEAD_DIM)
    values = qkv_low[:, 2 * width :].reshape(rows, HEADS, HEAD_DIM)
    return (query, keys, values)


def scores_of(query, keys, same, decay):
    raw = (
        jnp.einsum("qhe,khe->hqk", query, keys, preferred_element_type=f32) * HEAD_DIM ** (-0.5)
        - decay
    )
    return jnp.where(same[None, :, :], raw, masked_score)


def dot(a, b):
    return jnp.dot(a, b, preferred_element_type=f32)


class Net:
    def __init__(self, mesh):
        self.n_dp = mesh.shape["dp"]
        self.n_t = mesh.shape["tensor"]
        self.flying = []

    def flip(self, value, bit, wait=True):
        got = lax.ppermute(value, "dp", [(i, i ^ bit) for i in range(self.n_dp)])
        if wait:
            self.flying.append(got)
        return got

    def shift(self, value, step, wait=True):
        n = self.n_t
        got = lax.ppermute(value, "tensor", [(i, (i + step) % n) for i in range(n)])
        if wait:
            self.flying.append(got)
        return got


CHIPS = (0, 2, 4, 6)
COLOURS = ((2, 4), (4, 2))


def order_of(colour):
    one, two = COLOURS[colour]
    return [0, one, two, one ^ two]


def fold_order(colour):
    one, two = COLOURS[colour]
    return [0, two, one, one ^ two]


class Line:
    def __init__(self, net):
        self.net = net
        self.last = []

    def after(self, value):
        if not self.last:
            return value
        return lax.optimization_barrier((value, *self.last))[0]

    def sync(self):
        self.need(*self.net.flying)
        self.net.flying = []

    def need(self, *values):
        self.last = self.last + list(values)

    def run(self, call, first, *rest):
        out = call(self.after(first), *rest)
        self.last = [out[0] if isinstance(out, (tuple, list)) else out]
        self.sync()
        return out


class Gather:
    def __init__(self, net, line, slices):
        self.net, self.line = net, line
        n = len(slices) // 2
        self.held = [
            jnp.stack([line.after(one) for one in slices[c * n : (c + 1) * n]])[None]
            for c in range(2)
        ]
        self.got = [net.flip(self.held[c], COLOURS[c][0]) for c in range(2)]

    def join(self):
        self.held = [
            jnp.concatenate([self.held[c], self.line.after(self.got[c])], axis=0) for c in range(2)
        ]

    def second(self):
        self.join()
        self.got = [self.net.flip(self.held[c], COLOURS[c][1]) for c in range(2)]

    def core(self):
        self.join()
        self.held = jnp.concatenate(self.held, axis=0)
        self.got = self.net.flip(self.held, 1)

    def pieces(self):
        return [self.held, self.got]


VMEM_SPEC = pl.BlockSpec(memory_space=pltpu.VMEM)
ANY_SPEC = pl.BlockSpec(memory_space=pl.ANY)
SMEM_SPEC = pl.BlockSpec(memory_space=pltpu.SMEM)
NN = (((1,), (0,)), ((), ()))
NT = (((1,), (1,)), ((), ()))
TN = (((0,), (0,)), ((), ()))


def mm(a, b, dims=NN):
    return lax.dot_general(a, b, dims, preferred_element_type=f32)


def params(mib):
    return pltpu.CompilerParams(vmem_limit_bytes=60 << 20)


def cost(flops, nbytes):
    return pl.CostEstimate(flops=1024, transcendentals=0, bytes_accessed=1024)


def shape(dims, kind):
    return jax.ShapeDtypeStruct(dims, kind)


HBM_SPEC = pl.BlockSpec(memory_space=pltpu.MemorySpace.HBM)


class Copies:
    def __init__(self, ins, outs, sems):
        self.ins = [pltpu.make_async_copy(src, dst, sems.at[i]) for i, (src, dst) in enumerate(ins)]
        n = len(ins)
        self.outs = [
            pltpu.make_async_copy(src, dst, sems.at[n + i]) for i, (src, dst) in enumerate(outs)
        ]
        self.waited, self.put_out = set(), set()
        for copy in self.ins:
            copy.start()

    def wait(self, *which):
        for i in which or range(len(self.ins)):
            if i not in self.waited:
                self.waited.add(i)
                self.ins[i].wait()

    def put(self, *which):
        for i in which or range(len(self.outs)):
            if i not in self.put_out:
                self.put_out.add(i)
                self.outs[i].start()

    def finish(self):
        self.put()
        for copy in self.outs:
            copy.wait()


def staged_kernel(body, layers, n_smem, n_raw, n_out, n_raw_out, *refs):
    n_in = len(layers)
    smem, refs = refs[:n_smem], refs[n_smem:]
    ins, refs = refs[:n_in], refs[n_in:]
    raw, refs = refs[:n_raw], refs[n_raw:]
    outs, refs = refs[:n_out], refs[n_out:]
    raw_outs, refs = refs[:n_raw_out], refs[n_raw_out:]
    held, refs = refs[:n_in], refs[n_in:]
    made, refs = refs[:n_out], refs[n_out:]
    sems, scratch = refs[0], refs[1:]
    copies = Copies(
        [
            (ref if layer is None else ref.at[layer], to)
            for ref, layer, to in zip(ins, layers, held)
        ],
        list(zip(made, outs)),
        sems,
    )
    body(copies, smem, held, raw, made, raw_outs, scratch)
    copies.finish()


def staged(body, name, smem, ins, raw, outs, raw_outs, scratch, mib, work, aliases=None):
    pairs = [one if isinstance(one, tuple) else (one, None) for one in ins]
    layers = [layer for _, layer in pairs]
    held = [
        pltpu.VMEM(one.shape if layer is None else one.shape[1:], one.dtype) for one, layer in pairs
    ]
    made = [pltpu.VMEM(one.shape, one.dtype) for one in outs]
    n_copies = len(pairs) + len(outs)
    found = pl.pallas_call(
        functools.partial(
            staged_kernel, body, layers, len(smem), len(raw), len(outs), len(raw_outs)
        ),
        name=name,
        out_shape=tuple(outs) + tuple(raw_outs),
        in_specs=[SMEM_SPEC] * len(smem) + [HBM_SPEC] * (len(pairs) + len(raw)),
        out_specs=(HBM_SPEC,) * (len(outs) + len(raw_outs)),
        scratch_shapes=held + made + [pltpu.SemaphoreType.DMA((n_copies,))] + scratch,
        input_output_aliases=aliases or {},
        compiler_params=params(mib),
        cost_estimate=work,
    )(*smem, *[one for one, _ in pairs], *raw)
    return found


def normed_of(value):
    mean = jnp.mean(value, axis=-1, keepdims=True)
    centered = value - mean
    var = jnp.mean(centered * centered, axis=-1, keepdims=True)
    rstd = lax.rsqrt(var + eps_norm)
    return centered * rstd, rstd


def norm_back(grad, xhat, rstd, gain):
    scaled = grad * gain
    first = jnp.mean(scaled, axis=-1, keepdims=True)
    second = jnp.mean(scaled * xhat, axis=-1, keepdims=True)
    return rstd * (scaled - first - xhat * second)


def attn_fwd_kernel(copies, smem, ins, raw, outs, raw_outs, scratch):
    (slopes,) = smem
    x_ref, wqkv_ref, dist_ref, wo_ref, g_ref, b_ref = ins
    qkv_ref, lse_ref, ctx_ref, ctx_t_ref, pre_ref, hb_ref, hb_t_ref = outs
    rows, width = x_ref.shape
    copies.wait(0, 1)
    x = x_ref[...]
    for c in range(3):
        cols = pl.ds(c * width, width)
        qkv_ref[:, cols] = mm(x, wqkv_ref[:, cols]).astype(bf16)
    copies.put(0)
    copies.wait()
    lse_ref[...] = jnp.zeros_like(lse_ref)
    s_ref, p_ref = scratch

    def pair(p, _):
        def at(c):
            return pl.ds(pl.multiple_of(c * width + p * 128, 128), 128)

        key, val = qkv_ref[:, at(1)], qkv_ref[:, at(2)]
        query = qkv_ref[:, at(0)] * bf16(HEAD_DIM ** (-0.5))
        wide = lax.broadcasted_iota(jnp.int32, (rows, 128), 1)
        for side in range(2):
            mine = (wide < HEAD_DIM) == (side == 0)
            s_ref[side] = mm(jnp.where(mine, query, bf16(0)), key, NT)

        dist = dist_ref[...]
        total_lse = lse_ref[...]
        for side in range(2):
            s = s_ref[side] - slopes[2 * p + side] * dist
            top = jnp.max(s, axis=-1, keepdims=True)
            e = jnp.exp(s - top)
            total = jnp.sum(e, axis=-1, keepdims=True)
            p_ref[side] = (e * (1.0 / total)).astype(bf16)
            total_lse += jnp.where(wide == 2 * p + side, top + jnp.log(total), 0.0)
        lse_ref[...] = total_lse
        found = [mm(p_ref[side], val) for side in range(2)]
        ctx_ref[:, at(0)] = jnp.where(wide < HEAD_DIM, found[0], found[1]).astype(bf16)
        return 0

    lax.fori_loop(0, width // 128, pair, 0)
    copies.put(1, 2)
    ctx = ctx_ref[...]
    pre = x.astype(f32) + mm(ctx, wo_ref[...])
    pre_ref[...] = pre
    ctx_t_ref[...] = ctx.T
    copies.put(3, 4)
    xhat, _ = normed_of(pre)
    hb = (xhat * g_ref[...] + b_ref[...]).astype(bf16)
    hb_ref[...] = hb
    hb_t_ref[...] = hb.T


def slopes_of():
    steps = jnp.arange(HEADS, dtype=f32)
    return jnp.exp2(-8.0 * (steps + 1.0) / HEADS)


def attn_fwd(layer, x, wqkv, wo, gain, bias, dist, slopes):
    rows, width = x.shape
    return staged(
        attn_fwd_kernel,
        "attn_fwd",
        [slopes],
        [x, (wqkv, layer), dist, (wo, layer), gain, bias],
        [],
        [
            shape((rows, 3 * width), bf16),
            shape((rows, 128), f32),
            shape((rows, width), bf16),
            shape((width, rows), bf16),
            shape((rows, width), f32),
            shape((rows, width), bf16),
            shape((width, rows), bf16),
        ],
        [],
        [pltpu.VMEM((2, rows, rows), f32), pltpu.VMEM((2, rows, rows), bf16)],
        36,
        cost(0, 0),
    )


def attn_bwd_kernel(copies, smem, ins, raw, outs, raw_outs, scratch):
    slopes, at_ref = smem
    dab_ref, wo_ref, qkv_ref, lse_ref, dist_ref, x_t_ref, c_t_ref, wqkv_ref, dpre_ref = ins[:9]
    small_refs = ins[9:]
    dctx_ref, s_ref, dp_ref, p_ref, ds_ref, out_ref, rows_ref = scratch
    sent_ref, kept_ref, grad_ref = outs
    rows, width = dab_ref.shape
    scale = HEAD_DIM ** (-0.5)
    copies.wait(0, 1)
    dctx_ref[...] = mm(dab_ref[...], wo_ref[...], NT).astype(bf16)
    copies.wait(2, 3, 4)
    def pair(p, _):
        def at(c):
            return pl.ds(pl.multiple_of(c * width + p * 128, 128), 128)

        key, val, query = qkv_ref[:, at(1)], qkv_ref[:, at(2)], qkv_ref[:, at(0)]
        dctx = dctx_ref[:, at(0)]
        wide = lax.broadcasted_iota(jnp.int32, (rows, 128), 1)
        low = wide < HEAD_DIM
        for side in range(2):
            mine = low == (side == 0)
            s_ref[side] = mm(jnp.where(mine, query * bf16(scale), bf16(0)), key, NT)
            dp_ref[side] = mm(jnp.where(mine, dctx, bf16(0)), val, NT)

        dist = dist_ref[...]
        for side in range(2):
            lse = jnp.sum(jnp.where(wide == 2 * p + side, lse_ref[...], 0.0), axis=-1, keepdims=True)
            prob = jnp.exp(s_ref[side] - slopes[2 * p + side] * dist - lse)
            d_prob = dp_ref[side]
            mean = jnp.sum(prob * d_prob, axis=-1, keepdims=True)
            p_ref[side] = prob.astype(bf16)
            ds_ref[side] = (prob * (d_prob - mean)).astype(bf16)
        d_q = [mm(ds_ref[side], key) for side in range(2)]
        query_t, dctx_t = query.T, dctx.T
        d_k = [mm(query_t, ds_ref[side]).T for side in range(2)]
        d_v = [mm(dctx_t, p_ref[side]).T for side in range(2)]
        out_ref[:, at(0)] = (jnp.where(low, d_q[0], d_q[1]) * scale).astype(bf16)
        out_ref[:, at(1)] = (jnp.where(low, d_k[0], d_k[1]) * scale).astype(bf16)
        out_ref[:, at(2)] = jnp.where(low, d_v[0], d_v[1]).astype(bf16)
        return 0

    lax.fori_loop(0, width // 128, pair, 0)
    part = width // 8
    copies.wait()
    for colour in range(2):
        order = fold_order(colour)
        order = order + [j ^ 1 for j in order]
        pick_rows(at_ref[0], order, x_t_ref, rows_ref)
        for block in (2 * colour, 2 * colour + 1):
            if block < 3:
                rhs = out_ref[:, pl.ds(block * width, width)]
            else:
                rhs = dab_ref[...]
                pick_rows(at_ref[0], order, c_t_ref, rows_ref)
            total = mm(rows_ref[...], rhs).astype(bf16)
            few = small_refs[block // 2][block % 2 : block % 2 + 1]
            for i, j in enumerate(order):
                to = (kept_ref, sent_ref)[i // 4].at[block, i % 4]
                to[pl.ds(0, part)] = total[i * part : (i + 1) * part]
                here = jnp.where(jnp.bitwise_xor(at_ref[0], j) == 0, few, 0.0)
                to[pl.ds(part, FEW)] = jnp.broadcast_to(here, (FEW, width)).astype(bf16)
    copies.put(0, 1)
    grad_ref[...] = dpre_ref[...] + mm(out_ref[...], wqkv_ref[...], NT)


FEW = 8


def attn_bwd(layer, d, dab, qkv, lse, wo, dist, slopes, d_pre, x_t, ctx_t, wqkv, small):
    rows, width = dab.shape
    part = shape((4, 4, width // 8 + FEW, width), bf16)
    return staged(
        attn_bwd_kernel,
        "attn_bwd",
        [slopes, d],
        [dab, (wo, layer), qkv, lse, dist, x_t, ctx_t, (wqkv, layer), d_pre, *small],
        [],
        [part, part, shape((rows, width), f32)],
        [],
        [
            pltpu.VMEM((rows, width), bf16),
            pltpu.VMEM((2, rows, rows), f32),
            pltpu.VMEM((2, rows, rows), f32),
            pltpu.VMEM((2, rows, rows), bf16),
            pltpu.VMEM((2, rows, rows), bf16),
            pltpu.VMEM((rows, 3 * width), bf16),
            pltpu.VMEM((width, rows), bf16),
        ],
        40,
        cost(0, 0),
    )


def load_groups(groups, d, refs, w_ref, sems, slots):
    loads = []
    at = 0
    sources = {}
    for g, (kind, index) in enumerate(groups):
        mine = []
        s = g % slots
        if kind not in sources:
            count = 1 if kind == "all" else 2
            sources[kind] = refs[at : at + count]
            at += count
        source = sources[kind]
        part = source[0].shape[2] if kind != "own" else 0
        if kind == "own":
            split = source[0].shape[1]
            rest = source[1].shape[1]
            pairs = [
                (source[0], w_ref.at[s, :, pl.ds(0, split)]),
                (source[1], w_ref.at[s, :, pl.ds(split, rest)]),
            ]
        elif kind == "all":
            pairs = [(source[0].at[j, index], w_ref.at[s, pl.ds(j * part, part)]) for j in range(8)]
        else:
            pairs = []
            for colour in (index,) if kind == "two" else (0, 1):
                for c in range(2):
                    for i, j in enumerate(order_of(colour)):
                        slot = jnp.bitwise_xor(d, j ^ c)
                        if kind == "two":
                            row = slot * part
                        else:
                            row = slot * (2 * part) + colour * part
                        row = pl.multiple_of(row, part)
                        one = source[c].at[4 * colour + i, 0]
                        pairs.append((one, w_ref.at[s, pl.ds(row, part)]))
        for i, (one, to) in enumerate(pairs):
            mine.append(pltpu.make_async_copy(one, to, sems.at[g, i]))
        loads.append(mine)
    return loads


def gelu_parts(gate):
    square = gate * gate
    t = jnp.tanh(gelu_coef * gate * (1.0 + 0.044715 * square))
    half = 0.5 * (1.0 + t)
    slope = half + 0.5 * gate * (1.0 - t * t) * gelu_coef * (1.0 + 3 * 0.044715 * square)
    return gate * half, slope


TILE = 768


def ff_fwd_kernel(groups, first, last, copies, smem, ins, raw, outs, raw_outs, scratch):
    (at_ref,) = smem
    hb_ref, acc_refs, norm_refs = ins[0], ins[1 : 4 if first else 2], ins[4 if first else 2 :]
    pre_ref = outs[0]
    w_ref, sems = scratch
    width = hb_ref.shape[1]
    loads = load_groups(groups, at_ref[0], raw, w_ref, sems, len(groups))
    for load in loads:
        for copy in load:
            copy.start()
    copies.wait()
    if first:
        xhat, _ = normed_of(acc_refs[0][...])
        pre_ref[...] = xhat * acc_refs[1][...] + acc_refs[2][...]
    else:
        pre_ref[...] = acc_refs[0][...]
    for s in range(len(groups)):
        for copy in loads[s]:
            copy.wait()

        def step(n, _, s=s):
            def at(c):
                return pl.ds(pl.multiple_of(c * width + n * TILE, TILE), TILE)

            hb = hb_ref[...]
            gate, value = mm(hb, w_ref[s, :, at(0)]), mm(hb, w_ref[s, :, at(1)])
            act = (gelu_parts(gate)[0] * value).astype(bf16)
            pre_ref[...] += mm(act, w_ref[s, at(0), pl.ds(2 * width, width)])
            return 0

        step(0, 0)
    if last:
        copies.put(0)
        xhat, _ = normed_of(pre_ref[...])
        out = (xhat * norm_refs[0][...] + norm_refs[1][...]).astype(bf16)
        outs[1][...] = out
        outs[2][...] = out.T


def ff_fwd(groups, d, hb, acc, weights, norm=None):
    rows, width = hb.shape
    last = norm is not None
    acc = acc if isinstance(acc, tuple) else (acc,)
    outs = [shape((rows, width), f32)]
    if last:
        outs += [shape((rows, width), bf16), shape((width, rows), bf16)]
    n = len(groups)
    return staged(
        functools.partial(ff_fwd_kernel, groups, len(acc) == 3, last),
        "ff_fwd",
        [d],
        [hb, *acc, *(norm if last else ())],
        weights,
        outs,
        [],
        [
            pltpu.VMEM((n, width, 3 * width), bf16),
            pltpu.SemaphoreType.DMA((n, 16)),
        ],
        36,
        cost(0, 0),
    )


def pick_rows(d, order, from_ref, to_ref):
    rows = from_ref.shape[0] // 8
    for i, j in enumerate(order):
        at = pl.multiple_of(jnp.bitwise_xor(d, j) * rows, rows)
        to_ref[pl.ds(i * rows, rows), :] = from_ref[pl.ds(at, rows), :]


def norm_bwd(grad, pre, gain_ref, small_ref):
    xhat, rstd = normed_of(pre)
    small_ref[0:1] = jnp.sum(grad * xhat, axis=0, keepdims=True)
    small_ref[1:2] = jnp.sum(grad, axis=0, keepdims=True)
    return norm_back(grad, xhat, rstd, gain_ref[...])


def ff_bwd_kernel(
    groups, first, last, slot, with_grads, copies, smem, ins, raw, outs, raw_outs, scratch
):
    (at_ref,) = smem
    hb_ref, *ins = ins
    w_ref, sems, *scratch = scratch
    if with_grads:
        hb_t_ref, *ins = ins
        g_ref, out_sems = scratch
    width = hb_ref.shape[1]
    part = width // 8
    n = len(groups)
    loads = load_groups(groups, at_ref[0], raw, w_ref, sems, 2)
    for copy in loads[0]:
        copy.start()
    copies.wait()
    dh_ref, *outs = outs
    if first:
        grad_ref, pre_ref, gain_ref, *ins = ins
        dyb_ref, dyb_t_ref, small2_ref, *outs = outs
        d_pre = norm_bwd(grad_ref[...].astype(f32), pre_ref[...], gain_ref, small2_ref)
        dh_ref[...] = d_pre
        dyb_ref[...] = d_pre.astype(bf16)
        dyb_t_ref[...] = dyb_ref[...].T
    else:
        dyb_ref, dyb_t_ref, acc_ref, *ins = ins
        dh_ref[...] = acc_ref[...]
    out = []
    for s in range(n):
        if s + 1 < n:
            for copy in loads[s + 1]:
                copy.start()
        for copy in loads[s]:
            copy.wait()
        weights = w_ref.at[s % 2]

        def at(c):
            return pl.ds(c * width, width)

        hb = hb_ref[...]
        gate, value = mm(hb, weights[:, at(0)]), mm(hb, weights[:, at(1)])
        d_act = mm(dyb_ref[...], weights[:, at(2)], NT)
        gelu, slope = gelu_parts(gate)
        d_gate = (d_act * value * slope).astype(bf16)
        d_value = (d_act * gelu).astype(bf16)
        act = (gelu * value).astype(bf16)
        dh_ref[...] += mm(d_gate, weights[:, at(0)], NT) + mm(d_value, weights[:, at(1)], NT)
        if not with_grads:
            continue
        if s >= 2:
            out[s - 2].wait()
        grads = g_ref.at[s % 2]
        for c, (lhs, rhs) in enumerate(((hb_t_ref, d_gate), (hb_t_ref, d_value), (dyb_t_ref, act))):
            total = mm(lhs[...], rhs).astype(bf16)
            for j in range(8):
                grads[j, :, at(c)] = total[j * part : (j + 1) * part]
        out.append(pltpu.make_async_copy(grads, raw_outs[0].at[:, slot + s], out_sems.at[s]))
        out[s].start()
    if last:
        pre_ref, gain_ref = ins
        dab_ref, small1_ref = outs
        d_pre = norm_bwd(dh_ref[...], pre_ref[...], gain_ref, small1_ref)
        dh_ref[...] = d_pre
        dab_ref[...] = d_pre.astype(bf16)
    for one in out[-2:]:
        one.wait()


def ff_bwd(groups, slot, d, hb, hb_t, ins, weights, first=False, last=False, into=None, grads=True):
    rows, width = hb.shape
    n = len(groups)
    low, few = shape((rows, width), bf16), shape((2, width), f32)
    outs = [shape((rows, width), f32)]
    outs += [low, shape((width, rows), bf16), few] if first else []
    outs += [low, few] if last else []
    extra = [] if into is None else [into]
    n_in = 3 + len(ins) + len(weights)
    scratch = [pltpu.VMEM((2, width, 3 * width), bf16), pltpu.SemaphoreType.DMA((n, 16))]
    if grads:
        scratch += [
            pltpu.VMEM((2, 8, width // 8, 3 * width), bf16),
            pltpu.SemaphoreType.DMA((n,)),
        ]
    return staged(
        functools.partial(ff_bwd_kernel, groups, first, last, slot, grads),
        "ff_bwd",
        [d],
        [hb, *([hb_t] if grads else []), *ins],
        weights + extra,
        outs,
        [shape((8, 4, width // 8, 3 * width), bf16)] if grads else [],
        scratch,
        60,
        cost(0, 0),
        {n_in: len(outs)} if extra else {},
    )


def ff_grads_kernel(n, copies, smem, ins, raw, outs, raw_outs, scratch):
    up_ref, down_ref, *rows_refs = ins
    (total_ref,) = scratch
    (at_ref,) = smem
    sent_ref, kept_ref = outs
    width = up_ref.shape[0]
    part = width // 8
    copies.wait(0, 1)
    for s in range(n):
        copies.wait(2 + 2 * s, 3 + 2 * s)
        hb, dyb = rows_refs[2 * s][...], rows_refs[2 * s + 1][...]
        gate, value = mm(hb, up_ref[:, pl.ds(0, width)]), mm(hb, up_ref[:, pl.ds(width, width)])
        d_act = mm(dyb, down_ref[...], NT)
        gelu, slope = gelu_parts(gate)
        d_gate = (d_act * value * slope).astype(bf16)
        d_value = (d_act * gelu).astype(bf16)
        act = (gelu * value).astype(bf16)
        hb_t, dyb_t = hb.T, dyb.T
        for c, (lhs, rhs) in enumerate(((hb_t, d_gate), (hb_t, d_value), (dyb_t, act))):
            at = pl.ds(c * width, width)
            total = mm(lhs, rhs)
            total_ref[:, at] = total if s == 0 else total + total_ref[:, at]
    order = fold_order(0)
    for to_ref, flip in ((sent_ref, 1), (kept_ref, 0)):
        for i, j in enumerate(order):
            row = pl.multiple_of(jnp.bitwise_xor(at_ref[0], j ^ flip) * part, part)
            to_ref[i] = total_ref[pl.ds(row, part), :].astype(bf16)
        copies.put(flip ^ 1)


def ff_grads(d, up, down, all_hb, all_dyb):
    width = up.shape[0]
    return staged(
        functools.partial(ff_grads_kernel, all_hb.shape[0]),
        "ff_grads",
        [d],
        [up, down, *[(one, s) for s in range(all_hb.shape[0]) for one in (all_hb, all_dyb)]],
        [],
        [shape((4, width // 8, 3 * width), bf16)] * 2,
        [],
        [pltpu.VMEM((width, 3 * width), f32)],
        60,
        cost(0, 0),
    )


def add_low(a, b):
    return (a.astype(f32) + b.astype(f32)).astype(bf16)


class Fold:
    def __init__(self, net, line, sent, kept):
        self.net, self.line = net, line
        self.kept, self.got = kept, net.flip(line.after(sent), 1)

    def step(self, bit):
        got = self.line.after(self.got)
        half = self.kept.shape[0] // 2
        self.got = self.net.flip(add_low(self.kept[half:], got[half:]), bit, wait=False)
        self.kept = add_low(self.kept[:half], got[:half])

    def first(self):
        self.step(COLOURS[0][0])

    def second(self):
        self.step(COLOURS[0][1])

    def done(self):
        return self.kept[0].astype(f32) + self.line.after(self.got)[0].astype(f32)


class Share:
    def __init__(self, net, line, z, sent, kept):
        self.net, self.line, self.z = net, line, z
        self.kept, self.got = kept, net.flip(line.after(sent), 1)

    def first(self):
        got = self.line.after(self.got)
        half = [(self.kept[2 * c : 2 * c + 2], got[2 * c : 2 * c + 2]) for c in range(2)]
        self.got = [
            self.net.flip(add_low(kept[:, 2:], got[:, 2:]), COLOURS[c][0])
            for c, (kept, got) in enumerate(half)
        ]
        self.kept = [add_low(kept[:, :2], got[:, :2]) for kept, got in half]

    def second(self):
        got = [self.line.after(one) for one in self.got]
        self.got = [
            self.net.flip(add_low(self.kept[c][:, 1], got[c][:, 1]), COLOURS[c][1])
            for c in range(2)
        ]
        self.kept = [add_low(self.kept[c][:, 0], got[c][:, 0]) for c in range(2)]

    def far(self):
        n = self.net.n_t
        total = [add_low(self.kept[c], self.line.after(self.got[c])) for c in range(2)]
        total = jnp.concatenate(total, axis=0)
        parts = [
            lax.dynamic_index_in_dim(total, lax.rem(self.z - k + n, n), 0, keepdims=False)
            for k in range(n)
        ]
        self.parts = [parts[0]] + [self.net.shift(parts[k], -k) for k in range(1, n)]

    def far_back(self):
        total = self.parts[0].astype(f32)
        for part in self.parts[1:]:
            total = total + self.line.after(part).astype(f32)
        total = total.astype(bf16)
        self.slices = [total] + [self.net.shift(total, k) for k in range(1, self.net.n_t)]

    def gather(self):
        self.gathered = Gather(self.net, self.line, self.slices)


def spread_kernel(layer, copies, smem, ins, raw, outs, raw_outs, scratch):
    (at_ref,) = smem
    held = ins
    (small_ref,) = outs
    qkv_out, wo_out = raw_outs
    buf, sems = scratch
    d, z = at_ref[0], at_ref[1]
    rows, cols = held[0].shape[2:]
    rows = rows - FEW

    def each(act):
        for c in range(2):
            for k in range(4):
                block = lax.rem(z - k + 4, 4)
                for i, j in enumerate(order_of(k // 2)):
                    act(c, k, i, j, block, 16 * c + 4 * k + i)

    def copy_of(n, slot, block, to_qkv):
        row = pl.ds(pl.multiple_of(slot * rows, rows), rows)
        if to_qkv:
            col = pl.ds(pl.multiple_of(block * cols, cols), cols)
            to = qkv_out.at[layer, row, col]
        else:
            to = wo_out.at[layer, row, :]
        return pltpu.make_async_copy(buf.at[n], to, sems.at[n])

    def begin(c, k, i, j, block, n):
        if k == 0 and i == 0:
            copies.wait(c)
        ref = held[c].at[4 * (k // 2) + i, k % 2]
        slot = jnp.bitwise_xor(d, j ^ c)
        buf[n] = ref[pl.ds(0, rows)].astype(f32)

        @pl.when(block < 3)
        def _():
            copy_of(n, slot, block, True).start()

        @pl.when(block == 3)
        def _():
            copy_of(n, slot, block, False).start()

        @pl.when(slot == 0)
        def _():
            small_ref[block] = ref[pl.ds(rows, FEW)].astype(f32)

    def end(c, k, i, j, block, n):
        slot = jnp.bitwise_xor(d, j ^ c)

        @pl.when(block < 3)
        def _():
            copy_of(n, slot, block, True).wait()

        @pl.when(block == 3)
        def _():
            copy_of(n, slot, block, False).wait()

    each(begin)
    each(end)


def spread_out(layer, where, pieces, before):
    rows, cols = pieces[0].shape[2:]
    width = 8 * (rows - FEW)
    return staged(
        functools.partial(spread_kernel, layer),
        "spread_out",
        [where],
        pieces,
        [] if before is None else list(before),
        [shape((4, FEW, cols), f32)],
        [shape((LAYERS, width, 3 * cols), f32), shape((LAYERS, width, cols), f32)],
        [pltpu.VMEM((32, rows - FEW, cols), f32), pltpu.SemaphoreType.DMA((32,))],
        24,
        cost(0, 0),
        {} if before is None else {3: 1, 4: 2},
    )


def quick_program(
    net,
    x_in,
    bucket,
    lengths,
    qkv_weight,
    out_weight,
    norm_gain1,
    norm_bias1,
    up_weight,
    down_weight,
    norm_gain2,
    norm_bias2,
    cotangent,
):
    rows, width = x_in.shape
    d, z = lax.axis_index("dp").astype(jnp.int32), lax.axis_index("tensor").astype(jnp.int32)
    d_at, dz_at = jnp.reshape(d, (1,)), jnp.stack([d, z])
    part = width // net.n_dp
    net.flying = []
    line = Line(net)
    gains1, biases1 = norm_gain1[:, None], norm_bias1[:, None]
    gains2, biases2 = norm_gain2[:, None], norm_bias2[:, None]

    def own_slice(l):
        up = lax.dynamic_slice(up_weight, (l, d * part, 0, 0), (1, part, 2, width))
        down = lax.dynamic_slice(down_weight, (l, d * part, 0), (1, part, width))
        return jnp.concatenate([up.reshape(part, 2 * width), down[0]], axis=1)

    def own_weights(l):
        return [up_weight[l].reshape(width, 2 * width), down_weight[l]]

    seg = segments(bucket[0], lengths[0], rows, SHORT)
    same = seg[:, None] == seg[None, :]
    place = jnp.arange(rows, dtype=f32)
    dist = jnp.where(same, jnp.abs(place[:, None] - place[None, :]), 1e34)
    slopes = slopes_of()
    outputs, kept = [], []

    def run_attn(l, x):
        def call(x):
            return attn_fwd(l, x, qkv_weight, out_weight, gains1[l], biases1[l], dist, slopes)

        return line.run(call, x)

    def run_ff(groups, hb, acc, weights, norm=None):
        return line.run(lambda hb: ff_fwd(groups, d_at, hb, acc, weights, norm), hb)

    OWN, HALF, TWO, ALL = "own", "half", "two", "all"
    own = own_slice(0)
    far = {k: net.shift(own, k, wait=k != 2) for k in (1, 3, 2)}
    x_t = x_in.T
    qkv, lse, ctx, ctx_t, pre1, hb, hb_t = run_attn(0, x_in)
    planes = lax.all_gather(line.after(own_slice(1)), "tensor")
    near = Gather(net, line, [far[1], far[3]])
    mine = own_weights(0)
    acc = run_ff(((OWN, 0),), hb, (pre1, gains1[0], biases1[0]), mine)[0]
    line.need(far[2])
    near.second()
    back = Gather(net, line, [far[2][: part // 2], far[2][part // 2 :]])
    line.sync()
    line.need(planes)
    planes = line.after(planes)
    others = jnp.stack(
        [
            lax.dynamic_index_in_dim(planes, lax.rem(z - k + net.n_t, net.n_t), 0, keepdims=False)
            for k in range(1, net.n_t)
        ]
    )
    others = lax.all_gather(others, "dp")
    near.core()
    back.second()
    line.sync()
    back.core()
    acc = run_ff(((TWO, 0), (TWO, 1)), hb, acc, near.pieces())[0]
    pre2, out, out_t = run_ff(((HALF, 0),), hb, acc, back.pieces(), (gains2[0], biases2[0]))
    kept.append((x_t, qkv, lse, ctx_t, pre1, hb, hb_t, pre2))
    outputs.append(out)
    weights = [
        [
            (((OWN, 0),), mine),
            (((HALF, 0), (TWO, 0), (TWO, 1)), back.pieces() + near.pieces()),
        ]
    ]
    qkv, lse, ctx, ctx_t, pre1, hb, hb_t = run_attn(1, out)
    mine = own_weights(1)
    acc = run_ff(((OWN, 0),), hb, (pre1, gains1[1], biases1[1]), mine)[0]
    line.need(others)
    all_hb = lax.all_gather(line.after(hb), "tensor")
    pre2, out, _ = run_ff(
        ((ALL, 0), (ALL, 1), (ALL, 2)), hb, acc, [others], (gains2[1], biases2[1])
    )
    weights.append([(((OWN, 0), (ALL, 1), (ALL, 0), (ALL, 2)), mine + [others])])
    kept.append((out_t, qkv, lse, ctx_t, pre1, hb, hb_t, pre2))
    outputs.append(out)

    order = (0, 2, 1, 3)

    def run_ff_bwd(l, at, ins, **how):
        groups, arrays = weights[l][at]
        hb, hb_t = kept[l][5:7]
        return line.run(lambda hb: ff_bwd(groups, at, d_at, hb, hb_t, ins, arrays, **how), hb)

    def run_attn_bwd(l, dab, d_pre, small):
        x_t, qkv, lse, ctx_t = kept[l][:4]
        return line.run(
            lambda dab: attn_bwd(
                l,
                d_at,
                dab,
                qkv,
                lse,
                out_weight,
                dist,
                slopes,
                d_pre,
                x_t,
                ctx_t,
                qkv_weight,
                small,
            ),
            dab,
        )

    def over_dp(grads):
        return lax.psum_scatter(line.after(grads), "dp", scatter_dimension=0, tiled=True)[0]

    def to_owner(l, i):
        return net.shift(line.after(ff[l][i]), -order[i])

    pre1, pre2 = kept[1][4], kept[1][7]
    d_pre1, dyb, _, small2, dab, small1 = run_ff_bwd(
        1, 0, (cotangent, pre2, gains2[1], pre1, gains1[1]), first=True, last=True, grads=False
    )
    sent, keep, grad = run_attn_bwd(1, dab, d_pre1, (small1, small2))
    line.need(all_hb)
    all_dyb = lax.all_gather(line.after(dyb), "tensor")
    pre1, pre2 = kept[0][4], kept[0][7]
    share = Share(net, line, z, sent, keep)
    d_h, dyb, dyb_t, small2, g = run_ff_bwd(0, 0, (grad, pre2, gains2[0]), first=True)
    share.first()
    d_pre1, dab, small1, g = run_ff_bwd(
        0, 1, (dyb, dyb_t, d_h, pre1, gains1[0]), into=g, last=True
    )
    share.second()
    sent, keep, grad = run_attn_bwd(0, dab, d_pre1, (small1, small2))
    line.need(all_dyb)
    ff = {0: over_dp(g)}
    last_share = Share(net, line, z, sent, keep)
    share.far()
    line.sync()
    last_share.first()
    share.far_back()
    own_up, own_down = weights[1][0][1][:2]
    sent, keep = line.run(lambda up: ff_grads(d_at, up, own_down, all_hb, all_dyb), own_up)
    last_share.second()
    share.gather()
    fold = Fold(net, line, sent, keep)
    line.sync()
    last_share.far()
    share.gathered.second()
    line.sync()
    last_share.far_back()
    share.gathered.core()
    fold.first()
    line.sync()
    last_share.gather()
    found = line.run(
        lambda first: spread_out(1, dz_at, [first] + share.gathered.pieces()[1:], None),
        share.gathered.pieces()[0],
    )
    small = {1: found[0]}
    line.need(ff[0], fold.got)
    last_share.gathered.second()
    ff_parts = {0: [ff[0][0], to_owner(0, 1), to_owner(0, 2)]}
    fold.second()
    line.sync()
    last_share.gathered.core()
    line.sync()
    ff_parts[0].append(to_owner(0, 3))
    rest = found[1:]
    found = line.run(
        lambda first: spread_out(0, dz_at, [first] + last_share.gathered.pieces()[1:], rest),
        last_share.gathered.pieces()[0],
    )
    ff_parts[1] = [fold.done()]
    small[0] = found[0]
    attention_grads = found[1:]
    small = jnp.stack([small[l][:, 0] for l in range(LAYERS)])
    up_grads, down_grads = [], []
    for l in range(LAYERS):
        total = ff_parts[l][0].astype(f32)
        for one in ff_parts[l][1:]:
            total = total + one.astype(f32)
        up_grads.append(total[:, : 2 * width].reshape(part, 2, width))
        down_grads.append(total[:, 2 * width :].T)
    return (
        jnp.stack(outputs),
        grad,
        attention_grads[0],
        attention_grads[1],
        small[:, 0],
        small[:, 1],
        jnp.stack(up_grads),
        jnp.stack(down_grads),
        small[:, 2],
        small[:, 3],
    )


def attention_forward(x_low, wqkv, wo, g1, b1, same, decay):
    rows, width = x_low.shape
    qkv_low = dot(x_low, wqkv).astype(bf16)
    query, keys, values = split_heads(qkv_low, width)
    scores = scores_of(query, keys, same, decay)
    top = jnp.max(scores, axis=-1, keepdims=True)
    log_total = top + jnp.log(jnp.sum(jnp.exp(scores - top), axis=-1, keepdims=True))
    probs_low = jnp.exp(scores - log_total).astype(bf16)
    ctx_low = (
        jnp.einsum("hqk,khe->qhe", probs_low, values, preferred_element_type=f32)
        .reshape(rows, width)
        .astype(bf16)
    )
    pre_first = x_low.astype(f32) + dot(ctx_low, wo)
    normed = layer_norm(pre_first, g1, b1)
    return normed, (qkv_low, log_total, ctx_low, pre_first)


def attention_backward(d_attn_low, qkv_low, log_total, ctx_low, wo, same, decay):
    rows, width = d_attn_low.shape
    d_ctx = dot(d_attn_low, wo.T).astype(bf16).reshape(rows, HEADS, HEAD_DIM)
    query, keys, values = split_heads(qkv_low, width)
    probs = jnp.exp(scores_of(query, keys, same, decay) - log_total)
    probs_low = probs.astype(bf16)
    d_values = jnp.einsum("hqk,qhe->khe", probs_low, d_ctx, preferred_element_type=f32)
    d_probs = jnp.einsum("qhe,khe->hqk", d_ctx, values, preferred_element_type=f32)
    d_scores = (probs * (d_probs - jnp.sum(probs * d_probs, axis=-1, keepdims=True))).astype(bf16)
    d_query = jnp.einsum("hqk,khe->qhe", d_scores, keys, preferred_element_type=f32)
    d_keys = jnp.einsum("hqk,qhe->khe", d_scores, query, preferred_element_type=f32)
    scale = HEAD_DIM ** (-0.5)
    return jnp.concatenate(
        [
            (d_query * scale).reshape(rows, width),
            (d_keys * scale).reshape(rows, width),
            d_values.reshape(rows, width),
        ],
        axis=1,
    ).astype(bf16)


def plain_program(
    net,
    x_in,
    bucket,
    lengths,
    qkv_weight,
    out_weight,
    norm_gain1,
    norm_bias1,
    up_weight,
    down_weight,
    norm_gain2,
    norm_bias2,
    cotangent,
):
    rows, width = x_in.shape
    n_t = net.n_t
    hidden = down_weight.shape[1]
    seg = segments(bucket[0], lengths[0], rows, SHORT)
    same = seg[:, None] == seg[None, :]
    decay = alibi(rows, HEADS)
    ups = lax.all_gather(up_weight, "tensor", axis=0)
    downs = lax.all_gather(down_weight, "tensor", axis=0)
    groups = [
        [(ups[k, l].reshape(width, -1), downs[k, l]) for k in range(n_t)] for l in range(LAYERS)
    ]
    layer_in = x_in
    outputs, kept = [], []
    for l in range(LAYERS):
        x_low = layer_in
        normed, keep = attention_forward(
            x_low, qkv_weight[l], out_weight[l], norm_gain1[l], norm_bias1[l], same, decay
        )
        hb = normed.astype(bf16)
        pre_second = normed
        joined, act = [], []
        for up, down in groups[l]:
            joined.append(dot(hb, up))
            act.append(geglu(joined[-1]).astype(bf16))
            pre_second = pre_second + dot(act[-1], down)
        layer_in = layer_norm(pre_second, norm_gain2[l], norm_bias2[l]).astype(bf16)
        outputs.append(layer_in)
        kept.append((x_low, *keep, hb, pre_second, joined, act))
    grad = cotangent.astype(f32)
    attention_grads, small, up_grads, down_grads = ([None] * LAYERS for _ in range(4))
    for l in reversed(range(LAYERS)):
        x_low, qkv_low, log_total, ctx_low, pre_first, hb, pre_second, joined, act = kept[l]
        pull = jax.vjp(layer_norm, pre_second, norm_gain2[l], norm_bias2[l])[1]
        d_pre2, d_gain2, d_bias2 = pull(grad)
        dyb = d_pre2.astype(bf16)
        d_h = d_pre2
        d_joined = []
        for k, (up, down) in enumerate(groups[l]):
            d_act = dot(dyb, down.T)
            d_joined.append(jax.vjp(geglu, joined[k])[1](d_act)[0].astype(bf16))
            d_h = d_h + dot(d_joined[k], up.T)
        d_up = jnp.stack([dot(hb.T, one) for one in d_joined]).astype(bf16)
        d_down = jnp.stack([dot(dyb.T, one) for one in act]).astype(bf16)
        d_up = lax.psum_scatter(d_up, "tensor", scatter_dimension=0)
        d_down = lax.psum_scatter(d_down, "tensor", scatter_dimension=0)
        d_up = lax.psum_scatter(d_up, "dp", scatter_dimension=0, tiled=True)
        d_down = lax.psum_scatter(d_down, "dp", scatter_dimension=0, tiled=True)
        up_grads[l], down_grads[l] = d_up.astype(f32), d_down.astype(f32)
        pull = jax.vjp(layer_norm, pre_first, norm_gain1[l], norm_bias1[l])[1]
        d_pre1, d_gain1, d_bias1 = pull(d_h)
        small[l] = [d_gain1, d_bias1, d_gain2, d_bias2]
        dab = d_pre1.astype(bf16)
        d_qkv = attention_backward(dab, qkv_low, log_total, ctx_low, out_weight[l], same, decay)
        found = lax.psum(
            (dot(x_low.T, d_qkv).astype(bf16), dot(ctx_low.T, dab).astype(bf16)), BOTH
        )
        attention_grads[l] = [one.astype(f32) for one in found]
        grad = d_pre1 + dot(d_qkv, qkv_weight[l].T)
    small = lax.psum(jnp.stack(small[0] + small[1]), BOTH).reshape(LAYERS, 4, width)
    return (
        jnp.stack(outputs),
        grad,
        jnp.stack([one[0] for one in attention_grads]),
        jnp.stack([one[1] for one in attention_grads]),
        small[:, 0],
        small[:, 1],
        jnp.stack(up_grads).reshape(LAYERS, -1, 2, hidden),
        jnp.stack([one.T for one in down_grads]),
        small[:, 2],
        small[:, 3],
    )


def program(net, *args):
    width, hidden = args[0].shape[1], args[8].shape[1]
    quick = net.n_dp == 8 and net.n_t == 4 and hidden == width and width % 256 == 0
    return (quick_program if quick else plain_program)(net, *args)


def solution(mesh):
    in_specs = (
        P(BOTH, None),
        P(BOTH),
        P(BOTH, None),
        P(),
        P(),
        P(),
        P(),
        P(None, None, None, "tensor"),
        P(None, "tensor", None),
        P(),
        P(),
        P(BOTH, None),
    )
    out_specs = (
        P(None, BOTH, None),
        P(BOTH, None),
        P(),
        P(),
        P(),
        P(),
        P(None, "dp", None, "tensor"),
        P(None, "tensor", "dp"),
        P(),
        P(),
    )
    net = Net(mesh)
    return jax.shard_map(
        functools.partial(program, net),
        mesh=mesh,
        in_specs=in_specs,
        out_specs=out_specs,
        check_vma=False,
    )
```

```python
import functools

import jax
import jax.numpy as jnp
from jax import lax
from jax.experimental import pallas as pl
from jax.experimental.pallas import tpu as pltpu
from jax.sharding import PartitionSpec as P

HEADS = 12
HEAD_DIM = 64
SHORT = 128
LAYERS = 2

eps_norm = 1e-05
gelu_coef = 0.7978845608028654
masked_score = -1e30
bf16 = jnp.bfloat16
f32 = jnp.float32
BOTH = ("dp", "tensor")


def segments(bucket_one, lens, rows_dev, short_len):
    rows = jnp.arange(rows_dev, dtype=jnp.int32)
    slot = rows // short_len
    offset = rows - slot * short_len
    slots_all = jnp.arange(lens.shape[0], dtype=jnp.int32)
    slot_len = jnp.sum(jnp.where(slot[:, None] == slots_all[None, :], lens[None, :], 0), axis=1)
    total = jnp.sum(lens)
    is_long = bucket_one == 1
    real = jnp.where(is_long, rows < total, offset < slot_len)
    group = jnp.where(is_long, 0, slot)
    return jnp.where(real, group, lens.shape[0] + rows)


def alibi(rows_dev, heads):
    slopes = jnp.exp2(-8.0 * (jnp.arange(heads, dtype=f32) + 1.0) / heads)
    place = jnp.arange(rows_dev, dtype=f32)
    dist = jnp.abs(place[:, None] - place[None, :])
    return slopes[:, None, None] * dist[None, :, :]


def layer_norm(value, gain, bias):
    mean = jnp.mean(value, axis=-1, keepdims=True)
    centered = value - mean
    var = jnp.mean(centered * centered, axis=-1, keepdims=True)
    return centered * lax.rsqrt(var + eps_norm) * gain + bias


def geglu(joined):
    half = joined.shape[1] // 2
    gate = joined[:, :half]
    value = joined[:, half:]
    return 0.5 * gate * (1.0 + jnp.tanh(gelu_coef * (gate + 0.044715 * gate * gate * gate))) * value


def split_heads(qkv_low, width):
    rows = qkv_low.shape[0]
    query = qkv_low[:, :width].reshape(rows, HEADS, HEAD_DIM)
    keys = qkv_low[:, width : 2 * width].reshape(rows, HEADS, HEAD_DIM)
    values = qkv_low[:, 2 * width :].reshape(rows, HEADS, HEAD_DIM)
    return (query, keys, values)


def scores_of(query, keys, same, decay):
    raw = (
        jnp.einsum("qhe,khe->hqk", query, keys, preferred_element_type=f32) * HEAD_DIM ** (-0.5)
        - decay
    )
    return jnp.where(same[None, :, :], raw, masked_score)


def dot(a, b):
    return jnp.dot(a, b, preferred_element_type=f32)


class Net:
    def __init__(self, mesh):
        self.n_dp = mesh.shape["dp"]
        self.n_t = mesh.shape["tensor"]
        self.flying = []

    def flip(self, value, bit, wait=True):
        got = lax.ppermute(value, "dp", [(i, i ^ bit) for i in range(self.n_dp)])
        if wait:
            self.flying.append(got)
        return got

    def shift(self, value, step, wait=True):
        n = self.n_t
        got = lax.ppermute(value, "tensor", [(i, (i + step) % n) for i in range(n)])
        if wait:
            self.flying.append(got)
        return got


CHIPS = (0, 2, 4, 6)
COLOURS = ((2, 4), (4, 2))


def order_of(colour):
    one, two = COLOURS[colour]
    return [0, one, two, one ^ two]


def fold_order(colour):
    one, two = COLOURS[colour]
    return [0, two, one, one ^ two]


class Line:
    def __init__(self, net):
        self.net = net
        self.last = []

    def after(self, value):
        if not self.last:
            return value
        return lax.optimization_barrier((value, *self.last))[0]

    def sync(self):
        self.need(*self.net.flying)
        self.net.flying = []

    def need(self, *values):
        self.last = self.last + list(values)

    def run(self, call, first, *rest):
        out = call(self.after(first), *rest)
        self.last = [out[0] if isinstance(out, (tuple, list)) else out]
        self.sync()
        return out


class Gather:
    def __init__(self, net, line, slices):
        self.net, self.line = net, line
        n = len(slices) // 2
        self.held = [
            jnp.stack([line.after(one) for one in slices[c * n : (c + 1) * n]])[None]
            for c in range(2)
        ]
        self.got = [net.flip(self.held[c], COLOURS[c][0]) for c in range(2)]

    def join(self):
        self.held = [
            jnp.concatenate([self.held[c], self.line.after(self.got[c])], axis=0) for c in range(2)
        ]

    def second(self):
        self.join()
        self.got = [self.net.flip(self.held[c], COLOURS[c][1]) for c in range(2)]

    def core(self):
        self.join()
        self.held = jnp.concatenate(self.held, axis=0)
        self.got = self.net.flip(self.held, 1)

    def pieces(self):
        return [self.held, self.got]


VMEM_SPEC = pl.BlockSpec(memory_space=pltpu.VMEM)
ANY_SPEC = pl.BlockSpec(memory_space=pl.ANY)
SMEM_SPEC = pl.BlockSpec(memory_space=pltpu.SMEM)
NN = (((1,), (0,)), ((), ()))
NT = (((1,), (1,)), ((), ()))
TN = (((0,), (0,)), ((), ()))


def mm(a, b, dims=NN):
    return lax.dot_general(a, b, dims, preferred_element_type=f32)


def params(mib):
    return pltpu.CompilerParams(vmem_limit_bytes=60 << 20)


def cost(flops, nbytes):
    return pl.CostEstimate(flops=1024, transcendentals=0, bytes_accessed=1024)


def shape(dims, kind):
    return jax.ShapeDtypeStruct(dims, kind)


HBM_SPEC = pl.BlockSpec(memory_space=pltpu.MemorySpace.HBM)


class Copies:
    def __init__(self, ins, outs, sems):
        self.ins = [pltpu.make_async_copy(src, dst, sems.at[i]) for i, (src, dst) in enumerate(ins)]
        n = len(ins)
        self.outs = [
            pltpu.make_async_copy(src, dst, sems.at[n + i]) for i, (src, dst) in enumerate(outs)
        ]
        self.waited, self.put_out = set(), set()
        for copy in self.ins:
            copy.start()

    def wait(self, *which):
        for i in which or range(len(self.ins)):
            if i not in self.waited:
                self.waited.add(i)
                self.ins[i].wait()

    def put(self, *which):
        for i in which or range(len(self.outs)):
            if i not in self.put_out:
                self.put_out.add(i)
                self.outs[i].start()

    def finish(self):
        self.put()
        for copy in self.outs:
            copy.wait()


def staged_kernel(body, layers, n_smem, n_raw, n_out, n_raw_out, *refs):
    n_in = len(layers)
    smem, refs = refs[:n_smem], refs[n_smem:]
    ins, refs = refs[:n_in], refs[n_in:]
    raw, refs = refs[:n_raw], refs[n_raw:]
    outs, refs = refs[:n_out], refs[n_out:]
    raw_outs, refs = refs[:n_raw_out], refs[n_raw_out:]
    held, refs = refs[:n_in], refs[n_in:]
    made, refs = refs[:n_out], refs[n_out:]
    sems, scratch = refs[0], refs[1:]
    copies = Copies(
        [
            (ref if layer is None else ref.at[layer], to)
            for ref, layer, to in zip(ins, layers, held)
        ],
        list(zip(made, outs)),
        sems,
    )
    body(copies, smem, held, raw, made, raw_outs, scratch)
    copies.finish()


def staged(body, name, smem, ins, raw, outs, raw_outs, scratch, mib, work, aliases=None):
    pairs = [one if isinstance(one, tuple) else (one, None) for one in ins]
    layers = [layer for _, layer in pairs]
    held = [
        pltpu.VMEM(one.shape if layer is None else one.shape[1:], one.dtype) for one, layer in pairs
    ]
    made = [pltpu.VMEM(one.shape, one.dtype) for one in outs]
    n_copies = len(pairs) + len(outs)
    found = pl.pallas_call(
        functools.partial(
            staged_kernel, body, layers, len(smem), len(raw), len(outs), len(raw_outs)
        ),
        name=name,
        out_shape=tuple(outs) + tuple(raw_outs),
        in_specs=[SMEM_SPEC] * len(smem) + [HBM_SPEC] * (len(pairs) + len(raw)),
        out_specs=(HBM_SPEC,) * (len(outs) + len(raw_outs)),
        scratch_shapes=held + made + [pltpu.SemaphoreType.DMA((n_copies,))] + scratch,
        input_output_aliases=aliases or {},
        compiler_params=params(mib),
        cost_estimate=work,
    )(*smem, *[one for one, _ in pairs], *raw)
    return found


def normed_of(value):
    mean = jnp.mean(value, axis=-1, keepdims=True)
    centered = value - mean
    var = jnp.mean(centered * centered, axis=-1, keepdims=True)
    rstd = lax.rsqrt(var + eps_norm)
    return centered * rstd, rstd


def norm_back(grad, xhat, rstd, gain):
    scaled = grad * gain
    first = jnp.mean(scaled, axis=-1, keepdims=True)
    second = jnp.mean(scaled * xhat, axis=-1, keepdims=True)
    return rstd * (scaled - first - xhat * second)


def attn_fwd_kernel(copies, smem, ins, raw, outs, raw_outs, scratch):
    (slopes,) = smem
    x_ref, wqkv_ref, dist_ref, wo_ref, g_ref, b_ref = ins
    qkv_ref, lse_ref, ctx_ref, ctx_t_ref, pre_ref, hb_ref, hb_t_ref = outs
    rows, width = x_ref.shape
    copies.wait(0, 1)
    x = x_ref[...]
    for c in range(3):
        cols = pl.ds(c * width, width)
        qkv_ref[:, cols] = mm(x, wqkv_ref[:, cols]).astype(bf16)
    copies.put(0)
    copies.wait()
    lse_ref[...] = jnp.zeros_like(lse_ref)
    s_ref, p_ref = scratch

    def pair(p, _):
        def at(c):
            return pl.ds(pl.multiple_of(c * width + p * 128, 128), 128)

        key, val = qkv_ref[:, at(1)], qkv_ref[:, at(2)]
        query = qkv_ref[:, at(0)] * bf16(HEAD_DIM ** (-0.5))
        wide = lax.broadcasted_iota(jnp.int32, (rows, 128), 1)
        for side in range(2):
            mine = (wide < HEAD_DIM) == (side == 0)
            s_ref[side] = mm(jnp.where(mine, query, bf16(0)), key, NT)

        dist = dist_ref[...]
        total_lse = lse_ref[...]
        for side in range(2):
            s = s_ref[side] - slopes[2 * p + side] * dist
            top = jnp.max(s, axis=-1, keepdims=True)
            e = jnp.exp(s - top)
            total = jnp.sum(e, axis=-1, keepdims=True)
            p_ref[side] = (e * (1.0 / total)).astype(bf16)
            total_lse += jnp.where(wide == 2 * p + side, top + jnp.log(total), 0.0)
        lse_ref[...] = total_lse
        found = [mm(p_ref[side], val) for side in range(2)]
        ctx_ref[:, at(0)] = jnp.where(wide < HEAD_DIM, found[0], found[1]).astype(bf16)
        return 0

    lax.fori_loop(0, width // 128, pair, 0)
    copies.put(1, 2)
    ctx = ctx_ref[...]
    pre = x.astype(f32) + mm(ctx, wo_ref[...])
    pre_ref[...] = pre
    ctx_t_ref[...] = ctx.T
    copies.put(3, 4)
    xhat, _ = normed_of(pre)
    hb = (xhat * g_ref[...] + b_ref[...]).astype(bf16)
    hb_ref[...] = hb
    hb_t_ref[...] = hb.T


def slopes_of():
    steps = jnp.arange(HEADS, dtype=f32)
    return jnp.exp2(-8.0 * (steps + 1.0) / HEADS)


def attn_fwd(layer, x, wqkv, wo, gain, bias, dist, slopes):
    rows, width = x.shape
    return staged(
        attn_fwd_kernel,
        "attn_fwd",
        [slopes],
        [x, (wqkv, layer), dist, (wo, layer), gain, bias],
        [],
        [
            shape((rows, 3 * width), bf16),
            shape((rows, 128), f32),
            shape((rows, width), bf16),
            shape((width, rows), bf16),
            shape((rows, width), f32),
            shape((rows, width), bf16),
            shape((width, rows), bf16),
        ],
        [],
        [pltpu.VMEM((2, rows, rows), f32), pltpu.VMEM((2, rows, rows), bf16)],
        36,
        cost(0, 0),
    )


def attn_bwd_kernel(copies, smem, ins, raw, outs, raw_outs, scratch):
    slopes, at_ref = smem
    dab_ref, wo_ref, qkv_ref, lse_ref, dist_ref, x_t_ref, c_t_ref, wqkv_ref, dpre_ref = ins[:9]
    small_refs = ins[9:]
    dctx_ref, s_ref, dp_ref, p_ref, ds_ref, out_ref, rows_ref = scratch
    sent_ref, kept_ref, grad_ref = outs
    rows, width = dab_ref.shape
    scale = HEAD_DIM ** (-0.5)
    copies.wait(0, 1)
    dctx_ref[...] = mm(dab_ref[...], wo_ref[...], NT).astype(bf16)
    copies.wait(2, 3, 4)
    def pair(p, _):
        def at(c):
            return pl.ds(pl.multiple_of(c * width + p * 128, 128), 128)

        key, val, query = qkv_ref[:, at(1)], qkv_ref[:, at(2)], qkv_ref[:, at(0)]
        dctx = dctx_ref[:, at(0)]
        wide = lax.broadcasted_iota(jnp.int32, (rows, 128), 1)
        low = wide < HEAD_DIM
        for side in range(2):
            mine = low == (side == 0)
            s_ref[side] = mm(jnp.where(mine, query * bf16(scale), bf16(0)), key, NT)
            dp_ref[side] = mm(jnp.where(mine, dctx, bf16(0)), val, NT)

        dist = dist_ref[...]
        for side in range(2):
            lse = jnp.sum(jnp.where(wide == 2 * p + side, lse_ref[...], 0.0), axis=-1, keepdims=True)
            prob = jnp.exp(s_ref[side] - slopes[2 * p + side] * dist - lse)
            d_prob = dp_ref[side]
            mean = jnp.sum(prob * d_prob, axis=-1, keepdims=True)
            p_ref[side] = prob.astype(bf16)
            ds_ref[side] = (prob * (d_prob - mean)).astype(bf16)
        d_q = [mm(ds_ref[side], key) for side in range(2)]
        query_t, dctx_t = query.T, dctx.T
        d_k = [mm(query_t, ds_ref[side]).T for side in range(2)]
        d_v = [mm(dctx_t, p_ref[side]).T for side in range(2)]
        out_ref[:, at(0)] = (jnp.where(low, d_q[0], d_q[1]) * scale).astype(bf16)
        out_ref[:, at(1)] = (jnp.where(low, d_k[0], d_k[1]) * scale).astype(bf16)
        out_ref[:, at(2)] = jnp.where(low, d_v[0], d_v[1]).astype(bf16)
        return 0

    lax.fori_loop(0, width // 128, pair, 0)
    part = width // 8
    copies.wait()
    for colour in range(2):
        order = fold_order(colour)
        order = order + [j ^ 1 for j in order]
        pick_rows(at_ref[0], order, x_t_ref, rows_ref)
        for block in (2 * colour, 2 * colour + 1):
            if block < 3:
                rhs = out_ref[:, pl.ds(block * width, width)]
            else:
                rhs = dab_ref[...]
                pick_rows(at_ref[0], order, c_t_ref, rows_ref)
            total = mm(rows_ref[...], rhs).astype(bf16)
            few = small_refs[block // 2][block % 2 : block % 2 + 1]
            for i, j in enumerate(order):
                to = (kept_ref, sent_ref)[i // 4].at[block, i % 4]
                to[pl.ds(0, part)] = total[i * part : (i + 1) * part]
                here = jnp.where(jnp.bitwise_xor(at_ref[0], j) == 0, few, 0.0)
                to[pl.ds(part, FEW)] = jnp.broadcast_to(here, (FEW, width)).astype(bf16)
    copies.put(0, 1)
    grad_ref[...] = dpre_ref[...] + mm(out_ref[...], wqkv_ref[...], NT)


FEW = 8


def attn_bwd(layer, d, dab, qkv, lse, wo, dist, slopes, d_pre, x_t, ctx_t, wqkv, small):
    rows, width = dab.shape
    part = shape((4, 4, width // 8 + FEW, width), bf16)
    return staged(
        attn_bwd_kernel,
        "attn_bwd",
        [slopes, d],
        [dab, (wo, layer), qkv, lse, dist, x_t, ctx_t, (wqkv, layer), d_pre, *small],
        [],
        [part, part, shape((rows, width), f32)],
        [],
        [
            pltpu.VMEM((rows, width), bf16),
            pltpu.VMEM((2, rows, rows), f32),
            pltpu.VMEM((2, rows, rows), f32),
            pltpu.VMEM((2, rows, rows), bf16),
            pltpu.VMEM((2, rows, rows), bf16),
            pltpu.VMEM((rows, 3 * width), bf16),
            pltpu.VMEM((width, rows), bf16),
        ],
        40,
        cost(0, 0),
    )


def load_groups(groups, d, refs, w_ref, sems, slots):
    loads = []
    at = 0
    sources = {}
    for g, (kind, index) in enumerate(groups):
        mine = []
        s = g % slots
        if kind not in sources:
            count = 1 if kind == "all" else 2
            sources[kind] = refs[at : at + count]
            at += count
        source = sources[kind]
        part = source[0].shape[2] if kind != "own" else 0
        if kind == "own":
            split = source[0].shape[1]
            rest = source[1].shape[1]
            pairs = [
                (source[0], w_ref.at[s, :, pl.ds(0, split)]),
                (source[1], w_ref.at[s, :, pl.ds(split, rest)]),
            ]
        elif kind == "all":
            pairs = [(source[0].at[j, index], w_ref.at[s, pl.ds(j * part, part)]) for j in range(8)]
        else:
            pairs = []
            for colour in (index,) if kind == "two" else (0, 1):
                for c in range(2):
                    for i, j in enumerate(order_of(colour)):
                        slot = jnp.bitwise_xor(d, j ^ c)
                        if kind == "two":
                            row = slot * part
                        else:
                            row = slot * (2 * part) + colour * part
                        row = pl.multiple_of(row, part)
                        one = source[c].at[4 * colour + i, 0]
                        pairs.append((one, w_ref.at[s, pl.ds(row, part)]))
        for i, (one, to) in enumerate(pairs):
            mine.append(pltpu.make_async_copy(one, to, sems.at[g, i]))
        loads.append(mine)
    return loads


def gelu_parts(gate):
    square = gate * gate
    t = jnp.tanh(gelu_coef * gate * (1.0 + 0.044715 * square))
    half = 0.5 * (1.0 + t)
    slope = half + 0.5 * gate * (1.0 - t * t) * gelu_coef * (1.0 + 3 * 0.044715 * square)
    return gate * half, slope


TILE = 768


def ff_fwd_kernel(groups, first, last, copies, smem, ins, raw, outs, raw_outs, scratch):
    (at_ref,) = smem
    hb_ref, acc_refs, norm_refs = ins[0], ins[1 : 4 if first else 2], ins[4 if first else 2 :]
    pre_ref = outs[0]
    w_ref, sems = scratch
    width = hb_ref.shape[1]
    loads = load_groups(groups, at_ref[0], raw, w_ref, sems, len(groups))
    for load in loads:
        for copy in load:
            copy.start()
    copies.wait()
    if first:
        xhat, _ = normed_of(acc_refs[0][...])
        pre_ref[...] = xhat * acc_refs[1][...] + acc_refs[2][...]
    else:
        pre_ref[...] = acc_refs[0][...]
    for s in range(len(groups)):
        for copy in loads[s]:
            copy.wait()

        def step(n, _, s=s):
            def at(c):
                return pl.ds(pl.multiple_of(c * width + n * TILE, TILE), TILE)

            hb = hb_ref[...]
            gate, value = mm(hb, w_ref[s, :, at(0)]), mm(hb, w_ref[s, :, at(1)])
            act = (gelu_parts(gate)[0] * value).astype(bf16)
            pre_ref[...] += mm(act, w_ref[s, at(0), pl.ds(2 * width, width)])
            return 0

        step(0, 0)
    if last:
        copies.put(0)
        xhat, _ = normed_of(pre_ref[...])
        out = (xhat * norm_refs[0][...] + norm_refs[1][...]).astype(bf16)
        outs[1][...] = out
        outs[2][...] = out.T


def ff_fwd(groups, d, hb, acc, weights, norm=None):
    rows, width = hb.shape
    last = norm is not None
    acc = acc if isinstance(acc, tuple) else (acc,)
    outs = [shape((rows, width), f32)]
    if last:
        outs += [shape((rows, width), bf16), shape((width, rows), bf16)]
    n = len(groups)
    return staged(
        functools.partial(ff_fwd_kernel, groups, len(acc) == 3, last),
        "ff_fwd",
        [d],
        [hb, *acc, *(norm if last else ())],
        weights,
        outs,
        [],
        [
            pltpu.VMEM((n, width, 3 * width), bf16),
            pltpu.SemaphoreType.DMA((n, 16)),
        ],
        36,
        cost(0, 0),
    )


def pick_rows(d, order, from_ref, to_ref):
    rows = from_ref.shape[0] // 8
    for i, j in enumerate(order):
        at = pl.multiple_of(jnp.bitwise_xor(d, j) * rows, rows)
        to_ref[pl.ds(i * rows, rows), :] = from_ref[pl.ds(at, rows), :]


def norm_bwd(grad, pre, gain_ref, small_ref):
    xhat, rstd = normed_of(pre)
    small_ref[0:1] = jnp.sum(grad * xhat, axis=0, keepdims=True)
    small_ref[1:2] = jnp.sum(grad, axis=0, keepdims=True)
    return norm_back(grad, xhat, rstd, gain_ref[...])


def ff_bwd_kernel(
    groups, first, last, slot, with_grads, copies, smem, ins, raw, outs, raw_outs, scratch
):
    (at_ref,) = smem
    hb_ref, *ins = ins
    w_ref, sems, *scratch = scratch
    if with_grads:
        hb_t_ref, *ins = ins
        g_ref, out_sems = scratch
    width = hb_ref.shape[1]
    part = width // 8
    n = len(groups)
    loads = load_groups(groups, at_ref[0], raw, w_ref, sems, 2)
    for copy in loads[0]:
        copy.start()
    copies.wait()
    dh_ref, *outs = outs
    if first:
        grad_ref, pre_ref, gain_ref, *ins = ins
        dyb_ref, dyb_t_ref, small2_ref, *outs = outs
        d_pre = norm_bwd(grad_ref[...].astype(f32), pre_ref[...], gain_ref, small2_ref)
        dh_ref[...] = d_pre
        dyb_ref[...] = d_pre.astype(bf16)
        dyb_t_ref[...] = dyb_ref[...].T
    else:
        dyb_ref, dyb_t_ref, acc_ref, *ins = ins
        dh_ref[...] = acc_ref[...]
    out = []
    for s in range(n):
        if s + 1 < n:
            for copy in loads[s + 1]:
                copy.start()
        for copy in loads[s]:
            copy.wait()
        weights = w_ref.at[s % 2]

        def at(c):
            return pl.ds(c * width, width)

        hb = hb_ref[...]
        gate, value = mm(hb, weights[:, at(0)]), mm(hb, weights[:, at(1)])
        d_act = mm(dyb_ref[...], weights[:, at(2)], NT)
        gelu, slope = gelu_parts(gate)
        d_gate = (d_act * value * slope).astype(bf16)
        d_value = (d_act * gelu).astype(bf16)
        act = (gelu * value).astype(bf16)
        dh_ref[...] += mm(d_gate, weights[:, at(0)], NT) + mm(d_value, weights[:, at(1)], NT)
        if not with_grads:
            continue
        if s >= 2:
            out[s - 2].wait()
        grads = g_ref.at[s % 2]
        for c, (lhs, rhs) in enumerate(((hb_t_ref, d_gate), (hb_t_ref, d_value), (dyb_t_ref, act))):
            total = mm(lhs[...], rhs).astype(bf16)
            for j in range(8):
                grads[j, :, at(c)] = total[j * part : (j + 1) * part]
        out.append(pltpu.make_async_copy(grads, raw_outs[0].at[:, slot + s], out_sems.at[s]))
        out[s].start()
    if last:
        pre_ref, gain_ref = ins
        dab_ref, small1_ref = outs
        d_pre = norm_bwd(dh_ref[...], pre_ref[...], gain_ref, small1_ref)
        dh_ref[...] = d_pre
        dab_ref[...] = d_pre.astype(bf16)
    for one in out[-2:]:
        one.wait()


def ff_bwd(groups, slot, d, hb, hb_t, ins, weights, first=False, last=False, into=None, grads=True):
    rows, width = hb.shape
    n = len(groups)
    low, few = shape((rows, width), bf16), shape((2, width), f32)
    outs = [shape((rows, width), f32)]
    outs += [low, shape((width, rows), bf16), few] if first else []
    outs += [low, few] if last else []
    extra = [] if into is None else [into]
    n_in = 3 + len(ins) + len(weights)
    scratch = [pltpu.VMEM((2, width, 3 * width), bf16), pltpu.SemaphoreType.DMA((n, 16))]
    if grads:
        scratch += [
            pltpu.VMEM((2, 8, width // 8, 3 * width), bf16),
            pltpu.SemaphoreType.DMA((n,)),
        ]
    return staged(
        functools.partial(ff_bwd_kernel, groups, first, last, slot, grads),
        "ff_bwd",
        [d],
        [hb, *([hb_t] if grads else []), *ins],
        weights + extra,
        outs,
        [shape((8, 4, width // 8, 3 * width), bf16)] if grads else [],
        scratch,
        60,
        cost(0, 0),
        {n_in: len(outs)} if extra else {},
    )


def ff_grads_kernel(n, copies, smem, ins, raw, outs, raw_outs, scratch):
    up_ref, down_ref, *rows_refs = ins
    (total_ref,) = scratch
    (at_ref,) = smem
    sent_ref, kept_ref = outs
    width = up_ref.shape[0]
    part = width // 8
    copies.wait(0, 1)
    for s in range(n):
        copies.wait(2 + 2 * s, 3 + 2 * s)
        hb, dyb = rows_refs[2 * s][...], rows_refs[2 * s + 1][...]
        gate, value = mm(hb, up_ref[:, pl.ds(0, width)]), mm(hb, up_ref[:, pl.ds(width, width)])
        d_act = mm(dyb, down_ref[...], NT)
        gelu, slope = gelu_parts(gate)
        d_gate = (d_act * value * slope).astype(bf16)
        d_value = (d_act * gelu).astype(bf16)
        act = (gelu * value).astype(bf16)
        hb_t, dyb_t = hb.T, dyb.T
        for c, (lhs, rhs) in enumerate(((hb_t, d_gate), (hb_t, d_value), (dyb_t, act))):
            at = pl.ds(c * width, width)
            total = mm(lhs, rhs)
            total_ref[:, at] = total if s == 0 else total + total_ref[:, at]
    order = fold_order(0)
    for to_ref, flip in ((sent_ref, 1), (kept_ref, 0)):
        for i, j in enumerate(order):
            row = pl.multiple_of(jnp.bitwise_xor(at_ref[0], j ^ flip) * part, part)
            to_ref[i] = total_ref[pl.ds(row, part), :].astype(bf16)
        copies.put(flip ^ 1)


def ff_grads(d, up, down, all_hb, all_dyb):
    width = up.shape[0]
    return staged(
        functools.partial(ff_grads_kernel, all_hb.shape[0]),
        "ff_grads",
        [d],
        [up, down, *[(one, s) for s in range(all_hb.shape[0]) for one in (all_hb, all_dyb)]],
        [],
        [shape((4, width // 8, 3 * width), bf16)] * 2,
        [],
        [pltpu.VMEM((width, 3 * width), f32)],
        60,
        cost(0, 0),
    )


def add_low(a, b):
    return (a.astype(f32) + b.astype(f32)).astype(bf16)


class Fold:
    def __init__(self, net, line, sent, kept):
        self.net, self.line = net, line
        self.kept, self.got = kept, net.flip(line.after(sent), 1)

    def step(self, bit):
        got = self.line.after(self.got)
        half = self.kept.shape[0] // 2
        self.got = self.net.flip(add_low(self.kept[half:], got[half:]), bit, wait=False)
        self.kept = add_low(self.kept[:half], got[:half])

    def first(self):
        self.step(COLOURS[0][0])

    def second(self):
        self.step(COLOURS[0][1])

    def done(self):
        return self.kept[0].astype(f32) + self.line.after(self.got)[0].astype(f32)


class Share:
    def __init__(self, net, line, z, sent, kept):
        self.net, self.line, self.z = net, line, z
        self.kept, self.got = kept, net.flip(line.after(sent), 1)

    def first(self):
        got = self.line.after(self.got)
        half = [(self.kept[2 * c : 2 * c + 2], got[2 * c : 2 * c + 2]) for c in range(2)]
        self.got = [
            self.net.flip(add_low(kept[:, 2:], got[:, 2:]), COLOURS[c][0])
            for c, (kept, got) in enumerate(half)
        ]
        self.kept = [add_low(kept[:, :2], got[:, :2]) for kept, got in half]

    def second(self):
        got = [self.line.after(one) for one in self.got]
        self.got = [
            self.net.flip(add_low(self.kept[c][:, 1], got[c][:, 1]), COLOURS[c][1])
            for c in range(2)
        ]
        self.kept = [add_low(self.kept[c][:, 0], got[c][:, 0]) for c in range(2)]

    def far(self):
        n = self.net.n_t
        total = [add_low(self.kept[c], self.line.after(self.got[c])) for c in range(2)]
        total = jnp.concatenate(total, axis=0)
        parts = [
            lax.dynamic_index_in_dim(total, lax.rem(self.z - k + n, n), 0, keepdims=False)
            for k in range(n)
        ]
        self.parts = [parts[0]] + [self.net.shift(parts[k], -k) for k in range(1, n)]

    def far_back(self):
        total = self.parts[0].astype(f32)
        for part in self.parts[1:]:
            total = total + self.line.after(part).astype(f32)
        total = total.astype(bf16)
        self.slices = [total] + [self.net.shift(total, k) for k in range(1, self.net.n_t)]

    def gather(self):
        self.gathered = Gather(self.net, self.line, self.slices)


def spread_kernel(layer, copies, smem, ins, raw, outs, raw_outs, scratch):
    (at_ref,) = smem
    held = ins
    (small_ref,) = outs
    qkv_out, wo_out = raw_outs
    buf, sems = scratch
    d, z = at_ref[0], at_ref[1]
    rows, cols = held[0].shape[2:]
    rows = rows - FEW

    def each(act):
        for c in range(2):
            for k in range(4):
                block = lax.rem(z - k + 4, 4)
                for i, j in enumerate(order_of(k // 2)):
                    act(c, k, i, j, block, 16 * c + 4 * k + i)

    def copy_of(n, slot, block, to_qkv):
        row = pl.ds(pl.multiple_of(slot * rows, rows), rows)
        if to_qkv:
            col = pl.ds(pl.multiple_of(block * cols, cols), cols)
            to = qkv_out.at[layer, row, col]
        else:
            to = wo_out.at[layer, row, :]
        return pltpu.make_async_copy(buf.at[n], to, sems.at[n])

    def begin(c, k, i, j, block, n):
        if k == 0 and i == 0:
            copies.wait(c)
        ref = held[c].at[4 * (k // 2) + i, k % 2]
        slot = jnp.bitwise_xor(d, j ^ c)
        buf[n] = ref[pl.ds(0, rows)].astype(f32)

        @pl.when(block < 3)
        def _():
            copy_of(n, slot, block, True).start()

        @pl.when(block == 3)
        def _():
            copy_of(n, slot, block, False).start()

        @pl.when(slot == 0)
        def _():
            small_ref[block] = ref[pl.ds(rows, FEW)].astype(f32)

    def end(c, k, i, j, block, n):
        slot = jnp.bitwise_xor(d, j ^ c)

        @pl.when(block < 3)
        def _():
            copy_of(n, slot, block, True).wait()

        @pl.when(block == 3)
        def _():
            copy_of(n, slot, block, False).wait()

    each(begin)
    each(end)


def spread_out(layer, where, pieces, before):
    rows, cols = pieces[0].shape[2:]
    width = 8 * (rows - FEW)
    return staged(
        functools.partial(spread_kernel, layer),
        "spread_out",
        [where],
        pieces,
        [] if before is None else list(before),
        [shape((4, FEW, cols), f32)],
        [shape((LAYERS, width, 3 * cols), f32), shape((LAYERS, width, cols), f32)],
        [pltpu.VMEM((32, rows - FEW, cols), f32), pltpu.SemaphoreType.DMA((32,))],
        24,
        cost(0, 0),
        {} if before is None else {3: 1, 4: 2},
    )


def quick_program(
    net,
    x_in,
    bucket,
    lengths,
    qkv_weight,
    out_weight,
    norm_gain1,
    norm_bias1,
    up_weight,
    down_weight,
    norm_gain2,
    norm_bias2,
    cotangent,
):
    rows, width = x_in.shape
    d, z = lax.axis_index("dp").astype(jnp.int32), lax.axis_index("tensor").astype(jnp.int32)
    d_at, dz_at = jnp.reshape(d, (1,)), jnp.stack([d, z])
    part = width // net.n_dp
    net.flying = []
    line = Line(net)
    gains1, biases1 = norm_gain1[:, None], norm_bias1[:, None]
    gains2, biases2 = norm_gain2[:, None], norm_bias2[:, None]

    def own_slice(l):
        up = lax.dynamic_slice(up_weight, (l, d * part, 0, 0), (1, part, 2, width))
        down = lax.dynamic_slice(down_weight, (l, d * part, 0), (1, part, width))
        return jnp.concatenate([up.reshape(part, 2 * width), down[0]], axis=1)

    def own_weights(l):
        return [up_weight[l].reshape(width, 2 * width), down_weight[l]]

    seg = segments(bucket[0], lengths[0], rows, SHORT)
    same = seg[:, None] == seg[None, :]
    place = jnp.arange(rows, dtype=f32)
    dist = jnp.where(same, jnp.abs(place[:, None] - place[None, :]), 1e34)
    slopes = slopes_of()
    outputs, kept = [], []

    def run_attn(l, x):
        def call(x):
            return attn_fwd(l, x, qkv_weight, out_weight, gains1[l], biases1[l], dist, slopes)

        return line.run(call, x)

    def run_ff(groups, hb, acc, weights, norm=None):
        return line.run(lambda hb: ff_fwd(groups, d_at, hb, acc, weights, norm), hb)

    OWN, HALF, TWO, ALL = "own", "half", "two", "all"
    own = own_slice(0)
    far = {k: net.shift(own, k, wait=k != 2) for k in (1, 3, 2)}
    x_t = x_in.T
    qkv, lse, ctx, ctx_t, pre1, hb, hb_t = run_attn(0, x_in)
    planes = lax.all_gather(line.after(own_slice(1)), "tensor")
    near = Gather(net, line, [far[1], far[3]])
    mine = own_weights(0)
    acc = run_ff(((OWN, 0),), hb, (pre1, gains1[0], biases1[0]), mine)[0]
    line.need(far[2])
    near.second()
    back = Gather(net, line, [far[2][: part // 2], far[2][part // 2 :]])
    line.sync()
    line.need(planes)
    planes = line.after(planes)
    others = jnp.stack(
        [
            lax.dynamic_index_in_dim(planes, lax.rem(z - k + net.n_t, net.n_t), 0, keepdims=False)
            for k in range(1, net.n_t)
        ]
    )
    others = lax.all_gather(others, "dp")
    near.core()
    back.second()
    line.sync()
    back.core()
    acc = run_ff(((TWO, 0), (TWO, 1)), hb, acc, near.pieces())[0]
    pre2, out, out_t = run_ff(((HALF, 0),), hb, acc, back.pieces(), (gains2[0], biases2[0]))
    kept.append((x_t, qkv, lse, ctx_t, pre1, hb, hb_t, pre2))
    outputs.append(out)
    weights = [
        [
            (((OWN, 0),), mine),
            (((HALF, 0), (TWO, 0), (TWO, 1)), back.pieces() + near.pieces()),
        ]
    ]
    qkv, lse, ctx, ctx_t, pre1, hb, hb_t = run_attn(1, out)
    mine = own_weights(1)
    acc = run_ff(((OWN, 0),), hb, (pre1, gains1[1], biases1[1]), mine)[0]
    line.need(others)
    all_hb = lax.all_gather(line.after(hb), "tensor")
    pre2, out, _ = run_ff(
        ((ALL, 0), (ALL, 1), (ALL, 2)), hb, acc, [others], (gains2[1], biases2[1])
    )
    weights.append([(((OWN, 0), (ALL, 1), (ALL, 0), (ALL, 2)), mine + [others])])
    kept.append((out_t, qkv, lse, ctx_t, pre1, hb, hb_t, pre2))
    outputs.append(out)

    order = (0, 2, 1, 3)

    def run_ff_bwd(l, at, ins, **how):
        groups, arrays = weights[l][at]
        hb, hb_t = kept[l][5:7]
        return line.run(lambda hb: ff_bwd(groups, at, d_at, hb, hb_t, ins, arrays, **how), hb)

    def run_attn_bwd(l, dab, d_pre, small):
        x_t, qkv, lse, ctx_t = kept[l][:4]
        return line.run(
            lambda dab: attn_bwd(
                l,
                d_at,
                dab,
                qkv,
                lse,
                out_weight,
                dist,
                slopes,
                d_pre,
                x_t,
                ctx_t,
                qkv_weight,
                small,
            ),
            dab,
        )

    def over_dp(grads):
        return lax.psum_scatter(line.after(grads), "dp", scatter_dimension=0, tiled=True)[0]

    def to_owner(l, i):
        return net.shift(line.after(ff[l][i]), -order[i])

    pre1, pre2 = kept[1][4], kept[1][7]
    d_pre1, dyb, _, small2, dab, small1 = run_ff_bwd(
        1, 0, (cotangent, pre2, gains2[1], pre1, gains1[1]), first=True, last=True, grads=False
    )
    sent, keep, grad = run_attn_bwd(1, dab, d_pre1, (small1, small2))
    line.need(all_hb)
    all_dyb = lax.all_gather(line.after(dyb), "tensor")
    pre1, pre2 = kept[0][4], kept[0][7]
    share = Share(net, line, z, sent, keep)
    d_h, dyb, dyb_t, small2, g = run_ff_bwd(0, 0, (grad, pre2, gains2[0]), first=True)
    share.first()
    d_pre1, dab, small1, g = run_ff_bwd(
        0, 1, (dyb, dyb_t, d_h, pre1, gains1[0]), into=g, last=True
    )
    share.second()
    sent, keep, grad = run_attn_bwd(0, dab, d_pre1, (small1, small2))
    line.need(all_dyb)
    ff = {0: over_dp(g)}
    last_share = Share(net, line, z, sent, keep)
    share.far()
    line.sync()
    last_share.first()
    share.far_back()
    own_up, own_down = weights[1][0][1][:2]
    sent, keep = line.run(lambda up: ff_grads(d_at, up, own_down, all_hb, all_dyb), own_up)
    last_share.second()
    share.gather()
    fold = Fold(net, line, sent, keep)
    line.sync()
    last_share.far()
    share.gathered.second()
    line.sync()
    last_share.far_back()
    share.gathered.core()
    fold.first()
    line.sync()
    last_share.gather()
    found = line.run(
        lambda first: spread_out(1, dz_at, [first] + share.gathered.pieces()[1:], None),
        share.gathered.pieces()[0],
    )
    small = {1: found[0]}
    line.need(ff[0], fold.got)
    last_share.gathered.second()
    ff_parts = {0: [ff[0][0], to_owner(0, 2), to_owner(0, 3)]}
    fold.second()
    line.sync()
    last_share.gathered.core()
    line.sync()
    ff_parts[0].append(to_owner(0, 1))
    rest = found[1:]
    found = line.run(
        lambda first: spread_out(0, dz_at, [first] + last_share.gathered.pieces()[1:], rest),
        last_share.gathered.pieces()[0],
    )
    ff_parts[1] = [fold.done()]
    small[0] = found[0]
    attention_grads = found[1:]
    small = jnp.stack([small[l][:, 0] for l in range(LAYERS)])
    up_grads, down_grads = [], []
    for l in range(LAYERS):
        total = ff_parts[l][0].astype(f32)
        for one in ff_parts[l][1:]:
            total = total + one.astype(f32)
        up_grads.append(total[:, : 2 * width].reshape(part, 2, width))
        down_grads.append(total[:, 2 * width :].T)
    return (
        jnp.stack(outputs),
        grad,
        attention_grads[0],
        attention_grads[1],
        small[:, 0],
        small[:, 1],
        jnp.stack(up_grads),
        jnp.stack(down_grads),
        small[:, 2],
        small[:, 3],
    )


def attention_forward(x_low, wqkv, wo, g1, b1, same, decay):
    rows, width = x_low.shape
    qkv_low = dot(x_low, wqkv).astype(bf16)
    query, keys, values = split_heads(qkv_low, width)
    scores = scores_of(query, keys, same, decay)
    top = jnp.max(scores, axis=-1, keepdims=True)
    log_total = top + jnp.log(jnp.sum(jnp.exp(scores - top), axis=-1, keepdims=True))
    probs_low = jnp.exp(scores - log_total).astype(bf16)
    ctx_low = (
        jnp.einsum("hqk,khe->qhe", probs_low, values, preferred_element_type=f32)
        .reshape(rows, width)
        .astype(bf16)
    )
    pre_first = x_low.astype(f32) + dot(ctx_low, wo)
    normed = layer_norm(pre_first, g1, b1)
    return normed, (qkv_low, log_total, ctx_low, pre_first)


def attention_backward(d_attn_low, qkv_low, log_total, ctx_low, wo, same, decay):
    rows, width = d_attn_low.shape
    d_ctx = dot(d_attn_low, wo.T).astype(bf16).reshape(rows, HEADS, HEAD_DIM)
    query, keys, values = split_heads(qkv_low, width)
    probs = jnp.exp(scores_of(query, keys, same, decay) - log_total)
    probs_low = probs.astype(bf16)
    d_values = jnp.einsum("hqk,qhe->khe", probs_low, d_ctx, preferred_element_type=f32)
    d_probs = jnp.einsum("qhe,khe->hqk", d_ctx, values, preferred_element_type=f32)
    d_scores = (probs * (d_probs - jnp.sum(probs * d_probs, axis=-1, keepdims=True))).astype(bf16)
    d_query = jnp.einsum("hqk,khe->qhe", d_scores, keys, preferred_element_type=f32)
    d_keys = jnp.einsum("hqk,qhe->khe", d_scores, query, preferred_element_type=f32)
    scale = HEAD_DIM ** (-0.5)
    return jnp.concatenate(
        [
            (d_query * scale).reshape(rows, width),
            (d_keys * scale).reshape(rows, width),
            d_values.reshape(rows, width),
        ],
        axis=1,
    ).astype(bf16)


def plain_program(
    net,
    x_in,
    bucket,
    lengths,
    qkv_weight,
    out_weight,
    norm_gain1,
    norm_bias1,
    up_weight,
    down_weight,
    norm_gain2,
    norm_bias2,
    cotangent,
):
    rows, width = x_in.shape
    n_t = net.n_t
    hidden = down_weight.shape[1]
    seg = segments(bucket[0], lengths[0], rows, SHORT)
    same = seg[:, None] == seg[None, :]
    decay = alibi(rows, HEADS)
    ups = lax.all_gather(up_weight, "tensor", axis=0)
    downs = lax.all_gather(down_weight, "tensor", axis=0)
    groups = [
        [(ups[k, l].reshape(width, -1), downs[k, l]) for k in range(n_t)] for l in range(LAYERS)
    ]
    layer_in = x_in
    outputs, kept = [], []
    for l in range(LAYERS):
        x_low = layer_in
        normed, keep = attention_forward(
            x_low, qkv_weight[l], out_weight[l], norm_gain1[l], norm_bias1[l], same, decay
        )
        hb = normed.astype(bf16)
        pre_second = normed
        joined, act = [], []
        for up, down in groups[l]:
            joined.append(dot(hb, up))
            act.append(geglu(joined[-1]).astype(bf16))
            pre_second = pre_second + dot(act[-1], down)
        layer_in = layer_norm(pre_second, norm_gain2[l], norm_bias2[l]).astype(bf16)
        outputs.append(layer_in)
        kept.append((x_low, *keep, hb, pre_second, joined, act))
    grad = cotangent.astype(f32)
    attention_grads, small, up_grads, down_grads = ([None] * LAYERS for _ in range(4))
    for l in reversed(range(LAYERS)):
        x_low, qkv_low, log_total, ctx_low, pre_first, hb, pre_second, joined, act = kept[l]
        pull = jax.vjp(layer_norm, pre_second, norm_gain2[l], norm_bias2[l])[1]
        d_pre2, d_gain2, d_bias2 = pull(grad)
        dyb = d_pre2.astype(bf16)
        d_h = d_pre2
        d_joined = []
        for k, (up, down) in enumerate(groups[l]):
            d_act = dot(dyb, down.T)
            d_joined.append(jax.vjp(geglu, joined[k])[1](d_act)[0].astype(bf16))
            d_h = d_h + dot(d_joined[k], up.T)
        d_up = jnp.stack([dot(hb.T, one) for one in d_joined]).astype(bf16)
        d_down = jnp.stack([dot(dyb.T, one) for one in act]).astype(bf16)
        d_up = lax.psum_scatter(d_up, "tensor", scatter_dimension=0)
        d_down = lax.psum_scatter(d_down, "tensor", scatter_dimension=0)
        d_up = lax.psum_scatter(d_up, "dp", scatter_dimension=0, tiled=True)
        d_down = lax.psum_scatter(d_down, "dp", scatter_dimension=0, tiled=True)
        up_grads[l], down_grads[l] = d_up.astype(f32), d_down.astype(f32)
        pull = jax.vjp(layer_norm, pre_first, norm_gain1[l], norm_bias1[l])[1]
        d_pre1, d_gain1, d_bias1 = pull(d_h)
        small[l] = [d_gain1, d_bias1, d_gain2, d_bias2]
        dab = d_pre1.astype(bf16)
        d_qkv = attention_backward(dab, qkv_low, log_total, ctx_low, out_weight[l], same, decay)
        found = lax.psum(
            (dot(x_low.T, d_qkv).astype(bf16), dot(ctx_low.T, dab).astype(bf16)), BOTH
        )
        attention_grads[l] = [one.astype(f32) for one in found]
        grad = d_pre1 + dot(d_qkv, qkv_weight[l].T)
    small = lax.psum(jnp.stack(small[0] + small[1]), BOTH).reshape(LAYERS, 4, width)
    return (
        jnp.stack(outputs),
        grad,
        jnp.stack([one[0] for one in attention_grads]),
        jnp.stack([one[1] for one in attention_grads]),
        small[:, 0],
        small[:, 1],
        jnp.stack(up_grads).reshape(LAYERS, -1, 2, hidden),
        jnp.stack([one.T for one in down_grads]),
        small[:, 2],
        small[:, 3],
    )


def program(net, *args):
    width, hidden = args[0].shape[1], args[8].shape[1]
    quick = net.n_dp == 8 and net.n_t == 4 and hidden == width and width % 256 == 0
    return (quick_program if quick else plain_program)(net, *args)


def solution(mesh):
    in_specs = (
        P(BOTH, None),
        P(BOTH),
        P(BOTH, None),
        P(),
        P(),
        P(),
        P(),
        P(None, None, None, "tensor"),
        P(None, "tensor", None),
        P(),
        P(),
        P(BOTH, None),
    )
    out_specs = (
        P(None, BOTH, None),
        P(BOTH, None),
        P(),
        P(),
        P(),
        P(),
        P(None, "dp", None, "tensor"),
        P(None, "tensor", "dp"),
        P(),
        P(),
    )
    net = Net(mesh)
    return jax.shard_map(
        functools.partial(program, net),
        mesh=mesh,
        in_specs=in_specs,
        out_specs=out_specs,
        check_vma=False,
    )
```
